256 devices in a mesh: gx: 16 (over z, x_lo), gy: 4 (over x_hi, core), gz: 4 (over y).
Axes of the slice: x: 4 (x_hi: 2, x_lo: 2; x = x_hi * 2 + x_lo), y: 4, z: 8, core: 2. Of those that a mesh axis runs over, the one named last changes fastest.
Arguments:
- positions: float32 [3, 32, 8, 16, 128], P(None, 'gx', 'gy', 'gz'), may hold values from 0 to 1
- species: int32 [32, 8, 16, 128], P('gx', 'gy', 'gz'), may hold values from 0 to 1
- counts: int32 [32, 8, 16], P('gx', 'gy', 'gz'), may hold values from 0 to 128, as said below
Outputs:
- forces: float32 [3, 32, 8, 16, 128], P(None, 'gx', 'gy', 'gz')
- energy: float32 [32, 8, 16, 128], P('gx', 'gy', 'gz')
The draws below stay inside these ranges and needn't reach their ends.
Inputs may be any that keep to these rules, and one draw needn't show every extreme that they name: `counts`: slots at or beyond a tile's count are empty; tiles in the lower half of the surface normal are nearly full, those above it nearly empty except for a block of tiles holding the nanoparticle.
All inputs are finite; a program needn't handle non-finite values.
Results may differ from the reference program's by a relative error of at most 0.0001.
Values sent between devices are 32-bit elements; how exact they have to be, the bound alone decides.
A program may use at most 64 MiB of HBM per device.

```python
import jax
import jax.numpy as jnp
from jax import lax

TILE = 128
NTX = 32
NTY = 8
NTZ = 16


def draw_counts(key, part):
    crowded_key, sparse_key = jax.random.split(jax.random.fold_in(key, 17))
    shape = (NTX, NTY, NTZ)
    crowded = jax.random.randint(crowded_key, shape, TILE * 3 // 4, TILE + 1)
    sparse = jax.random.randint(sparse_key, shape, 0, TILE // 8 + 1)
    position_x = lax.broadcasted_iota(jnp.int32, shape, 0)
    position_y = lax.broadcasted_iota(jnp.int32, shape, 1)
    height = lax.broadcasted_iota(jnp.int32, shape, 2)
    cluster = (height >= NTZ // 2) & (height < NTZ // 2 + 2) & (position_x < 2) & (position_y < 2)
    filled_tile = (height < NTZ // 2) | cluster
    return jnp.where(filled_tile, crowded, sparse).astype(jnp.int32)


def with_ends(drawn, stream_key, low, high):
    longest = drawn.shape.index(max(drawn.shape))
    spots = []
    for shift in (0, 1):
        where = [jax.random.randint(jax.random.fold_in(stream_key, axis), (), 0, length) for axis, length in enumerate(drawn.shape)]
        where[longest] = (where[longest] + shift) % drawn.shape[longest]
        spots.append(tuple(where))
    return drawn.at[spots[0]].set(low).at[spots[1]].set(high)


def block_scale(own_key, shape, pieces, least, top_value):
    factor_of = 1.0
    for dim, blocks in pieces:
        heights = jax.random.uniform(jax.random.fold_in(jax.random.fold_in(own_key, 6), dim), (blocks,), jnp.float32, least / len(pieces), top_value / len(pieces))
        factor_of = factor_of * jnp.repeat(jnp.exp(heights), shape[dim] // blocks).reshape((-1,) + (1,) * (len(shape) - 1 - dim))
    return factor_of


def setup_inputs(seed: int = 0) -> dict:
    keys = jax.random.split(jax.random.key(seed), 4)
    return {
        "positions": jnp.clip(1.0 * jax.random.uniform(keys[0], (3, NTX, NTY, NTZ, TILE), jnp.float32) ** block_scale(keys[0], (3, NTX, NTY, NTZ, TILE), ((1, 16), (2, 4), (3, 4)), -0.2, 0.2), 0.0, 1.0),
        "species": with_ends(jax.random.randint(keys[1], (NTX, NTY, NTZ, TILE), 0, 2), jax.random.fold_in(keys[1], 1), 0, 1).astype(jnp.int32),
        "counts": draw_counts(jax.random.fold_in(keys[3], 71), 0),
    }


CUTOFF_SQUARED = 0.2025
DENSITY_BASE = 1.0
DENSITY_STEP = 0.4
EMBED_BASE = 1.0
EMBED_STEP = -0.3
PAIR_BASE = 0.6
PAIR_STEP = 0.3

def neighbour_offsets():
    return [(first, second, third) for first in (-1, 0, 1) for second in (-1, 0, 1) for third in (-1, 0, 1)]

def kernels(squared):
    reach = jnp.maximum(1.0 - squared / CUTOFF_SQUARED, 0.0)
    reach_two = reach * reach
    return (reach_two * reach, reach_two * reach_two, -3.0 * reach_two / CUTOFF_SQUARED, -4.0 * reach_two * reach / CUTOFF_SQUARED)

def shifted(field, offset):
    extent_x = field.shape[-4] - 2
    extent_y = field.shape[-3] - 2
    extent_z = field.shape[-2] - 2
    return field[..., 1 + offset[0]:1 + offset[0] + extent_x, 1 + offset[1]:1 + offset[1] + extent_y, 1 + offset[2]:1 + offset[2] + extent_z, :]

def geometry(centre, beside, offset):
    parts = [beside[comp][..., None, :] + float(offset[comp]) - centre[comp][..., :, None] for comp in range(3)]
    squared = parts[0] * parts[0] + parts[1] * parts[1] + parts[2] * parts[2]
    return (parts, squared)

def densities(extended):
    centre = shifted(extended, (0, 0, 0))
    self_mask = 1.0 - jnp.eye(centre.shape[-1], dtype=jnp.float32)
    total = jnp.zeros(centre.shape[1:], jnp.float32)
    for offset in neighbour_offsets():
        beside = shifted(extended, offset)
        parts, squared = geometry(centre, beside, offset)
        cube = kernels(squared)[0]
        weight = beside[3] * (DENSITY_BASE + DENSITY_STEP * beside[4])
        terms = cube * weight[..., None, :]
        if offset == (0, 0, 0):
            terms = terms * self_mask
        total = total + lax.optimization_barrier(jnp.sum(terms, axis=-1))
    return total

def embedding(density, state):
    strength = state[3] * (EMBED_BASE + EMBED_STEP * state[4])
    root = jnp.sqrt(1.0 + density)
    return (-strength * root, -0.5 * strength / root)

def forces_of(extended, derivative_ext):
    centre = shifted(extended, (0, 0, 0))
    slope_own = shifted(derivative_ext, (0, 0, 0))
    dens_own = centre[3] * (DENSITY_BASE + DENSITY_STEP * centre[4])
    pair_own = centre[3] * (PAIR_BASE + PAIR_STEP * centre[4])
    self_mask = 1.0 - jnp.eye(centre.shape[-1], dtype=jnp.float32)
    total = jnp.zeros((3,) + centre.shape[1:], jnp.float32)
    pair_total = jnp.zeros(centre.shape[1:], jnp.float32)
    for offset in neighbour_offsets():
        beside = shifted(extended, offset)
        slope_beside = shifted(derivative_ext, offset)
        parts, squared = geometry(centre, beside, offset)
        cube, quart, cube_slope, quart_slope = kernels(squared)
        dens_beside = beside[3] * (DENSITY_BASE + DENSITY_STEP * beside[4])
        pair_beside = beside[3] * (PAIR_BASE + PAIR_STEP * beside[4])
        pair_weight = pair_own[..., :, None] * pair_beside[..., None, :]
        weight_pair = cube_slope * (slope_own[..., :, None] * dens_beside[..., None, :] + slope_beside[..., None, :] * dens_own[..., :, None]) + quart_slope * pair_weight
        energy_terms = quart * pair_weight
        if offset == (0, 0, 0):
            weight_pair = weight_pair * self_mask
            energy_terms = energy_terms * self_mask
        total = total + 2.0 * jnp.stack([lax.optimization_barrier(jnp.sum(weight_pair * parts[comp], axis=-1)) for comp in range(3)])
        pair_total = pair_total + lax.optimization_barrier(jnp.sum(energy_terms, axis=-1))
    return (total, pair_total)

def surround(field):
    lead = field.ndim - 4
    wrapped = jnp.pad(field, [(0, 0)] * lead + [(1, 1), (1, 1), (0, 0), (0, 0)], mode='wrap')
    return jnp.pad(wrapped, [(0, 0)] * lead + [(0, 0), (0, 0), (1, 1), (0, 0)])

def reference(positions, species, counts):
    occupied = (lax.broadcasted_iota(jnp.int32, species.shape, 3) < counts[..., None]).astype(jnp.float32)
    state = jnp.concatenate([positions, occupied[None], species.astype(jnp.float32)[None]], axis=0)
    extended = surround(state)
    starts = jnp.arange(NTX, dtype=jnp.int32)

    def density_slab(start):
        return densities(lax.dynamic_slice_in_dim(extended, start, 3, axis=1))[0]
    density = lax.map(density_slab, starts)
    embed, derivative = embedding(density, state)
    derivative_ext = surround(derivative)

    def force_slab(start):
        piece = lax.dynamic_slice_in_dim(extended, start, 3, axis=1)
        slope_piece = lax.dynamic_slice_in_dim(derivative_ext, start, 3, axis=0)
        force_piece, pair_piece = forces_of(piece, slope_piece)
        return (force_piece[:, 0], pair_piece[0])
    force_rows, pair_rows = lax.map(force_slab, starts)
    forces = jnp.moveaxis(force_rows, 1, 0)
    return (forces, embed + 0.5 * pair_rows)
```

```python
import math

import jax
import jax.numpy as jnp
from jax import lax
from jax.experimental import pallas as pl
from jax.experimental.pallas import tpu as pltpu
from jax.sharding import PartitionSpec as P

F32 = jnp.float32
BF16 = jnp.bfloat16
MESH = pl.DeviceIdType.MESH
CUTOFF_SQUARED = 0.2025
SCALE = math.sqrt(2.0 / CUTOFF_SQUARED)
TILE = 128
OWN = (2, 2, 4)
EXT = (4, 4, 6)
OFFSETS = [
    (a, b, c) for a in (-1, 0, 1) for b in (-1, 0, 1) for c in (-1, 0, 1) if (a, b, c) != (0, 0, 0)
]
ALPHA = -3.0 / CUTOFF_SQUARED
BETA = -4.0 / CUTOFF_SQUARED * 0.09
SLOPE = ALPHA / (5.0 * BETA)
HIGHEST = lax.Precision.HIGHEST
NT = (((1,), (1,)), ((), ()))


def pieces(v):
    first = v.astype(BF16).astype(F32)
    rest = v - first
    second = rest.astype(BF16).astype(F32)
    return first, second, rest - second


def beside_features(v):
    a, b, c = pieces(v)
    return jnp.concatenate([a, b, a, b, c, a], axis=0).astype(BF16)


def own_features(v):
    a, b, c = pieces(v)
    return jnp.concatenate([a, a, b, b, a, c], axis=0).T.astype(BF16)


def rows_of(*rows):
    row = lax.broadcasted_iota(jnp.int32, (8, TILE), 0)
    out = jnp.zeros((8, TILE), F32)
    for index, value in enumerate(rows):
        if value is not None:
            out = jnp.where(row == index, value, out)
    return out


def tile_of(index, extent):
    plane = extent[1] * extent[2]
    return index // plane, (index // extent[2]) % extent[1], index % extent[2]


def span(offset, own, sending):
    if offset == 0:
        return pl.ds(1, own)
    if sending:
        return pl.ds(own if offset > 0 else 1, 1)
    return pl.ds(0 if offset > 0 else own + 1, 1)


def region(offset, sending):
    return tuple(span(o, n, sending) for o, n in zip(offset, OWN))


def exchange_kernel(
    sizes, pos_ref, spec_ref, count_ref, full_ref, embed_ref, wire, slope, beside, sends, recvs
):
    me = [lax.axis_index(name) for name in ("gx", "gy", "gz")]

    def peer(offset):
        return tuple(lax.rem(m + o + n, n) for m, o, n in zip(me, offset, sizes))

    barrier = pltpu.get_barrier_semaphore()
    for offset in OFFSETS:
        pl.semaphore_signal(barrier, inc=1, device_id=peer(offset), device_id_type=MESH)

    lane = lax.broadcasted_iota(jnp.int32, (1, TILE), 1)
    row4 = lax.broadcasted_iota(jnp.int32, (4, TILE), 0)
    for x in range(OWN[0]):
        for y in range(OWN[1]):
            for z in range(OWN[2]):
                kind = spec_ref[x, y, z : z + 1, :]
                weight = jnp.where(
                    lane < count_ref[x, y, z], jnp.where(kind == 1, 7.0, 5.0), 0.0
                )
                value = jnp.broadcast_to(weight, (4, TILE))
                for comp in range(3):
                    value = jnp.where(row4 == comp, pos_ref[comp, x, y, z : z + 1, :], value)
                wire[x + 1, y + 1, z + 1] = value
    pl.semaphore_wait(barrier, len(OFFSETS))

    def copies(ref, which):
        return [
            pltpu.make_async_remote_copy(
                src_ref=ref.at[region(offset, True)],
                dst_ref=ref.at[region(offset, False)],
                send_sem=sends.at[which, k],
                recv_sem=recvs.at[which, k],
                device_id=peer(offset),
                device_id_type=MESH,
            )
            for k, offset in enumerate(OFFSETS)
        ]

    state_copies = copies(wire, 0)
    for copy in state_copies:
        copy.start()
    for copy in state_copies:
        copy.wait()

    below = me[2] > 0
    above = me[2] < sizes[2] - 1

    def weights(z, value):
        inside = jnp.where(
            z == 0, below.astype(F32), jnp.where(z == EXT[2] - 1, above.astype(F32), 1.0)
        )
        return value[3:4] * inside

    def place(x, y, z, value):
        cx = (value[0:1] + (x - 2).astype(F32)) * SCALE
        cy = (value[1:2] + (y - 2).astype(F32)) * SCALE
        cz = (value[2:3] + (z - 3).astype(F32)) * SCALE
        return cx, cy, cz, 0.5 * (cx * cx + cy * cy + cz * cz)

    def prepare(index, _):
        x, y, z = tile_of(index, EXT)
        value = wire[x, y, z]
        cx, cy, cz, norm = place(x, y, z, value)
        weight = weights(z, value)
        root = jnp.where(weight > 6.0, 1.4 ** (1.0 / 3.0), jnp.where(weight > 0.0, 1.0, 0.0))
        pair = jnp.where(weight > 0.0, 0.5 * weight - 0.5, 0.0)
        beside[x * EXT[1] + y, :, pl.ds(pl.multiple_of(z * TILE, TILE), TILE)] = beside_features(
            rows_of(root * cx, root * cy, root * cz, root, -root * norm)
        )
        full_ref[x, y, z] = rows_of(cx, cy, cz, weight, 1.0, -norm, None, pair)
        return _

    lax.fori_loop(0, EXT[0] * EXT[1] * EXT[2], prepare, 0)

    ones = jnp.ones((8, TILE), F32)
    half = 32

    def density(index, _):
        x, y, z = tile_of(index, OWN)
        value = wire[x + 1, y + 1, z + 1]
        cx, cy, cz, norm = place(x + 1, y + 1, z + 1, value)
        own = own_features(rows_of(cx, cy, cz, 1.0 - norm, 1.0))
        totals = []
        for part in range(TILE // half):
            rows = own[part * half : (part + 1) * half]
            total = jnp.zeros((half, TILE), F32)
            for dx in range(3):
                for dy in range(3):
                    there = beside[
                        (x + dx) * EXT[1] + y + dy,
                        :,
                        pl.ds(pl.multiple_of(z * TILE, TILE), 3 * TILE),
                    ]
                    reach = jnp.dot(rows, there, preferred_element_type=F32)
                    reach = jnp.maximum(reach, 0.0)
                    cube = reach * reach * reach
                    middle = cube[:, TILE : 2 * TILE]
                    if (dx, dy) == (1, 1):
                        here = lax.broadcasted_iota(jnp.int32, (half, TILE), 0) + part * half
                        self_pair = here == lax.broadcasted_iota(jnp.int32, (half, TILE), 1)
                        middle = jnp.where(self_pair, 0.0, middle)
                    total = total + cube[:, :TILE] + middle + cube[:, 2 * TILE :]
            totals.append(total)
        total = jnp.concatenate(totals, axis=0)
        result = lax.dot_general(ones, total, NT, precision=HIGHEST, preferred_element_type=F32)
        root = jnp.sqrt(1.0 + result[0:1])
        weight = value[3:4]
        strength = jnp.where(weight > 6.0, 0.7, jnp.where(weight > 0.0, 1.0, 0.0))
        embed_ref[x, y, z] = -strength * root
        slope[x + 1, y + 1, z + 1] = -0.5 * SLOPE * strength / root
        return _

    lax.fori_loop(0, OWN[0] * OWN[1] * OWN[2], density, 0)

    slope_copies = copies(slope, 1)
    for copy in slope_copies:
        copy.start()
    for copy in slope_copies:
        copy.wait()

    def finish(index, _):
        x, y, z = tile_of(index, EXT)
        full_ref[x, y, z, 6:7, :] = jnp.where(
            full_ref[x, y, z, 3:4, :] > 0.0, slope[x, y, z], 0.0
        )
        return _

    lax.fori_loop(0, EXT[0] * EXT[1] * EXT[2], finish, 0)


def force_kernel(full_ref, embed_ref, forces_ref, energy_ref, beside, sums):
    row = lax.broadcasted_iota(jnp.int32, (8, TILE), 0)
    masks = ((row < 3) | (row == 4) | (row == 5), (row == 3) | (row == 6), row == 7)

    def prepare(index, _):
        x, y, z = tile_of(index, EXT)
        value = full_ref[x, y, z]
        for k, mask in enumerate(masks):
            beside[k, x * EXT[1] + y, :, pl.ds(pl.multiple_of(z * TILE, TILE), TILE)] = (
                beside_features(jnp.where(mask, value, 0.0))
            )
        return _

    lax.fori_loop(0, EXT[0] * EXT[1] * EXT[2], prepare, 0)
    half = 32

    def forces(index, _):
        x, y, z = tile_of(index, OWN)
        value = full_ref[x + 1, y + 1, z + 1]
        own_value = jnp.where(row == 3, value[6:7], value)
        own_value = jnp.where(row == 4, 1.0 + value[5:6], own_value)
        own_value = jnp.where(row == 5, 1.0, own_value)
        own_value = jnp.where(row == 6, value[3:4], own_value)
        own = own_features(own_value)
        lanes = lax.broadcasted_iota(jnp.int32, (half, TILE), 1)
        for part in range(TILE // half):
            rows = own[part * half : (part + 1) * half]
            total = [jnp.zeros((half, TILE), F32) for _ in range(5)]
            for dx in range(3):
                for dy in range(3):
                    at = (
                        (x + dx) * EXT[1] + y + dy,
                        slice(None),
                        pl.ds(pl.multiple_of(z * TILE, TILE), 3 * TILE),
                    )
                    reach, both, pair = (
                        jnp.dot(rows, beside[(k,) + at], preferred_element_type=F32)
                        for k in range(3)
                    )
                    for dz in range(3):
                        cut = slice(dz * TILE, (dz + 1) * TILE)
                        q = jnp.maximum(reach[:, cut], 0.0)
                        if (dx, dy, dz) == (1, 1, 1):
                            here = lax.broadcasted_iota(jnp.int32, (half, TILE), 0) + part * half
                            q = jnp.where(here == lanes, 0.0, q)
                        square = q * q
                        pull = square * (q * pair[:, cut])
                        coef = pull + square * both[:, cut]
                        there = full_ref[x + dx, y + dy, z + dz]
                        for comp in range(3):
                            total[comp] = total[comp] + coef * there[comp : comp + 1]
                        total[3] = total[3] + coef
                        total[4] = total[4] + pull * q
            column = jnp.zeros((half, TILE), F32)
            for k in range(5):
                column = jnp.where(lanes == k, jnp.sum(total[k], axis=1, keepdims=True), column)
            sums[part * half : (part + 1) * half, :] = column
        result = sums[...].T[:8]
        coef = result[3:4]
        moved = (2.0 * BETA / SCALE) * (result - value * coef)
        energy = embed_ref[x, y, z] + (0.5 * 0.09) * result[4:5]
        energy_ref[index] = jnp.where(row == 3, energy, moved)
        return _

    lax.fori_loop(0, OWN[0] * OWN[1] * OWN[2], forces, 0)


def shards(sizes, positions, species, counts):
    vmem = pl.BlockSpec(memory_space=pltpu.VMEM)
    full, embed = pl.pallas_call(
        lambda *refs: exchange_kernel(sizes, *refs),
        name="exchange",
        out_shape=(
            jax.ShapeDtypeStruct(EXT + (8, TILE), F32),
            jax.ShapeDtypeStruct(OWN + (1, TILE), F32),
        ),
        in_specs=[vmem, vmem, pl.BlockSpec(memory_space=pltpu.SMEM)],
        out_specs=(vmem, vmem),
        scratch_shapes=[
            pltpu.VMEM(EXT + (4, TILE), F32),
            pltpu.VMEM(EXT + (1, TILE), F32),
            pltpu.VMEM((EXT[0] * EXT[1], 48, EXT[2] * TILE), BF16),
            pltpu.SemaphoreType.DMA((2, len(OFFSETS))),
            pltpu.SemaphoreType.DMA((2, len(OFFSETS))),
        ],
        compiler_params=pltpu.CompilerParams(collective_id=0, has_side_effects=True),
    )(positions, species, counts)
    result = pl.pallas_call(
        lambda full_ref, embed_ref, out_ref, *scratch: force_kernel(
            full_ref, embed_ref, None, out_ref, *scratch
        ),
        name="forces",
        out_shape=jax.ShapeDtypeStruct((OWN[0] * OWN[1] * OWN[2], 8, TILE), F32),
        in_specs=[vmem, vmem],
        out_specs=vmem,
        scratch_shapes=[
            pltpu.VMEM((3, EXT[0] * EXT[1], 48, EXT[2] * TILE), BF16),
            pltpu.VMEM((TILE, TILE), F32),
        ],
    )(full, embed)
    result = result.reshape(OWN + (8, TILE))
    return jnp.moveaxis(result[..., :3, :], 3, 0), result[..., 3, :]


def solution(mesh):
    placed = (P(None, "gx", "gy", "gz", None), P("gx", "gy", "gz", None), P("gx", "gy", "gz"))
    sizes = tuple(mesh.shape[name] for name in ("gx", "gy", "gz"))
    return jax.shard_map(
        lambda *args: shards(sizes, *args),
        mesh=mesh,
        in_specs=placed,
        out_specs=(P(None, "gx", "gy", "gz", None), P("gx", "gy", "gz", None)),
        check_vma=False,
    )
```

```python
import math

import jax
import jax.numpy as jnp
from jax import lax
from jax.experimental import pallas as pl
from jax.experimental.pallas import tpu as pltpu
from jax.sharding import PartitionSpec as P

F32 = jnp.float32
BF16 = jnp.bfloat16
MESH = pl.DeviceIdType.MESH
CUTOFF_SQUARED = 0.2025
SCALE = math.sqrt(2.0 / CUTOFF_SQUARED)
TILE = 128
OWN = (2, 2, 4)
EXT = (4, 4, 6)
OFFSETS = [
    (a, b, c) for a in (-1, 0, 1) for b in (-1, 0, 1) for c in (-1, 0, 1) if (a, b, c) != (0, 0, 0)
]
ALPHA = -3.0 / CUTOFF_SQUARED
BETA = -4.0 / CUTOFF_SQUARED * 0.09
SLOPE = ALPHA / (5.0 * BETA)
PART = 128
FORCE_PART = 64
GROUP = 6
HIGHEST = lax.Precision.HIGHEST
NT = (((1,), (1,)), ((), ()))


def pieces(v):
    first = v.astype(BF16).astype(F32)
    rest = v - first
    second = rest.astype(BF16).astype(F32)
    return first, second, rest - second


def beside_features(v):
    a, b, c = pieces(v)
    return jnp.concatenate([a, b, a, b, c, a], axis=0).astype(BF16)


def own_features(v):
    a, b, c = pieces(v)
    return jnp.concatenate([a, a, b, b, a, c], axis=0).T.astype(BF16)


def rows_of(*rows):
    row = lax.broadcasted_iota(jnp.int32, (8, TILE), 0)
    out = jnp.zeros((8, TILE), F32)
    for index, value in enumerate(rows):
        if value is not None:
            out = jnp.where(row == index, value, out)
    return out


def tile_of(index, extent):
    plane = extent[1] * extent[2]
    return index // plane, (index // extent[2]) % extent[1], index % extent[2]


def span(offset, own, sending):
    if offset == 0:
        return pl.ds(1, own)
    if sending:
        return pl.ds(own if offset > 0 else 1, 1)
    return pl.ds(0 if offset > 0 else own + 1, 1)


def region(offset, sending):
    return tuple(span(o, n, sending) for o, n in zip(offset, OWN))


def exchange_kernel(
    sizes,
    pos_ref,
    spec_ref,
    count_ref,
    full_ref,
    embed_ref,
    near_ref,
    held_ref,
    wire,
    slope,
    beside,
    own,
    totals,
    reach_rows,
    sends,
    recvs,
):
    me = [lax.axis_index(name) for name in ("gx", "gy", "gz")]

    def peer(offset):
        return tuple(lax.rem(m + o + n, n) for m, o, n in zip(me, offset, sizes))

    barrier = pltpu.get_barrier_semaphore()
    for offset in OFFSETS:
        pl.semaphore_signal(barrier, inc=1, device_id=peer(offset), device_id_type=MESH)

    lane = lax.broadcasted_iota(jnp.int32, (1, TILE), 1)
    row4 = lax.broadcasted_iota(jnp.int32, (4, TILE), 0)
    for x in range(OWN[0]):
        for y in range(OWN[1]):
            for z in range(OWN[2]):
                kind = spec_ref[x, y, z : z + 1, :]
                weight = jnp.where(
                    lane < count_ref[x, y, z], jnp.where(kind == 1, 7.0, 5.0), 0.0
                )
                value = jnp.broadcast_to(weight, (4, TILE))
                for comp in range(3):
                    value = jnp.where(row4 == comp, pos_ref[comp, x, y, z : z + 1, :], value)
                wire[x + 1, y + 1, z + 1] = value
    pl.semaphore_wait(barrier, len(OFFSETS))

    def copies(ref, which):
        return [
            pltpu.make_async_remote_copy(
                src_ref=ref.at[region(offset, True)],
                dst_ref=ref.at[region(offset, False)],
                send_sem=sends.at[which, k],
                recv_sem=recvs.at[which, k],
                device_id=peer(offset),
                device_id_type=MESH,
            )
            for k, offset in enumerate(OFFSETS)
        ]

    state_copies = copies(wire, 0)
    for copy in state_copies:
        copy.start()

    low = (me[2] > 0).astype(F32)
    high = (me[2] < sizes[2] - 1).astype(F32)

    def prepare(x, y, z):
        value = wire[x, y, z]
        weight = value[3:4] * (low if z == 0 else high if z == EXT[2] - 1 else 1.0)
        cx = (value[0:1] + (x - 2).astype(F32)) * SCALE
        cy = (value[1:2] + (y - 2).astype(F32)) * SCALE
        cz = (value[2:3] + float(z - 3)) * SCALE
        norm = 0.5 * (cx * cx + cy * cy + cz * cz)
        root = jnp.where(weight > 6.0, 1.4 ** (1.0 / 3.0), jnp.where(weight > 0.0, 1.0, 0.0))
        pair = jnp.where(weight > 0.0, 0.5 * weight - 0.5, 0.0)
        full = rows_of(cx, cy, cz, weight, 1.0, -norm, None, pair)
        full_ref[x, y, z] = full
        row = lax.broadcasted_iota(jnp.int32, (8, TILE), 0)
        part = root * jnp.where(row == 3, 1.0, jnp.where(row == 4, -norm, full))
        beside[x * EXT[1] + y, :, z * TILE : (z + 1) * TILE] = beside_features(
            jnp.where(row < 5, part, 0.0)
        )
        return full

    def prepare_own(index, _):
        x, y = 1 + index // OWN[1], 1 + index % OWN[1]
        for z in (0, EXT[2] - 1):
            beside[x * EXT[1] + y, :, z * TILE : (z + 1) * TILE] = jnp.zeros((48, TILE), BF16)
        for z in range(OWN[2]):
            full = prepare(x, y, z + 1)
            row = lax.broadcasted_iota(jnp.int32, (8, TILE), 0)
            value = jnp.where(row == 3, 1.0 + full[5:6], jnp.where(row < 5, full, 0.0))
            own[index * OWN[2] + z] = own_features(value)
        return _

    lax.fori_loop(0, OWN[0] * OWN[1], prepare_own, 0)

    def cubes(rows, there):
        value = jnp.maximum(jnp.dot(rows, there, preferred_element_type=F32), 0.0)
        return value * value * value

    def blocks(value):
        return sum(
            value[:, k * TILE : (k + 1) * TILE] for k in range(1, value.shape[1] // TILE)
        ) + value[:, :TILE]

    def window(column, z, width=3):
        return beside[column, :, pl.ds(pl.multiple_of(z * TILE, TILE), width * TILE)]

    parts = TILE // PART

    def inner(index, _):
        x, y, z = tile_of(index, OWN)
        for part in range(parts):
            cut = slice(part * PART, (part + 1) * PART)
            rows = own[index, cut]
            total = jnp.zeros((PART, TILE), F32)
            for dx in range(OWN[0]):
                for dy in range(OWN[1]):
                    there = lax.rem(x + dx, OWN[0]) + 1, lax.rem(y + dy, OWN[1]) + 1
                    cube = cubes(rows, window(there[0] * EXT[1] + there[1], z))
                    if (dx, dy) == (0, 0):
                        here = lax.broadcasted_iota(jnp.int32, (PART, TILE), 0) + part * PART
                        self_pair = here == lax.broadcasted_iota(jnp.int32, (PART, TILE), 1)
                        middle = jnp.where(self_pair, 0.0, cube[:, TILE : 2 * TILE])
                        total = total + cube[:, :TILE] + middle + cube[:, 2 * TILE :]
                    else:
                        total = total + blocks(cube)
            totals[index, cut] = total
        return _

    lax.fori_loop(0, OWN[0] * OWN[1] * OWN[2], inner, 0)

    for copy in state_copies:
        copy.wait()

    def prepare_side(index, _):
        x = jnp.where(index < 4, 0, jnp.where(index < 8, EXT[0] - 1, 1 + (index - 8) // 2))
        y = jnp.where(index < 8, lax.rem(index, 4), (EXT[1] - 1) * lax.rem(index, 2))
        for z in range(EXT[2]):
            prepare(x, y, z)
        return _

    lax.fori_loop(0, EXT[0] * EXT[1] - OWN[0] * OWN[1], prepare_side, 0)

    def prepare_ends(index, _):
        for z in (0, EXT[2] - 1):
            prepare(1 + index // OWN[1], 1 + index % OWN[1], z)
        return _

    lax.fori_loop(0, OWN[0] * OWN[1], prepare_ends, 0)

    ones = jnp.ones((8, TILE), F32)

    def ends(index, _):
        column, upper = index // 2, lax.rem(index, 2)
        tile = column * OWN[2] + upper * (OWN[2] - 1)
        for part in range(parts):
            cut = slice(part * PART, (part + 1) * PART)
            rows = own[tile, cut]
            total = totals[tile, cut]
            for x in range(OWN[0]):
                for y in range(OWN[1]):
                    there = (x + 1) * EXT[1] + y + 1
                    total = total + cubes(rows, window(there, upper * (EXT[2] - 1), 1))
            totals[tile, cut] = total
        return _

    lax.fori_loop(0, 2 * OWN[0] * OWN[1], ends, 0)

    def outer(index, _):
        x, y, z = tile_of(index, OWN)
        side_x, side_y = x * (EXT[0] - 1), y * (EXT[1] - 1)
        columns = [side_x * EXT[1] + y + dy for dy in range(3)]
        columns += [(dx + 1) * EXT[1] + side_y for dx in range(OWN[0])]
        for part in range(parts):
            cut = slice(part * PART, (part + 1) * PART)
            rows = own[index, cut]
            total = totals[index, cut]
            for column in columns:
                total = total + blocks(cubes(rows, window(column, z)))
            totals[index, cut] = total
        result = lax.dot_general(
            ones, totals[index], NT, precision=HIGHEST, preferred_element_type=F32
        )
        root = jnp.sqrt(1.0 + result[0:1])
        weight = wire[x + 1, y + 1, z + 1, 3:4, :]
        strength = jnp.where(weight > 6.0, 0.7, jnp.where(weight > 0.0, 1.0, 0.0))
        embed_ref[index] = -strength * root
        slope[x + 1, y + 1, z + 1] = -0.5 * SLOPE * strength / root
        return _

    lax.fori_loop(0, OWN[0] * OWN[1] * OWN[2], outer, 0)

    slope_copies = copies(slope, 1)
    for copy in slope_copies:
        copy.start()

    def distances(index, _):
        x, y, z = tile_of(index, OWN)
        for k, offset in enumerate(OFFSETS):
            at = tuple(a + 1 + o for a, o in zip((x, y, z), offset))
            there = wire[at]
            far = None
            for comp, o in enumerate(offset):
                if o:
                    gap = there[comp : comp + 1] if o > 0 else 1.0 - there[comp : comp + 1]
                    far = gap * gap if far is None else far + gap * gap
            weight = full_ref[at + (slice(3, 4),)]
            reach_rows[index, k : k + 1, :] = jnp.where(weight > 0.0, far, 9.0)
        for k in range(len(OFFSETS), 32):
            reach_rows[index, k : k + 1, :] = jnp.full((1, TILE), 9.0, F32)
        return _

    lax.fori_loop(0, OWN[0] * OWN[1] * OWN[2], distances, 0)

    first = lax.broadcasted_iota(jnp.int32, (TILE, TILE), 0)
    second = lax.broadcasted_iota(jnp.int32, (TILE, TILE), 1)
    earlier = (first < second).astype(F32).astype(BF16)

    def compress(group, _):
        rows = reach_rows[pl.ds(group * 4, 4)].reshape(TILE, TILE)
        near = rows < CUTOFF_SQUARED * 1.00002
        flags = near.astype(F32).astype(BF16)
        before = jnp.dot(flags, earlier, preferred_element_type=F32).astype(jnp.int32)
        word = jnp.where(near, 16384 + second * 128 + (second - before), 0)
        for bit in range(7):
            moved = pltpu.roll(word, TILE - (1 << bit), 1)
            stay = jnp.where((word & (1 << bit)) != 0, 0, word)
            word = jnp.where((moved & (1 << bit)) != 0, moved, stay)
        near_ref[pl.ds(group * 4, 4)] = ((word >> 7) & 127).reshape(4, 32, TILE)
        held = lax.dot_general(
            jnp.ones((8, TILE), BF16), flags, NT, preferred_element_type=F32
        )
        held_ref[:, pl.ds(pl.multiple_of(group * TILE, TILE), TILE)] = held[0:1].astype(jnp.int32)
        return _

    lax.fori_loop(0, 4, compress, 0)

    for copy in slope_copies:
        copy.wait()

    def finish(index, _):
        for z in range(EXT[2]):
            at = (index // EXT[1], lax.rem(index, EXT[1]), z)
            value = slope[at]
            if z in (0, EXT[2] - 1):
                value = value * (high if z else low)
            full_ref[at + (slice(6, 7),)] = value
        return _

    lax.fori_loop(0, EXT[0] * EXT[1], finish, 0)


def force_kernel(
    full_ref, embed_ref, near_ref, held_ref, forces_ref, energy_ref, packed, sums, results, total_ref
):
    row = lax.broadcasted_iota(jnp.int32, (8, TILE), 0)
    lane = lax.broadcasted_iota(jnp.int32, (8, TILE), 1)
    masks = ((row < 3) | (row == 4) | (row == 5), (row == 3) | (row == 6), row == 7)
    tiles = OWN[0] * OWN[1] * OWN[2]

    def pack(index, _):
        x, y, z = tile_of(index, OWN)
        packed[index, 0] = full_ref[x + 1, y + 1, z + 1]
        filled = 0
        current = jnp.zeros((8, TILE), F32)
        for k, offset in enumerate(OFFSETS):
            held = held_ref[0, index * 32 + k]
            there = full_ref[tuple(a + 1 + o for a, o in zip((x, y, z), offset))]
            places = jnp.broadcast_to(near_ref[index, k : k + 1, :], (8, TILE))
            value = jnp.take_along_axis(there, places, axis=1, mode="promise_in_bounds")
            value = jnp.where(lane < held, value, 0.0)
            start = filled & (TILE - 1)
            value = pltpu.roll(value, start, 1)
            behind = lane >= start
            merged = jnp.where(behind, value, current)
            beyond = jnp.where(behind, 0.0, value)
            chunk = 1 + (filled >> 7)
            packed[index, chunk] = merged
            packed[index, chunk + 1] = beyond
            filled = filled + held
            current = jnp.where((filled >> 7) + 1 > chunk, beyond, merged)
        for k in range(GROUP):
            packed[index, 2 + (filled >> 7) + k] = jnp.zeros((8, TILE), F32)
        total_ref[index] = filled
        return _

    lax.fori_loop(0, tiles, pack, 0)

    def group(index, own, start, count, with_self):
        lanes = lax.broadcasted_iota(jnp.int32, (FORCE_PART, TILE), 1)
        values = [packed[index, start + k] for k in range(count)]
        features = [
            [beside_features(jnp.where(mask, value, 0.0)) for mask in masks] for value in values
        ]
        for part in range(TILE // FORCE_PART):
            rows = own[part * FORCE_PART : (part + 1) * FORCE_PART]
            total = [jnp.zeros((FORCE_PART, TILE), F32) for _ in range(5)]
            for k, value in enumerate(values):
                reach, both, pair = (
                    jnp.dot(rows, feature, preferred_element_type=F32) for feature in features[k]
                )
                q = jnp.maximum(reach, 0.0)
                if with_self and k == 0:
                    here = lax.broadcasted_iota(jnp.int32, (FORCE_PART, TILE), 0) + part * FORCE_PART
                    q = jnp.where(here == lanes, 0.0, q)
                square = q * q
                pull = square * (q * pair)
                coef = pull + square * both
                for comp in range(3):
                    total[comp] = total[comp] + coef * value[comp : comp + 1]
                total[3] = total[3] + coef
                total[4] = total[4] + pull * q
            column = jnp.zeros((FORCE_PART, TILE), F32)
            for k in range(5):
                column = jnp.where(lanes == k, jnp.sum(total[k], axis=1, keepdims=True), column)
            sums[part * FORCE_PART : (part + 1) * FORCE_PART, :] = column
        return sums[...].T[:8]

    def own_rows(value):
        out = jnp.where(row == 3, value[6:7], value)
        out = jnp.where(row == 4, 1.0 + value[5:6], out)
        out = jnp.where(row == 5, 1.0, out)
        return own_features(jnp.where(row == 6, value[3:4], out))

    def forces(index, _):
        value = packed[index, 0]
        own = own_rows(value)
        chunks = 1 + ((total_ref[index] + TILE - 1) >> 7)
        result = group(index, own, 0, GROUP, True)
        more = (chunks - GROUP + 1) // 2
        result = lax.fori_loop(
            0,
            jnp.maximum(more, 0),
            lambda step, carry: carry + group(index, own, GROUP + 2 * step, 2, False),
            result,
        )
        moved = (2.0 * BETA / SCALE) * (result - value * result[3:4])
        energy = embed_ref[index] + (0.5 * 0.09) * result[4:5]
        results[index] = jnp.where(row == 3, energy, moved)
        return _

    lax.fori_loop(0, tiles, forces, 0)
    for index in range(tiles):
        x, y, z = tile_of(index, OWN)
        for comp in range(3):
            forces_ref[comp, x, y, z : z + 1, :] = results[index, comp : comp + 1, :]
        energy_ref[x, y, z : z + 1, :] = results[index, 3:4, :]


def shards(sizes, positions, species, counts):
    vmem = pl.BlockSpec(memory_space=pltpu.VMEM)
    smem = pl.BlockSpec(memory_space=pltpu.SMEM)
    tiles = OWN[0] * OWN[1] * OWN[2]
    full, embed, near, held = pl.pallas_call(
        lambda *refs: exchange_kernel(sizes, *refs),
        name="exchange",
        out_shape=(
            jax.ShapeDtypeStruct(EXT + (8, TILE), F32),
            jax.ShapeDtypeStruct((tiles, 1, TILE), F32),
            jax.ShapeDtypeStruct((tiles, 32, TILE), jnp.int32),
            jax.ShapeDtypeStruct((1, tiles * 32), jnp.int32),
        ),
        in_specs=[vmem, vmem, smem],
        out_specs=(vmem, vmem, vmem, vmem),
        scratch_shapes=[
            pltpu.VMEM(EXT + (4, TILE), F32),
            pltpu.VMEM(EXT + (1, TILE), F32),
            pltpu.VMEM((EXT[0] * EXT[1], 48, EXT[2] * TILE), BF16),
            pltpu.VMEM((tiles, TILE, 48), BF16),
            pltpu.VMEM((tiles, TILE, TILE), F32),
            pltpu.VMEM((tiles, 32, TILE), F32),
            pltpu.SemaphoreType.DMA((2, len(OFFSETS))),
            pltpu.SemaphoreType.DMA((2, len(OFFSETS))),
        ],
        compiler_params=pltpu.CompilerParams(collective_id=0, has_side_effects=True),
    )(positions, species, counts)
    return pl.pallas_call(
        force_kernel,
        name="forces",
        out_shape=(
            jax.ShapeDtypeStruct((3,) + OWN + (TILE,), F32),
            jax.ShapeDtypeStruct(OWN + (TILE,), F32),
        ),
        in_specs=[vmem, vmem, vmem, smem],
        out_specs=(vmem, vmem),
        scratch_shapes=[
            pltpu.VMEM((tiles, 32 + GROUP, 8, TILE), F32),
            pltpu.VMEM((TILE, TILE), F32),
            pltpu.VMEM((tiles, 8, TILE), F32),
            pltpu.SMEM((tiles,), jnp.int32),
        ],
    )(full, embed, near, held)


def solution(mesh):
    placed = (P(None, "gx", "gy", "gz", None), P("gx", "gy", "gz", None), P("gx", "gy", "gz"))
    sizes = tuple(mesh.shape[name] for name in ("gx", "gy", "gz"))
    return jax.shard_map(
        lambda *args: shards(sizes, *args),
        mesh=mesh,
        in_specs=placed,
        out_specs=(P(None, "gx", "gy", "gz", None), P("gx", "gy", "gz", None)),
        check_vma=False,
    )
```

```python
import math

import jax
import jax.numpy as jnp
from jax import lax
from jax.experimental import pallas as pl
from jax.experimental.pallas import tpu as pltpu
from jax.sharding import PartitionSpec as P

F32 = jnp.float32
BF16 = jnp.bfloat16
MESH = pl.DeviceIdType.MESH
CUTOFF_SQUARED = 0.2025
SCALE = math.sqrt(2.0 / CUTOFF_SQUARED)
TILE = 128
OWN = (2, 2, 4)
EXT = (4, 4, 6)
OFFSETS = [
    (a, b, c) for a in (-1, 0, 1) for b in (-1, 0, 1) for c in (-1, 0, 1) if (a, b, c) != (0, 0, 0)
]
ALPHA = -3.0 / CUTOFF_SQUARED
BETA = -4.0 / CUTOFF_SQUARED * 0.09
SLOPE = ALPHA / (5.0 * BETA)
PART = 128
TILES = OWN[0] * OWN[1] * OWN[2]
UNROLL = 4
FORCE_PART = 64
GROUP = 6
HIGHEST = lax.Precision.HIGHEST
NT = (((1,), (1,)), ((), ()))


def pieces(v):
    first = v.astype(BF16).astype(F32)
    rest = v - first
    second = rest.astype(BF16).astype(F32)
    return first, second, rest - second


def beside_features(v):
    a, b, c = pieces(v)
    return jnp.concatenate([a, b, a, b, c, a], axis=0).astype(BF16)


def own_features(v):
    a, b, c = pieces(v)
    return jnp.concatenate([a, a, b, b, a, c], axis=0).T.astype(BF16)


def rows_of(*rows):
    row = lax.broadcasted_iota(jnp.int32, (8, TILE), 0)
    out = jnp.zeros((8, TILE), F32)
    for index, value in enumerate(rows):
        if value is not None:
            out = jnp.where(row == index, value, out)
    return out


def tile_of(index, extent):
    plane = extent[1] * extent[2]
    return index // plane, (index // extent[2]) % extent[1], index % extent[2]


def span(offset, own, sending):
    if offset == 0:
        return pl.ds(1, own)
    if sending:
        return pl.ds(own if offset > 0 else 1, 1)
    return pl.ds(0 if offset > 0 else own + 1, 1)


def region(offset, sending):
    return tuple(span(o, n, sending) for o, n in zip(offset, OWN))


def exchange_kernel(
    sizes,
    pos_ref,
    spec_ref,
    count_ref,
    full_ref,
    embed_ref,
    near_ref,
    begin_ref,
    used_ref,
    wire,
    slope,
    beside,
    own,
    totals,
    reach_rows,
    weights,
    columns_ref,
    sends,
    recvs,
):
    me = [lax.axis_index(name) for name in ("gx", "gy", "gz")]

    def peer(offset):
        return tuple(lax.rem(m + o + n, n) for m, o, n in zip(me, offset, sizes))

    barrier = pltpu.get_barrier_semaphore()
    for offset in OFFSETS:
        pl.semaphore_signal(barrier, inc=1, device_id=peer(offset), device_id_type=MESH)

    lane = lax.broadcasted_iota(jnp.int32, (1, TILE), 1)
    row4 = lax.broadcasted_iota(jnp.int32, (4, TILE), 0)
    for x in range(OWN[0]):
        for y in range(OWN[1]):
            for z in range(OWN[2]):
                kind = spec_ref[x, y, z : z + 1, :]
                weight = jnp.where(
                    lane < count_ref[x, y, z], jnp.where(kind == 1, 7.0, 5.0), 0.0
                )
                value = jnp.broadcast_to(weight, (4, TILE))
                for comp in range(3):
                    value = jnp.where(row4 == comp, pos_ref[comp, x, y, z : z + 1, :], value)
                wire[x + 1, y + 1, z + 1] = value
                index = (x * OWN[1] + y) * OWN[2] + z
                weights[index : index + 1, :] = weight
    pl.semaphore_wait(barrier, len(OFFSETS))

    def copies(ref, which):
        return [
            pltpu.make_async_remote_copy(
                src_ref=ref.at[region(offset, True)],
                dst_ref=ref.at[region(offset, False)],
                send_sem=sends.at[which, k],
                recv_sem=recvs.at[which, k],
                device_id=peer(offset),
                device_id_type=MESH,
            )
            for k, offset in enumerate(OFFSETS)
        ]

    state_copies = copies(wire, 0)
    for copy in state_copies:
        copy.start()

    low = (me[2] > 0).astype(F32)
    high = (me[2] < sizes[2] - 1).astype(F32)

    def prepare(x, y, z):
        value = wire[x, y, z]
        weight = value[3:4] * (low if z == 0 else high if z == EXT[2] - 1 else 1.0)
        cx = (value[0:1] + (x - 2).astype(F32)) * SCALE
        cy = (value[1:2] + (y - 2).astype(F32)) * SCALE
        cz = (value[2:3] + float(z - 3)) * SCALE
        norm = 0.5 * (cx * cx + cy * cy + cz * cz)
        root = jnp.where(weight > 6.0, 1.4 ** (1.0 / 3.0), jnp.where(weight > 0.0, 1.0, 0.0))
        pair = jnp.where(weight > 0.0, 0.5 * weight - 0.5, 0.0)
        full = rows_of(cx, cy, cz, weight, 1.0, -norm, None, pair)
        full_ref[x, y, z] = full
        row = lax.broadcasted_iota(jnp.int32, (8, TILE), 0)
        part = root * jnp.where(row == 3, 1.0, jnp.where(row == 4, -norm, full))
        beside[x * EXT[1] + y, :, z * TILE : (z + 1) * TILE] = beside_features(
            jnp.where(row < 5, part, 0.0)
        )
        return full

    def prepare_own(index, _):
        x, y = 1 + index // OWN[1], 1 + index % OWN[1]
        for z in (0, EXT[2] - 1):
            beside[x * EXT[1] + y, :, z * TILE : (z + 1) * TILE] = jnp.zeros((48, TILE), BF16)
        for z in range(OWN[2]):
            full = prepare(x, y, z + 1)
            row = lax.broadcasted_iota(jnp.int32, (8, TILE), 0)
            value = jnp.where(row == 3, 1.0 + full[5:6], jnp.where(row < 5, full, 0.0))
            own[index * OWN[2] + z] = own_features(value)
        return _

    lax.fori_loop(0, OWN[0] * OWN[1], prepare_own, 0)

    def cubes(rows, there):
        value = jnp.maximum(jnp.dot(rows, there, preferred_element_type=F32), 0.0)
        return value * value * value

    def blocks(value):
        return sum(
            value[:, k * TILE : (k + 1) * TILE] for k in range(1, value.shape[1] // TILE)
        ) + value[:, :TILE]

    def window(column, z, width=3):
        return beside[column, :, pl.ds(pl.multiple_of(z * TILE, TILE), width * TILE)]

    parts = TILE // PART

    def inner_tile(index):
        x, y, z = tile_of(index, OWN)
        for part in range(parts):
            cut = slice(part * PART, (part + 1) * PART)
            rows = own[index, cut]
            total = jnp.zeros((PART, TILE), F32)
            for dx in range(OWN[0]):
                for dy in range(OWN[1]):
                    there = lax.rem(x + dx, OWN[0]) + 1, lax.rem(y + dy, OWN[1]) + 1
                    cube = cubes(rows, window(there[0] * EXT[1] + there[1], z))
                    if (dx, dy) == (0, 0):
                        here = lax.broadcasted_iota(jnp.int32, (PART, TILE), 0) + part * PART
                        self_pair = here == lax.broadcasted_iota(jnp.int32, (PART, TILE), 1)
                        middle = jnp.where(self_pair, 0.0, cube[:, TILE : 2 * TILE])
                        total = total + cube[:, :TILE] + middle + cube[:, 2 * TILE :]
                    else:
                        total = total + blocks(cube)
            totals[index, cut] = total

    def inner(step, _):
        for k in range(UNROLL):
            inner_tile(step * UNROLL + k)
        return _

    lax.fori_loop(0, TILES // UNROLL, inner, 0)

    for copy in state_copies:
        copy.wait()

    def prepare_side(index, _):
        x = jnp.where(index < 4, 0, jnp.where(index < 8, EXT[0] - 1, 1 + (index - 8) // 2))
        y = jnp.where(index < 8, lax.rem(index, 4), (EXT[1] - 1) * lax.rem(index, 2))
        for z in range(EXT[2]):
            prepare(x, y, z)
        return _

    lax.fori_loop(0, EXT[0] * EXT[1] - OWN[0] * OWN[1], prepare_side, 0)

    def prepare_ends(index, _):
        for z in (0, EXT[2] - 1):
            prepare(1 + index // OWN[1], 1 + index % OWN[1], z)
        return _

    lax.fori_loop(0, OWN[0] * OWN[1], prepare_ends, 0)

    def ends(index, _):
        column, upper = index // 2, lax.rem(index, 2)
        tile = column * OWN[2] + upper * (OWN[2] - 1)
        for part in range(parts):
            cut = slice(part * PART, (part + 1) * PART)
            rows = own[tile, cut]
            total = totals[tile, cut]
            for x in range(OWN[0]):
                for y in range(OWN[1]):
                    there = (x + 1) * EXT[1] + y + 1
                    total = total + cubes(rows, window(there, upper * (EXT[2] - 1), 1))
            totals[tile, cut] = total
        return _

    lax.fori_loop(0, 2 * OWN[0] * OWN[1], ends, 0)

    lanes = lax.broadcasted_iota(jnp.int32, (TILE, TILE), 1)

    def outer_tile(index):
        x, y, z = tile_of(index, OWN)
        side_x, side_y = x * (EXT[0] - 1), y * (EXT[1] - 1)
        columns = [side_x * EXT[1] + y + dy for dy in range(3)]
        columns += [(dx + 1) * EXT[1] + side_y for dx in range(OWN[0])]
        total = totals[index]
        for column in columns:
            total = total + blocks(cubes(own[index], window(column, z)))
        return jnp.sum(total, axis=1, keepdims=True)

    def outer(step, _):
        value = columns_ref[...]
        for k in range(UNROLL):
            index = step * UNROLL + k
            value = jnp.where(lanes == index, outer_tile(index), value)
        columns_ref[...] = value
        return _

    lax.fori_loop(0, TILES // UNROLL, outer, 0)
    root = jnp.sqrt(1.0 + columns_ref[...].T[:TILES])
    weight = weights[...]
    strength = jnp.where(weight > 6.0, 0.7, jnp.where(weight > 0.0, 1.0, 0.0))
    embed_ref[...] = -strength * root
    rows = -0.5 * SLOPE * strength / root
    for index in range(TILES):
        x, y, z = tile_of(index, OWN)
        slope[x + 1, y + 1, z + 1] = rows[index : index + 1]

    slope_copies = copies(slope, 1)
    for copy in slope_copies:
        copy.start()

    def distances(index, _):
        x, y, z = tile_of(index, OWN)
        for k, offset in enumerate(OFFSETS):
            at = tuple(a + 1 + o for a, o in zip((x, y, z), offset))
            there = wire[at]
            far = None
            for comp, o in enumerate(offset):
                if o:
                    gap = there[comp : comp + 1] if o > 0 else 1.0 - there[comp : comp + 1]
                    far = gap * gap if far is None else far + gap * gap
            weight = full_ref[at + (slice(3, 4),)]
            reach_rows[index, k : k + 1, :] = jnp.where(weight > 0.0, far, 9.0)
        for k in range(len(OFFSETS), 32):
            reach_rows[index, k : k + 1, :] = jnp.full((1, TILE), 9.0, F32)
        return _

    lax.fori_loop(0, OWN[0] * OWN[1] * OWN[2], distances, 0)

    first = lax.broadcasted_iota(jnp.int32, (TILE, TILE), 0)
    second = lax.broadcasted_iota(jnp.int32, (TILE, TILE), 1)
    earlier = (first < second).astype(F32).astype(BF16)
    ones = jnp.ones((TILE, TILE), BF16)
    above_rows = ((second < first) & (second // 32 == first // 32)).astype(F32).astype(BF16)
    first_lane = (lax.broadcasted_iota(jnp.int32, (8, TILE), 1) == 0).astype(F32).astype(BF16)

    def compress(group, _):
        rows = reach_rows[pl.ds(group * 4, 4)].reshape(TILE, TILE)
        near = rows < CUTOFF_SQUARED * 1.00002
        flags = near.astype(F32).astype(BF16)
        before = jnp.dot(flags, earlier, preferred_element_type=F32).astype(jnp.int32)
        held = jnp.dot(flags, ones, preferred_element_type=F32).astype(BF16)
        filled = jnp.dot(above_rows, held, preferred_element_type=F32).astype(jnp.int32)
        word = jnp.where(near, 16384 + second * 128 + (second - before), 0)
        for bit in range(7):
            moved = pltpu.roll(word, TILE - (1 << bit), 1)
            stay = jnp.where((word & (1 << bit)) != 0, 0, word)
            word = jnp.where((moved & (1 << bit)) != 0, moved, stay)
        for bit in range(7):
            word = jnp.where((filled & (1 << bit)) != 0, pltpu.roll(word, 1 << bit, 1), word)
        start = filled & (TILE - 1)
        code = ((word >> 7) & 127) + jnp.where(second < start, TILE, 0)
        near_ref[pl.ds(group * 4, 4)] = jnp.where(word >= 16384, code, 512).reshape(4, 32, TILE)
        cut = pl.ds(pl.multiple_of(group * TILE, TILE), TILE)
        for ref, value in (
            (begin_ref, 1 + (filled >> 7)),
            (used_ref, 1 + ((filled + TILE - 1) >> 7)),
        ):
            value = value.astype(F32).astype(BF16)
            value = lax.dot_general(first_lane, value, NT, preferred_element_type=F32)
            ref[:, cut] = value[0:1].astype(jnp.int32)
        return _

    lax.fori_loop(0, 4, compress, 0)

    for copy in slope_copies:
        copy.wait()

    def finish(index, _):
        for z in range(EXT[2]):
            at = (index // EXT[1], lax.rem(index, EXT[1]), z)
            value = slope[at]
            if z in (0, EXT[2] - 1):
                value = value * (high if z else low)
            full_ref[at + (slice(6, 7),)] = value
        return _

    lax.fori_loop(0, EXT[0] * EXT[1], finish, 0)


def force_kernel(
    full_ref, embed_ref, near_ref, begin_ref, used_ref, forces_ref, energy_ref, packed, sums, results
):
    row = lax.broadcasted_iota(jnp.int32, (8, TILE), 0)

    def pack_tile(index):
        x, y, z = tile_of(index, OWN)
        packed[index, 0] = full_ref[x + 1, y + 1, z + 1]
        current = jnp.zeros((8, TILE), F32)
        chunk = begin_ref[0, index * 32]
        for k, offset in enumerate(OFFSETS):
            there = full_ref[tuple(a + 1 + o for a, o in zip((x, y, z), offset))]
            code = jnp.broadcast_to(near_ref[index, k : k + 1, :], (8, TILE))
            places = code & (TILE - 1)
            value = jnp.take_along_axis(there, places, axis=1, mode="promise_in_bounds")
            merged = jnp.where(code < TILE, value, current)
            beyond = jnp.where((code & TILE) != 0, value, 0.0)
            packed[index, chunk] = merged
            packed[index, chunk + 1] = beyond
            later = begin_ref[0, index * 32 + k + 1]
            current = jnp.where(later > chunk, beyond, merged)
            chunk = later
        for k in range(1, GROUP + 1):
            packed[index, chunk + k] = jnp.zeros((8, TILE), F32)

    def pack(step, _):
        for k in range(UNROLL):
            pack_tile(step * UNROLL + k)
        return _

    lax.fori_loop(0, TILES // UNROLL, pack, 0)

    def group(index, own, start, count, with_self, room):
        shape = (FORCE_PART, TILE)
        lanes = lax.broadcasted_iota(jnp.int32, shape, 1)
        values = [packed[index, start + k] for k in range(count)]
        features = [
            jnp.concatenate([beside_features(value) for value in values[k : k + 2]], axis=1)
            for k in range(0, count, 2)
        ]
        for part in range(TILE // FORCE_PART):
            cut = slice(part * FORCE_PART, (part + 1) * FORCE_PART)
            total = [jnp.zeros(shape, F32) for _ in range(5)]
            for pair_index, feature in enumerate(features):
                products = [
                    jnp.dot(rows[cut], feature, preferred_element_type=F32) for rows in own
                ]
                for side in range(2):
                    k = 2 * pair_index + side
                    value = values[k]
                    reach, both, pair = (
                        product[:, side * TILE : (side + 1) * TILE] for product in products
                    )
                    q = jnp.maximum(reach, 0.0)
                    if with_self and k == 0:
                        here = lax.broadcasted_iota(jnp.int32, shape, 0) + part * FORCE_PART
                        q = jnp.where(here == lanes, 0.0, q)
                    square = q * q
                    pull = square * (q * pair)
                    coef = pull + square * both
                    for comp in range(3):
                        total[comp] = total[comp] + coef * value[comp : comp + 1]
                    total[3] = total[3] + coef
                    total[4] = total[4] + pull * q
            column = jnp.zeros(shape, F32)
            for k in range(5):
                column = jnp.where(lanes == k, jnp.sum(total[k], axis=1, keepdims=True), column)
            sums[room, cut, :] = column
        return sums[room].T[:8]

    def own_rows(value):
        out = jnp.where(row == 3, value[6:7], value)
        out = jnp.where(row == 4, 1.0 + value[5:6], out)
        out = jnp.where(row == 5, 1.0, out)
        a, b, c = pieces(jnp.where(row == 6, value[3:4], out))
        columns = jnp.concatenate([a, a, b, b, a, c], axis=0).T
        place = lax.broadcasted_iota(jnp.int32, columns.shape, 1) % 8
        masks = ((place < 3) | (place == 4) | (place == 5), (place == 3) | (place == 6), place == 7)
        return [jnp.where(mask, columns, 0.0).astype(BF16) for mask in masks]

    def forces(step, _):
        done = []
        for k in range(UNROLL):
            index = step * UNROLL + k
            own = own_rows(packed[index, 0])
            done.append((index, own, group(index, own, 0, GROUP, True, k)))
        for k, (index, own, result) in enumerate(done):
            results[index] = result
            more = (used_ref[0, index * 32 + 31] - GROUP + 1) // 2

            def further(extra, _, index=index, own=own, k=k):
                results[index] += group(index, own, GROUP + 2 * extra, 2, False, k)
                return _

            lax.fori_loop(0, jnp.maximum(more, 0), further, 0)
        return _

    lax.fori_loop(0, TILES // UNROLL, forces, 0)
    for index in range(TILES):
        x, y, z = tile_of(index, OWN)
        result = results[index]
        moved = (2.0 * BETA / SCALE) * (result - packed[index, 0] * result[3:4])
        for comp in range(3):
            forces_ref[comp, x, y, z : z + 1, :] = moved[comp : comp + 1]
        energy_ref[x, y, z : z + 1, :] = embed_ref[index : index + 1] + 0.045 * result[4:5]


def shards(sizes, positions, species, counts):
    vmem = pl.BlockSpec(memory_space=pltpu.VMEM)
    smem = pl.BlockSpec(memory_space=pltpu.SMEM)
    tiles = OWN[0] * OWN[1] * OWN[2]
    full, embed, near, begin, used = pl.pallas_call(
        lambda *refs: exchange_kernel(sizes, *refs),
        name="exchange",
        out_shape=(
            jax.ShapeDtypeStruct(EXT + (8, TILE), F32),
            jax.ShapeDtypeStruct((tiles, TILE), F32),
            jax.ShapeDtypeStruct((tiles, 32, TILE), jnp.int32),
            jax.ShapeDtypeStruct((1, tiles * 32), jnp.int32),
            jax.ShapeDtypeStruct((1, tiles * 32), jnp.int32),
        ),
        in_specs=[vmem, vmem, smem],
        out_specs=(vmem,) * 5,
        scratch_shapes=[
            pltpu.VMEM(EXT + (4, TILE), F32),
            pltpu.VMEM(EXT + (1, TILE), F32),
            pltpu.VMEM((EXT[0] * EXT[1], 48, EXT[2] * TILE), BF16),
            pltpu.VMEM((tiles, TILE, 48), BF16),
            pltpu.VMEM((tiles, TILE, TILE), F32),
            pltpu.VMEM((tiles, 32, TILE), F32),
            pltpu.VMEM((tiles, TILE), F32),
            pltpu.VMEM((TILE, TILE), F32),
            pltpu.SemaphoreType.DMA((2, len(OFFSETS))),
            pltpu.SemaphoreType.DMA((2, len(OFFSETS))),
        ],
        compiler_params=pltpu.CompilerParams(collective_id=0, has_side_effects=True, vmem_limit_bytes=24 << 20),
    )(positions, species, counts)
    return pl.pallas_call(
        force_kernel,
        name="forces",
        out_shape=(
            jax.ShapeDtypeStruct((3,) + OWN + (TILE,), F32),
            jax.ShapeDtypeStruct(OWN + (TILE,), F32),
        ),
        in_specs=[vmem, vmem, vmem, smem, smem],
        out_specs=(vmem, vmem),
        scratch_shapes=[
            pltpu.VMEM((tiles, 32 + GROUP, 8, TILE), F32),
            pltpu.VMEM((UNROLL, TILE, TILE), F32),
            pltpu.VMEM((tiles, 8, TILE), F32),
        ],
        compiler_params=pltpu.CompilerParams(vmem_limit_bytes=24 << 20),
    )(full, embed, near, begin, used)


def solution(mesh):
    placed = (P(None, "gx", "gy", "gz", None), P("gx", "gy", "gz", None), P("gx", "gy", "gz"))
    sizes = tuple(mesh.shape[name] for name in ("gx", "gy", "gz"))
    return jax.shard_map(
        lambda *args: shards(sizes, *args),
        mesh=mesh,
        in_specs=placed,
        out_specs=(P(None, "gx", "gy", "gz", None), P("gx", "gy", "gz", None)),
        check_vma=False,
    )
```

```python
import math

import jax
import jax.numpy as jnp
from jax import lax
from jax.experimental import pallas as pl
from jax.experimental.pallas import tpu as pltpu
from jax.sharding import PartitionSpec as P

F32 = jnp.float32
BF16 = jnp.bfloat16
MESH = pl.DeviceIdType.MESH
CUTOFF_SQUARED = 0.2025
SCALE = math.sqrt(2.0 / CUTOFF_SQUARED)
TILE = 128
OWN = (2, 2, 4)
EXT = (4, 4, 6)
OFFSETS = sorted(
    [(a, b, c) for a in (-1, 0, 1) for b in (-1, 0, 1) for c in (-1, 0, 1) if a or b or c],
    key=lambda offset: -sum(map(abs, offset)),
)
ALPHA = -3.0 / CUTOFF_SQUARED
BETA = -4.0 / CUTOFF_SQUARED * 0.09
SLOPE = ALPHA / (5.0 * BETA)
PART = 128
TILES = OWN[0] * OWN[1] * OWN[2]
UNROLL = 4
FORCE_PART = 64
GROUP = 6
HIGHEST = lax.Precision.HIGHEST
NT = (((1,), (1,)), ((), ()))


def pieces(v):
    first = v.astype(BF16).astype(F32)
    rest = v - first
    second = rest.astype(BF16).astype(F32)
    return first, second, rest - second


def beside_features(v):
    a, b, c = pieces(v)
    return jnp.concatenate([a, b, a, b, c, a], axis=0).astype(BF16)


def own_features(v):
    a, b, c = pieces(v)
    return jnp.concatenate([a, a, b, b, a, c], axis=0).T.astype(BF16)


def rows_of(*rows):
    row = lax.broadcasted_iota(jnp.int32, (8, TILE), 0)
    out = jnp.zeros((8, TILE), F32)
    for index, value in enumerate(rows):
        if value is not None:
            out = jnp.where(row == index, value, out)
    return out


def tile_of(index, extent):
    plane = extent[1] * extent[2]
    return index // plane, (index // extent[2]) % extent[1], index % extent[2]


def span(offset, own, sending):
    if offset == 0:
        return pl.ds(1, own)
    if sending:
        return pl.ds(own if offset > 0 else 1, 1)
    return pl.ds(0 if offset > 0 else own + 1, 1)


def region(offset, sending):
    return tuple(span(o, n, sending) for o, n in zip(offset, OWN))


def exchange_kernel(
    sizes,
    pos_hbm,
    spec_hbm,
    count_hbm,
    full_ref,
    embed_ref,
    near_ref,
    begin_ref,
    used_ref,
    wire,
    slope,
    beside,
    own,
    totals,
    reach_rows,
    weights,
    columns_ref,
    pos_ref,
    spec_ref,
    count_ref,
    loads,
    sends,
    recvs,
):
    arrivals = [
        pltpu.make_async_copy(source, target, loads.at[k])
        for k, (source, target) in enumerate(
            ((count_hbm, count_ref), (pos_hbm, pos_ref), (spec_hbm, spec_ref))
        )
    ]
    for copy in arrivals:
        copy.start()
    me = [lax.axis_index(name) for name in ("gx", "gy", "gz")]

    def peer(offset):
        return tuple(lax.rem(m + o + n, n) for m, o, n in zip(me, offset, sizes))

    barrier = pltpu.get_barrier_semaphore()
    for offset in OFFSETS:
        pl.semaphore_signal(barrier, inc=1, device_id=peer(offset), device_id_type=MESH)

    for copy in arrivals:
        copy.wait()
    lane = lax.broadcasted_iota(jnp.int32, (1, TILE), 1)
    row4 = lax.broadcasted_iota(jnp.int32, (4, TILE), 0)
    for x in range(OWN[0]):
        for y in range(OWN[1]):
            for z in range(OWN[2]):
                kind = spec_ref[x, y, z : z + 1, :]
                weight = jnp.where(
                    lane < count_ref[x, y, z], jnp.where(kind == 1, 7.0, 5.0), 0.0
                )
                value = jnp.broadcast_to(weight, (4, TILE))
                for comp in range(3):
                    value = jnp.where(row4 == comp, pos_ref[comp, x, y, z : z + 1, :], value)
                wire[x + 1, y + 1, z + 1] = value
                index = (x * OWN[1] + y) * OWN[2] + z
                weights[index : index + 1, :] = weight
    pl.semaphore_wait(barrier, len(OFFSETS))

    def copies(ref, which):
        return [
            pltpu.make_async_remote_copy(
                src_ref=ref.at[region(offset, True)],
                dst_ref=ref.at[region(offset, False)],
                send_sem=sends.at[which, k],
                recv_sem=recvs.at[which, k],
                device_id=peer(offset),
                device_id_type=MESH,
            )
            for k, offset in enumerate(OFFSETS)
        ]

    state_copies = copies(wire, 0)
    for copy in state_copies:
        copy.start()

    low = (me[2] > 0).astype(F32)
    high = (me[2] < sizes[2] - 1).astype(F32)

    def prepare(x, y, z):
        value = wire[x, y, z]
        weight = value[3:4] * (low if z == 0 else high if z == EXT[2] - 1 else 1.0)
        cx = (value[0:1] + (x - 2).astype(F32)) * SCALE
        cy = (value[1:2] + (y - 2).astype(F32)) * SCALE
        cz = (value[2:3] + float(z - 3)) * SCALE
        norm = 0.5 * (cx * cx + cy * cy + cz * cz)
        root = jnp.where(weight > 6.0, 1.4 ** (1.0 / 3.0), jnp.where(weight > 0.0, 1.0, 0.0))
        pair = jnp.where(weight > 0.0, 0.5 * weight - 0.5, 0.0)
        full = rows_of(cx, cy, cz, weight, 1.0, -norm, None, pair)
        full_ref[x, y, z] = full
        row = lax.broadcasted_iota(jnp.int32, (8, TILE), 0)
        part = root * jnp.where(row == 3, 1.0, jnp.where(row == 4, -norm, full))
        beside[x * EXT[1] + y, :, z * TILE : (z + 1) * TILE] = beside_features(
            jnp.where(row < 5, part, 0.0)
        )
        return full

    def prepare_own(index, _):
        x, y = 1 + index // OWN[1], 1 + index % OWN[1]
        for z in (0, EXT[2] - 1):
            beside[x * EXT[1] + y, :, z * TILE : (z + 1) * TILE] = jnp.zeros((48, TILE), BF16)
        for z in range(OWN[2]):
            full = prepare(x, y, z + 1)
            row = lax.broadcasted_iota(jnp.int32, (8, TILE), 0)
            value = jnp.where(row == 3, 1.0 + full[5:6], jnp.where(row < 5, full, 0.0))
            own[index * OWN[2] + z] = own_features(value)
        return _

    lax.fori_loop(0, OWN[0] * OWN[1], prepare_own, 0)

    def cubes(rows, there):
        value = jnp.maximum(jnp.dot(rows, there, preferred_element_type=F32), 0.0)
        return value * value * value

    def blocks(value):
        return sum(
            value[:, k * TILE : (k + 1) * TILE] for k in range(1, value.shape[1] // TILE)
        ) + value[:, :TILE]

    def window(column, z, width=3):
        return beside[column, :, pl.ds(pl.multiple_of(z * TILE, TILE), width * TILE)]

    parts = TILE // PART

    def inner_tile(index):
        x, y, z = tile_of(index, OWN)
        for part in range(parts):
            cut = slice(part * PART, (part + 1) * PART)
            rows = own[index, cut]
            total = jnp.zeros((PART, TILE), F32)
            for dx in range(OWN[0]):
                for dy in range(OWN[1]):
                    there = lax.rem(x + dx, OWN[0]) + 1, lax.rem(y + dy, OWN[1]) + 1
                    cube = cubes(rows, window(there[0] * EXT[1] + there[1], z))
                    if (dx, dy) == (0, 0):
                        here = lax.broadcasted_iota(jnp.int32, (PART, TILE), 0) + part * PART
                        self_pair = here == lax.broadcasted_iota(jnp.int32, (PART, TILE), 1)
                        middle = jnp.where(self_pair, 0.0, cube[:, TILE : 2 * TILE])
                        total = total + cube[:, :TILE] + middle + cube[:, 2 * TILE :]
                    else:
                        total = total + blocks(cube)
            totals[index, cut] = total

    def inner(step, _):
        for k in range(UNROLL):
            inner_tile(step * UNROLL + k)
        return _

    lax.fori_loop(0, TILES // UNROLL, inner, 0)

    for copy in state_copies:
        copy.wait_recv()

    def prepare_side(index, _):
        x = jnp.where(index < 4, 0, jnp.where(index < 8, EXT[0] - 1, 1 + (index - 8) // 2))
        y = jnp.where(index < 8, lax.rem(index, 4), (EXT[1] - 1) * lax.rem(index, 2))
        for z in range(EXT[2]):
            prepare(x, y, z)
        return _

    lax.fori_loop(0, EXT[0] * EXT[1] - OWN[0] * OWN[1], prepare_side, 0)

    def prepare_ends(index, _):
        for z in (0, EXT[2] - 1):
            prepare(1 + index // OWN[1], 1 + index % OWN[1], z)
        return _

    lax.fori_loop(0, OWN[0] * OWN[1], prepare_ends, 0)

    def ends_tile(index):
        column, upper = index // 2, lax.rem(index, 2)
        tile = column * OWN[2] + upper * (OWN[2] - 1)
        for part in range(parts):
            cut = slice(part * PART, (part + 1) * PART)
            rows = own[tile, cut]
            total = totals[tile, cut]
            for x in range(OWN[0]):
                for y in range(OWN[1]):
                    there = (x + 1) * EXT[1] + y + 1
                    total = total + cubes(rows, window(there, upper * (EXT[2] - 1), 1))
            totals[tile, cut] = total

    def ends(step, _):
        for k in range(UNROLL):
            ends_tile(step * UNROLL + k)
        return _

    lax.fori_loop(0, 2 * OWN[0] * OWN[1] // UNROLL, ends, 0)

    lanes = lax.broadcasted_iota(jnp.int32, (TILE, TILE), 1)

    def outer_tile(index):
        x, y, z = tile_of(index, OWN)
        side_x, side_y = x * (EXT[0] - 1), y * (EXT[1] - 1)
        columns = [side_x * EXT[1] + y + dy for dy in range(3)]
        columns += [(dx + 1) * EXT[1] + side_y for dx in range(OWN[0])]
        total = totals[index]
        for column in columns:
            total = total + blocks(cubes(own[index], window(column, z)))
        return jnp.sum(total, axis=1, keepdims=True)

    def outer(step, _):
        value = columns_ref[...]
        for k in range(UNROLL):
            index = step * UNROLL + k
            value = jnp.where(lanes == index, outer_tile(index), value)
        columns_ref[...] = value
        return _

    lax.fori_loop(0, TILES // UNROLL, outer, 0)
    root = jnp.sqrt(1.0 + columns_ref[...].T[:TILES])
    weight = weights[...]
    strength = jnp.where(weight > 6.0, 0.7, jnp.where(weight > 0.0, 1.0, 0.0))
    embed_ref[...] = -strength * root
    rows = -0.5 * SLOPE * strength / root
    for index in range(TILES):
        x, y, z = tile_of(index, OWN)
        slope[x + 1, y + 1, z + 1] = rows[index : index + 1]

    slope_copies = copies(slope, 1)
    for copy in slope_copies:
        copy.start()

    def distances(index, _):
        x, y, z = tile_of(index, OWN)
        for k, offset in enumerate(OFFSETS):
            at = tuple(a + 1 + o for a, o in zip((x, y, z), offset))
            there = wire[at]
            far = None
            for comp, o in enumerate(offset):
                if o:
                    gap = there[comp : comp + 1] if o > 0 else 1.0 - there[comp : comp + 1]
                    far = gap * gap if far is None else far + gap * gap
            weight = full_ref[at + (slice(3, 4),)]
            reach_rows[index, k : k + 1, :] = jnp.where(weight > 0.0, far, 9.0)
        for k in range(len(OFFSETS), 32):
            reach_rows[index, k : k + 1, :] = jnp.full((1, TILE), 9.0, F32)
        return _

    lax.fori_loop(0, OWN[0] * OWN[1] * OWN[2], distances, 0)

    first = lax.broadcasted_iota(jnp.int32, (TILE, TILE), 0)
    second = lax.broadcasted_iota(jnp.int32, (TILE, TILE), 1)
    earlier = (first < second).astype(F32).astype(BF16)
    ones = jnp.ones((TILE, TILE), BF16)
    above_rows = ((second < first) & (second // 32 == first // 32)).astype(F32).astype(BF16)
    first_lane = (lax.broadcasted_iota(jnp.int32, (8, TILE), 1) == 0).astype(F32).astype(BF16)

    def compress(group, _):
        rows = reach_rows[pl.ds(group * 4, 4)].reshape(TILE, TILE)
        near = rows < CUTOFF_SQUARED * 1.00002
        flags = near.astype(F32).astype(BF16)
        before = jnp.dot(flags, earlier, preferred_element_type=F32).astype(jnp.int32)
        held = jnp.dot(flags, ones, preferred_element_type=F32).astype(BF16)
        filled = jnp.dot(above_rows, held, preferred_element_type=F32).astype(jnp.int32)
        word = jnp.where(near, 16384 + second * 128 + (second - before), 0)
        for bit in range(7):
            moved = pltpu.roll(word, TILE - (1 << bit), 1)
            stay = jnp.where((word & (1 << bit)) != 0, 0, word)
            word = jnp.where((moved & (1 << bit)) != 0, moved, stay)
        for bit in range(7):
            word = jnp.where((filled & (1 << bit)) != 0, pltpu.roll(word, 1 << bit, 1), word)
        start = filled & (TILE - 1)
        code = ((word >> 7) & 127) + jnp.where(second < start, TILE, 0)
        near_ref[pl.ds(group * 4, 4)] = jnp.where(word >= 16384, code, 512).reshape(4, 32, TILE)
        cut = pl.ds(pl.multiple_of(group * TILE, TILE), TILE)
        for ref, value in (
            (begin_ref, 1 + (filled >> 7)),
            (used_ref, 1 + ((filled + TILE - 1) >> 7)),
        ):
            value = value.astype(F32).astype(BF16)
            value = lax.dot_general(first_lane, value, NT, preferred_element_type=F32)
            ref[:, cut] = value[0:1].astype(jnp.int32)
        return _

    lax.fori_loop(0, 4, compress, 0)

    for copy in state_copies:
        copy.wait_send()
    for copy in slope_copies:
        copy.wait_recv()

    def finish(index, _):
        for z in range(EXT[2]):
            at = (index // EXT[1], lax.rem(index, EXT[1]), z)
            value = slope[at]
            if z in (0, EXT[2] - 1):
                value = value * (high if z else low)
            full_ref[at + (slice(6, 7),)] = value
        return _

    lax.fori_loop(0, EXT[0] * EXT[1], finish, 0)
    for copy in slope_copies:
        copy.wait_send()


def force_kernel(
    full_ref, embed_ref, near_ref, begin_ref, used_ref, forces_ref, energy_ref, packed, sums, results
):
    row = lax.broadcasted_iota(jnp.int32, (8, TILE), 0)

    def pack_tile(index):
        x, y, z = tile_of(index, OWN)
        packed[index, 0] = full_ref[x + 1, y + 1, z + 1]
        current = jnp.zeros((8, TILE), F32)
        chunk = begin_ref[0, index * 32]
        for k, offset in enumerate(OFFSETS):
            there = full_ref[tuple(a + 1 + o for a, o in zip((x, y, z), offset))]
            code = jnp.broadcast_to(near_ref[index, k : k + 1, :], (8, TILE))
            places = code & (TILE - 1)
            value = jnp.take_along_axis(there, places, axis=1, mode="promise_in_bounds")
            merged = jnp.where(code < TILE, value, current)
            beyond = jnp.where((code & TILE) != 0, value, 0.0)
            packed[index, chunk] = merged
            packed[index, chunk + 1] = beyond
            later = begin_ref[0, index * 32 + k + 1]
            current = jnp.where(later > chunk, beyond, merged)
            chunk = later
        for k in range(1, GROUP + 1):
            packed[index, chunk + k] = jnp.zeros((8, TILE), F32)

    def pack(step, _):
        for k in range(UNROLL):
            pack_tile(step * UNROLL + k)
        return _

    lax.fori_loop(0, TILES // UNROLL, pack, 0)

    def group(index, own, start, count, with_self, room):
        shape = (FORCE_PART, TILE)
        lanes = lax.broadcasted_iota(jnp.int32, shape, 1)
        values = [packed[index, start + k] for k in range(count)]
        features = [
            jnp.concatenate([beside_features(value) for value in values[k : k + 2]], axis=1)
            for k in range(0, count, 2)
        ]
        for part in range(TILE // FORCE_PART):
            cut = slice(part * FORCE_PART, (part + 1) * FORCE_PART)
            total = [jnp.zeros(shape, F32) for _ in range(5)]
            for pair_index, feature in enumerate(features):
                products = [
                    jnp.dot(rows[cut], feature, preferred_element_type=F32) for rows in own
                ]
                for side in range(2):
                    k = 2 * pair_index + side
                    value = values[k]
                    reach, both, pair = (
                        product[:, side * TILE : (side + 1) * TILE] for product in products
                    )
                    q = jnp.maximum(reach, 0.0)
                    if with_self and k == 0:
                        here = lax.broadcasted_iota(jnp.int32, shape, 0) + part * FORCE_PART
                        q = jnp.where(here == lanes, 0.0, q)
                    square = q * q
                    pull = square * (q * pair)
                    coef = pull + square * both
                    for comp in range(3):
                        total[comp] = total[comp] + coef * value[comp : comp + 1]
                    total[3] = total[3] + coef
                    total[4] = total[4] + pull * q
            column = jnp.zeros(shape, F32)
            for k in range(5):
                column = jnp.where(lanes == k, jnp.sum(total[k], axis=1, keepdims=True), column)
            sums[room, cut, :] = column
        return sums[room].T[:8]

    def own_rows(value):
        out = jnp.where(row == 3, value[6:7], value)
        out = jnp.where(row == 4, 1.0 + value[5:6], out)
        out = jnp.where(row == 5, 1.0, out)
        a, b, c = pieces(jnp.where(row == 6, value[3:4], out))
        columns = jnp.concatenate([a, a, b, b, a, c], axis=0).T
        place = lax.broadcasted_iota(jnp.int32, columns.shape, 1) % 8
        masks = ((place < 3) | (place == 4) | (place == 5), (place == 3) | (place == 6), place == 7)
        return [jnp.where(mask, columns, 0.0).astype(BF16) for mask in masks]

    def forces(step, _):
        done = []
        for k in range(UNROLL):
            index = step * UNROLL + k
            own = own_rows(packed[index, 0])
            done.append((index, own, group(index, own, 0, GROUP, True, k)))
        for k, (index, own, result) in enumerate(done):
            results[index] = result
            more = (used_ref[0, index * 32 + 31] - GROUP + 1) // 2

            def further(extra, _, index=index, own=own, k=k):
                results[index] += group(index, own, GROUP + 2 * extra, 2, False, k)
                return _

            lax.fori_loop(0, jnp.maximum(more, 0), further, 0)
        return _

    lax.fori_loop(0, TILES // UNROLL, forces, 0)
    for index in range(TILES):
        x, y, z = tile_of(index, OWN)
        result = results[index]
        moved = (2.0 * BETA / SCALE) * (result - packed[index, 0] * result[3:4])
        for comp in range(3):
            forces_ref[comp, x, y, z : z + 1, :] = moved[comp : comp + 1]
        energy_ref[x, y, z : z + 1, :] = embed_ref[index : index + 1] + 0.045 * result[4:5]


def shards(sizes, positions, species, counts):
    vmem = pl.BlockSpec(memory_space=pltpu.VMEM)
    smem = pl.BlockSpec(memory_space=pltpu.SMEM)
    tiles = OWN[0] * OWN[1] * OWN[2]
    full, embed, near, begin, used = pl.pallas_call(
        lambda *refs: exchange_kernel(sizes, *refs),
        name="exchange",
        out_shape=(
            jax.ShapeDtypeStruct(EXT + (8, TILE), F32),
            jax.ShapeDtypeStruct((tiles, TILE), F32),
            jax.ShapeDtypeStruct((tiles, 32, TILE), jnp.int32),
            jax.ShapeDtypeStruct((1, tiles * 32), jnp.int32),
            jax.ShapeDtypeStruct((1, tiles * 32), jnp.int32),
        ),
        in_specs=[pl.BlockSpec(memory_space=pltpu.HBM)] * 3,
        out_specs=(vmem,) * 5,
        scratch_shapes=[
            pltpu.VMEM(EXT + (4, TILE), F32),
            pltpu.VMEM(EXT + (1, TILE), F32),
            pltpu.VMEM((EXT[0] * EXT[1], 48, EXT[2] * TILE), BF16),
            pltpu.VMEM((tiles, TILE, 48), BF16),
            pltpu.VMEM((tiles, TILE, TILE), F32),
            pltpu.VMEM((tiles, 32, TILE), F32),
            pltpu.VMEM((tiles, TILE), F32),
            pltpu.VMEM((TILE, TILE), F32),
            pltpu.VMEM((3,) + OWN + (TILE,), F32),
            pltpu.VMEM(OWN + (TILE,), jnp.int32),
            pltpu.SMEM(OWN, jnp.int32),
            pltpu.SemaphoreType.DMA((3,)),
            pltpu.SemaphoreType.DMA((2, len(OFFSETS))),
            pltpu.SemaphoreType.DMA((2, len(OFFSETS))),
        ],
        compiler_params=pltpu.CompilerParams(collective_id=0, has_side_effects=True, vmem_limit_bytes=24 << 20),
    )(*(pltpu.with_memory_space_constraint(a, pltpu.HBM) for a in (positions, species, counts)))
    return pl.pallas_call(
        force_kernel,
        name="forces",
        out_shape=(
            jax.ShapeDtypeStruct((3,) + OWN + (TILE,), F32),
            jax.ShapeDtypeStruct(OWN + (TILE,), F32),
        ),
        in_specs=[vmem, vmem, vmem, smem, smem],
        out_specs=(vmem, vmem),
        scratch_shapes=[
            pltpu.VMEM((tiles, 32 + GROUP, 8, TILE), F32),
            pltpu.VMEM((UNROLL, TILE, TILE), F32),
            pltpu.VMEM((tiles, 8, TILE), F32),
        ],
        compiler_params=pltpu.CompilerParams(vmem_limit_bytes=24 << 20),
    )(full, embed, near, begin, used)


def solution(mesh):
    placed = (P(None, "gx", "gy", "gz", None), P("gx", "gy", "gz", None), P("gx", "gy", "gz"))
    sizes = tuple(mesh.shape[name] for name in ("gx", "gy", "gz"))
    return jax.shard_map(
        lambda *args: shards(sizes, *args),
        mesh=mesh,
        in_specs=placed,
        out_specs=(P(None, "gx", "gy", "gz", None), P("gx", "gy", "gz", None)),
        check_vma=False,
    )
```

```python
import math

import jax
import jax.numpy as jnp
from jax import lax
from jax.experimental import pallas as pl
from jax.experimental.pallas import tpu as pltpu
from jax.sharding import PartitionSpec as P

F32 = jnp.float32
BF16 = jnp.bfloat16
MESH = pl.DeviceIdType.MESH
CUTOFF_SQUARED = 0.2025
SCALE = math.sqrt(2.0 / CUTOFF_SQUARED)
TILE = 128
OWN = (2, 2, 4)
EXT = (4, 4, 6)
OFFSETS = sorted(
    [(a, b, c) for a in (-1, 0, 1) for b in (-1, 0, 1) for c in (-1, 0, 1) if a or b or c],
    key=lambda offset: -sum(map(abs, offset)),
)
ALPHA = -3.0 / CUTOFF_SQUARED
BETA = -4.0 / CUTOFF_SQUARED * 0.09
SLOPE = ALPHA / (5.0 * BETA)
PART = 128
TILES = OWN[0] * OWN[1] * OWN[2]
UNROLL = 4
FORCE_PART = 64
GROUP = 6
HIGHEST = lax.Precision.HIGHEST
NT = (((1,), (1,)), ((), ()))


def pieces(v):
    first = v.astype(BF16).astype(F32)
    rest = v - first
    second = rest.astype(BF16).astype(F32)
    return first, second, rest - second


def beside_features(v):
    a, b, c = pieces(v)
    return jnp.concatenate([a, b, a, b, c, a], axis=0).astype(BF16)


def own_features(v):
    a, b, c = pieces(v)
    return jnp.concatenate([a, a, b, b, a, c], axis=0).T.astype(BF16)


def rows_of(*rows):
    row = lax.broadcasted_iota(jnp.int32, (8, TILE), 0)
    out = jnp.zeros((8, TILE), F32)
    for index, value in enumerate(rows):
        if value is not None:
            out = jnp.where(row == index, value, out)
    return out


def tile_of(index, extent):
    plane = extent[1] * extent[2]
    return index // plane, (index // extent[2]) % extent[1], index % extent[2]


def span(offset, own, sending):
    if offset == 0:
        return pl.ds(1, own)
    if sending:
        return pl.ds(own if offset > 0 else 1, 1)
    return pl.ds(0 if offset > 0 else own + 1, 1)


def region(offset, sending):
    return tuple(span(o, n, sending) for o, n in zip(offset, OWN))


def exchange_kernel(
    sizes,
    pos_hbm,
    spec_hbm,
    count_hbm,
    full_ref,
    embed_ref,
    near_ref,
    begin_ref,
    used_ref,
    wire,
    slope,
    beside,
    own,
    totals,
    reach_rows,
    weights,
    columns_ref,
    pos_ref,
    spec_ref,
    count_ref,
    loads,
    sends,
    recvs,
):
    arrivals = [
        pltpu.make_async_copy(source, target, loads.at[k])
        for k, (source, target) in enumerate(
            ((count_hbm, count_ref), (pos_hbm, pos_ref), (spec_hbm, spec_ref))
        )
    ]
    for copy in arrivals:
        copy.start()
    me = [lax.axis_index(name) for name in ("gx", "gy", "gz")]

    def peer(offset):
        return tuple(lax.rem(m + o + n, n) for m, o, n in zip(me, offset, sizes))

    barrier = pltpu.get_barrier_semaphore()
    for offset in OFFSETS:
        pl.semaphore_signal(barrier, inc=1, device_id=peer(offset), device_id_type=MESH)

    for copy in arrivals:
        copy.wait()
    lane = lax.broadcasted_iota(jnp.int32, (1, TILE), 1)
    row4 = lax.broadcasted_iota(jnp.int32, (4, TILE), 0)
    for x in range(OWN[0]):
        for y in range(OWN[1]):
            for z in range(OWN[2]):
                kind = spec_ref[x, y, z : z + 1, :]
                weight = jnp.where(
                    lane < count_ref[x, y, z], jnp.where(kind == 1, 7.0, 5.0), 0.0
                )
                value = jnp.broadcast_to(weight, (4, TILE))
                for comp in range(3):
                    value = jnp.where(row4 == comp, pos_ref[comp, x, y, z : z + 1, :], value)
                wire[x + 1, y + 1, z + 1] = value
                index = (x * OWN[1] + y) * OWN[2] + z
                weights[index : index + 1, :] = weight
    pl.semaphore_wait(barrier, len(OFFSETS))

    def copies(ref, which):
        return [
            pltpu.make_async_remote_copy(
                src_ref=ref.at[region(offset, True)],
                dst_ref=ref.at[region(offset, False)],
                send_sem=sends.at[which],
                recv_sem=recvs.at[which],
                device_id=peer(offset),
                device_id_type=MESH,
            )
            for offset in OFFSETS
        ]

    def settle(ref, sems, which):
        whole = ref.at[:, :, 0 : EXT[2] - 1]
        pltpu.make_async_copy(whole, whole, sems.at[which]).wait()

    state_copies = copies(wire, 0)
    for copy in state_copies:
        copy.start()

    low = (me[2] > 0).astype(F32)
    high = (me[2] < sizes[2] - 1).astype(F32)

    def prepare(x, y, z):
        value = wire[x, y, z]
        weight = value[3:4] * (low if z == 0 else high if z == EXT[2] - 1 else 1.0)
        cx = (value[0:1] + (x - 2).astype(F32)) * SCALE
        cy = (value[1:2] + (y - 2).astype(F32)) * SCALE
        cz = (value[2:3] + float(z - 3)) * SCALE
        norm = 0.5 * (cx * cx + cy * cy + cz * cz)
        root = jnp.where(weight > 6.0, 1.4 ** (1.0 / 3.0), jnp.where(weight > 0.0, 1.0, 0.0))
        pair = jnp.where(weight > 0.0, 0.5 * weight - 0.5, 0.0)
        full = rows_of(cx, cy, cz, weight, 1.0, -norm, None, pair)
        full_ref[x, y, z] = full
        row = lax.broadcasted_iota(jnp.int32, (8, TILE), 0)
        part = root * jnp.where(row == 3, 1.0, jnp.where(row == 4, -norm, full))
        beside[x * EXT[1] + y, :, z * TILE : (z + 1) * TILE] = beside_features(
            jnp.where(row < 5, part, 0.0)
        )
        return full

    def prepare_own(index, _):
        x, y = 1 + index // OWN[1], 1 + index % OWN[1]
        for z in (0, EXT[2] - 1):
            beside[x * EXT[1] + y, :, z * TILE : (z + 1) * TILE] = jnp.zeros((48, TILE), BF16)
        for z in range(OWN[2]):
            full = prepare(x, y, z + 1)
            row = lax.broadcasted_iota(jnp.int32, (8, TILE), 0)
            value = jnp.where(row == 3, 1.0 + full[5:6], jnp.where(row < 5, full, 0.0))
            own[index * OWN[2] + z] = own_features(value)
        return _

    lax.fori_loop(0, OWN[0] * OWN[1], prepare_own, 0)

    def cubes(rows, there):
        value = jnp.maximum(jnp.dot(rows, there, preferred_element_type=F32), 0.0)
        return value * value * value

    def blocks(value):
        return sum(
            value[:, k * TILE : (k + 1) * TILE] for k in range(1, value.shape[1] // TILE)
        ) + value[:, :TILE]

    def window(column, z, width=3):
        return beside[column, :, pl.ds(pl.multiple_of(z * TILE, TILE), width * TILE)]

    parts = TILE // PART

    def inner_tile(index):
        x, y, z = tile_of(index, OWN)
        for part in range(parts):
            cut = slice(part * PART, (part + 1) * PART)
            rows = own[index, cut]
            total = jnp.zeros((PART, TILE), F32)
            for dx in range(OWN[0]):
                for dy in range(OWN[1]):
                    there = lax.rem(x + dx, OWN[0]) + 1, lax.rem(y + dy, OWN[1]) + 1
                    cube = cubes(rows, window(there[0] * EXT[1] + there[1], z))
                    if (dx, dy) == (0, 0):
                        here = lax.broadcasted_iota(jnp.int32, (PART, TILE), 0) + part * PART
                        self_pair = here == lax.broadcasted_iota(jnp.int32, (PART, TILE), 1)
                        middle = jnp.where(self_pair, 0.0, cube[:, TILE : 2 * TILE])
                        total = total + cube[:, :TILE] + middle + cube[:, 2 * TILE :]
                    else:
                        total = total + blocks(cube)
            totals[index, cut] = total

    def inner(step, _):
        for k in range(UNROLL):
            inner_tile(step * UNROLL + k)
        return _

    lax.fori_loop(0, TILES // UNROLL, inner, 0)

    settle(wire, recvs, 0)

    def prepare_side(index, _):
        x = jnp.where(index < 4, 0, jnp.where(index < 8, EXT[0] - 1, 1 + (index - 8) // 2))
        y = jnp.where(index < 8, lax.rem(index, 4), (EXT[1] - 1) * lax.rem(index, 2))
        for z in range(EXT[2]):
            prepare(x, y, z)
        return _

    lax.fori_loop(0, EXT[0] * EXT[1] - OWN[0] * OWN[1], prepare_side, 0)

    def prepare_ends(index, _):
        for z in (0, EXT[2] - 1):
            prepare(1 + index // OWN[1], 1 + index % OWN[1], z)
        return _

    lax.fori_loop(0, OWN[0] * OWN[1], prepare_ends, 0)

    def ends_tile(index):
        column, upper = index // 2, lax.rem(index, 2)
        tile = column * OWN[2] + upper * (OWN[2] - 1)
        for part in range(parts):
            cut = slice(part * PART, (part + 1) * PART)
            rows = own[tile, cut]
            total = totals[tile, cut]
            for x in range(OWN[0]):
                for y in range(OWN[1]):
                    there = (x + 1) * EXT[1] + y + 1
                    total = total + cubes(rows, window(there, upper * (EXT[2] - 1), 1))
            totals[tile, cut] = total

    def ends(step, _):
        for k in range(UNROLL):
            ends_tile(step * UNROLL + k)
        return _

    lax.fori_loop(0, 2 * OWN[0] * OWN[1] // UNROLL, ends, 0)

    lanes = lax.broadcasted_iota(jnp.int32, (TILE, TILE), 1)

    def outer_tile(index):
        x, y, z = tile_of(index, OWN)
        side_x, side_y = x * (EXT[0] - 1), y * (EXT[1] - 1)
        columns = [side_x * EXT[1] + y + dy for dy in range(3)]
        columns += [(dx + 1) * EXT[1] + side_y for dx in range(OWN[0])]
        total = totals[index]
        for column in columns:
            total = total + blocks(cubes(own[index], window(column, z)))
        return jnp.sum(total, axis=1, keepdims=True)

    slope_copies = copies(slope, 1)
    plane = OWN[0] * OWN[1]

    def finish_density(first_z, stride_z):
        def outer(step, _):
            value = columns_ref[...]
            for k in range(plane):
                index = k * OWN[2] + first_z + stride_z * step
                value = jnp.where(lanes == index, outer_tile(index), value)
            columns_ref[...] = value
            return _

        lax.fori_loop(0, 2, outer, 0)
        root = jnp.sqrt(1.0 + columns_ref[...].T[:TILES])
        weight = weights[...]
        strength = jnp.where(weight > 6.0, 0.7, jnp.where(weight > 0.0, 1.0, 0.0))
        embed_ref[...] = -strength * root
        rows = -0.5 * SLOPE * strength / root
        for z in (first_z, first_z + stride_z):
            for k in range(plane):
                index = k * OWN[2] + z
                slope[k // OWN[1] + 1, k % OWN[1] + 1, z + 1] = rows[index : index + 1]

    columns_ref[...] = jnp.zeros((TILE, TILE), F32)
    finish_density(0, OWN[2] - 1)
    for copy, offset in zip(slope_copies, OFFSETS):
        if offset[2] != 0:
            copy.start()
    finish_density(1, 1)
    for copy, offset in zip(slope_copies, OFFSETS):
        if offset[2] == 0:
            copy.start()

    def distances_of(index):
        x, y, z = tile_of(index, OWN)
        for k, offset in enumerate(OFFSETS):
            at = tuple(a + 1 + o for a, o in zip((x, y, z), offset))
            there = wire[at]
            far = None
            for comp, o in enumerate(offset):
                if o:
                    gap = there[comp : comp + 1] if o > 0 else 1.0 - there[comp : comp + 1]
                    far = gap * gap if far is None else far + gap * gap
            weight = full_ref[at + (slice(3, 4),)]
            reach_rows[index, k : k + 1, :] = jnp.where(weight > 0.0, far, 9.0)
        for k in range(len(OFFSETS), 32):
            reach_rows[index, k : k + 1, :] = jnp.full((1, TILE), 9.0, F32)

    def distances(step, _):
        for k in range(2):
            distances_of(step * 2 + k)
        return _

    lax.fori_loop(0, TILES // 2, distances, 0)

    first = lax.broadcasted_iota(jnp.int32, (TILE, TILE), 0)
    second = lax.broadcasted_iota(jnp.int32, (TILE, TILE), 1)
    earlier = (first < second).astype(F32).astype(BF16)
    ones = jnp.ones((TILE, TILE), BF16)
    above_rows = ((second < first) & (second // 32 == first // 32)).astype(F32).astype(BF16)
    first_lane = (lax.broadcasted_iota(jnp.int32, (8, TILE), 1) == 0).astype(F32).astype(BF16)

    def compress_rows(group):
        rows = reach_rows[pl.ds(group * 4, 4)].reshape(TILE, TILE)
        near = rows < CUTOFF_SQUARED * 1.00002
        flags = near.astype(F32).astype(BF16)
        before = jnp.dot(flags, earlier, preferred_element_type=F32).astype(jnp.int32)
        held = jnp.dot(flags, ones, preferred_element_type=F32).astype(BF16)
        filled = jnp.dot(above_rows, held, preferred_element_type=F32).astype(jnp.int32)
        word = jnp.where(near, 16384 + second * 128 + (second - before), 0)
        for bit in range(7):
            moved = pltpu.roll(word, TILE - (1 << bit), 1)
            stay = jnp.where((word & (1 << bit)) != 0, 0, word)
            word = jnp.where((moved & (1 << bit)) != 0, moved, stay)
        for bit in range(7):
            word = jnp.where((filled & (1 << bit)) != 0, pltpu.roll(word, 1 << bit, 1), word)
        start = filled & (TILE - 1)
        code = ((word >> 7) & 127) + jnp.where(second < start, TILE, 0)
        near_ref[pl.ds(group * 4, 4)] = jnp.where(word >= 16384, code, 512).reshape(4, 32, TILE)
        cut = pl.ds(pl.multiple_of(group * TILE, TILE), TILE)
        for ref, value in (
            (begin_ref, 1 + (filled >> 7)),
            (used_ref, 1 + ((filled + TILE - 1) >> 7)),
        ):
            value = value.astype(F32).astype(BF16)
            value = lax.dot_general(first_lane, value, NT, preferred_element_type=F32)
            ref[:, cut] = value[0:1].astype(jnp.int32)

    def compress(step, _):
        for k in range(2):
            compress_rows(step * 2 + k)
        return _

    lax.fori_loop(0, 2, compress, 0)

    settle(wire, sends, 0)
    settle(slope, recvs, 1)

    def finish(index, _):
        for z in range(EXT[2]):
            at = (index // EXT[1], lax.rem(index, EXT[1]), z)
            value = slope[at]
            if z in (0, EXT[2] - 1):
                value = value * (high if z else low)
            full_ref[at + (slice(6, 7),)] = value
        return _

    lax.fori_loop(0, EXT[0] * EXT[1], finish, 0)
    settle(slope, sends, 1)


def force_kernel(
    full_ref, embed_ref, near_ref, begin_ref, used_ref, forces_ref, energy_ref, packed, sums, results
):
    row = lax.broadcasted_iota(jnp.int32, (8, TILE), 0)

    def pack_tile(index):
        x, y, z = tile_of(index, OWN)
        packed[index, 0] = full_ref[x + 1, y + 1, z + 1]
        current = jnp.zeros((8, TILE), F32)
        chunk = begin_ref[0, index * 32]
        for k, offset in enumerate(OFFSETS):
            there = full_ref[tuple(a + 1 + o for a, o in zip((x, y, z), offset))]
            code = jnp.broadcast_to(near_ref[index, k : k + 1, :], (8, TILE))
            places = code & (TILE - 1)
            value = jnp.take_along_axis(there, places, axis=1, mode="promise_in_bounds")
            merged = jnp.where(code < TILE, value, current)
            beyond = jnp.where((code & TILE) != 0, value, 0.0)
            packed[index, chunk] = merged
            packed[index, chunk + 1] = beyond
            later = begin_ref[0, index * 32 + k + 1]
            current = jnp.where(later > chunk, beyond, merged)
            chunk = later
        for k in range(1, GROUP + 1):
            packed[index, chunk + k] = jnp.zeros((8, TILE), F32)

    def pack(step, _):
        for k in range(UNROLL):
            pack_tile(step * UNROLL + k)
        return _

    lax.fori_loop(0, TILES // UNROLL, pack, 0)

    def group(index, own, start, count, with_self, room):
        shape = (FORCE_PART, TILE)
        lanes = lax.broadcasted_iota(jnp.int32, shape, 1)
        values = [packed[index, start + k] for k in range(count)]
        features = [
            jnp.concatenate([beside_features(value) for value in values[k : k + 2]], axis=1)
            for k in range(0, count, 2)
        ]
        for part in range(TILE // FORCE_PART):
            cut = slice(part * FORCE_PART, (part + 1) * FORCE_PART)
            total = [jnp.zeros(shape, F32) for _ in range(5)]
            for pair_index, feature in enumerate(features):
                products = [
                    jnp.dot(rows[cut], feature, preferred_element_type=F32) for rows in own
                ]
                for side in range(2):
                    k = 2 * pair_index + side
                    value = values[k]
                    reach, both, pair = (
                        product[:, side * TILE : (side + 1) * TILE] for product in products
                    )
                    q = jnp.maximum(reach, 0.0)
                    if with_self and k == 0:
                        here = lax.broadcasted_iota(jnp.int32, shape, 0) + part * FORCE_PART
                        q = jnp.where(here == lanes, 0.0, q)
                    square = q * q
                    pull = square * (q * pair)
                    coef = pull + square * both
                    for comp in range(3):
                        total[comp] = total[comp] + coef * value[comp : comp + 1]
                    total[3] = total[3] + coef
                    total[4] = total[4] + pull * q
            column = jnp.zeros(shape, F32)
            for k in range(5):
                column = jnp.where(lanes == k, jnp.sum(total[k], axis=1, keepdims=True), column)
            sums[room, cut, :] = column
        return sums[room].T[:8]

    def own_rows(value):
        out = jnp.where(row == 3, value[6:7], value)
        out = jnp.where(row == 4, 1.0 + value[5:6], out)
        out = jnp.where(row == 5, 1.0, out)
        a, b, c = pieces(jnp.where(row == 6, value[3:4], out))
        columns = jnp.concatenate([a, a, b, b, a, c], axis=0).T
        place = lax.broadcasted_iota(jnp.int32, columns.shape, 1) % 8
        masks = ((place < 3) | (place == 4) | (place == 5), (place == 3) | (place == 6), place == 7)
        return [jnp.where(mask, columns, 0.0).astype(BF16) for mask in masks]

    def forces(step, _):
        done = []
        for k in range(UNROLL):
            index = step * UNROLL + k
            own = own_rows(packed[index, 0])
            done.append((index, own, group(index, own, 0, GROUP, True, k)))
        for k, (index, own, result) in enumerate(done):
            results[index] = result
            more = (used_ref[0, index * 32 + 31] - GROUP + 1) // 2

            def further(extra, _, index=index, own=own, k=k):
                results[index] += group(index, own, GROUP + 2 * extra, 2, False, k)
                return _

            lax.fori_loop(0, jnp.maximum(more, 0), further, 0)
        return _

    lax.fori_loop(0, TILES // UNROLL, forces, 0)
    for index in range(TILES):
        x, y, z = tile_of(index, OWN)
        result = results[index]
        moved = (2.0 * BETA / SCALE) * (result - packed[index, 0] * result[3:4])
        for comp in range(3):
            forces_ref[comp, x, y, z : z + 1, :] = moved[comp : comp + 1]
        energy_ref[x, y, z : z + 1, :] = embed_ref[index : index + 1] + 0.045 * result[4:5]


def shards(sizes, positions, species, counts):
    vmem = pl.BlockSpec(memory_space=pltpu.VMEM)
    smem = pl.BlockSpec(memory_space=pltpu.SMEM)
    tiles = OWN[0] * OWN[1] * OWN[2]
    full, embed, near, begin, used = pl.pallas_call(
        lambda *refs: exchange_kernel(sizes, *refs),
        name="exchange",
        out_shape=(
            jax.ShapeDtypeStruct(EXT + (8, TILE), F32),
            jax.ShapeDtypeStruct((tiles, TILE), F32),
            jax.ShapeDtypeStruct((tiles, 32, TILE), jnp.int32),
            jax.ShapeDtypeStruct((1, tiles * 32), jnp.int32),
            jax.ShapeDtypeStruct((1, tiles * 32), jnp.int32),
        ),
        in_specs=[pl.BlockSpec(memory_space=pltpu.HBM)] * 3,
        out_specs=(vmem,) * 5,
        scratch_shapes=[
            pltpu.VMEM(EXT + (4, TILE), F32),
            pltpu.VMEM(EXT + (1, TILE), F32),
            pltpu.VMEM((EXT[0] * EXT[1], 48, EXT[2] * TILE), BF16),
            pltpu.VMEM((tiles, TILE, 48), BF16),
            pltpu.VMEM((tiles, TILE, TILE), F32),
            pltpu.VMEM((tiles, 32, TILE), F32),
            pltpu.VMEM((tiles, TILE), F32),
            pltpu.VMEM((TILE, TILE), F32),
            pltpu.VMEM((3,) + OWN + (TILE,), F32),
            pltpu.VMEM(OWN + (TILE,), jnp.int32),
            pltpu.SMEM(OWN, jnp.int32),
            pltpu.SemaphoreType.DMA((3,)),
            pltpu.SemaphoreType.DMA((2,)),
            pltpu.SemaphoreType.DMA((2,)),
        ],
        compiler_params=pltpu.CompilerParams(collective_id=0, has_side_effects=True, vmem_limit_bytes=24 << 20),
    )(*(pltpu.with_memory_space_constraint(a, pltpu.HBM) for a in (positions, species, counts)))
    return pl.pallas_call(
        force_kernel,
        name="forces",
        out_shape=(
            jax.ShapeDtypeStruct((3,) + OWN + (TILE,), F32),
            jax.ShapeDtypeStruct(OWN + (TILE,), F32),
        ),
        in_specs=[vmem, vmem, vmem, smem, smem],
        out_specs=(vmem, vmem),
        scratch_shapes=[
            pltpu.VMEM((tiles, 32 + GROUP, 8, TILE), F32),
            pltpu.VMEM((UNROLL, TILE, TILE), F32),
            pltpu.VMEM((tiles, 8, TILE), F32),
        ],
        compiler_params=pltpu.CompilerParams(vmem_limit_bytes=24 << 20),
    )(full, embed, near, begin, used)


def solution(mesh):
    placed = (P(None, "gx", "gy", "gz", None), P("gx", "gy", "gz", None), P("gx", "gy", "gz"))
    sizes = tuple(mesh.shape[name] for name in ("gx", "gy", "gz"))
    return jax.shard_map(
        lambda *args: shards(sizes, *args),
        mesh=mesh,
        in_specs=placed,
        out_specs=(P(None, "gx", "gy", "gz", None), P("gx", "gy", "gz", None)),
        check_vma=False,
    )
```

```python
import math

import jax
import jax.numpy as jnp
from jax import lax
from jax.experimental import pallas as pl
from jax.experimental.pallas import tpu as pltpu
from jax.sharding import PartitionSpec as P

F32 = jnp.float32
BF16 = jnp.bfloat16
MESH = pl.DeviceIdType.MESH
CUTOFF_SQUARED = 0.2025
SCALE = math.sqrt(2.0 / CUTOFF_SQUARED)
TILE = 128
OWN = (2, 2, 4)
EXT = (4, 4, 6)
OFFSETS = sorted(
    [(a, b, c) for a in (-1, 0, 1) for b in (-1, 0, 1) for c in (-1, 0, 1) if a or b or c],
    key=lambda offset: -sum(map(abs, offset)),
)
ALPHA = -3.0 / CUTOFF_SQUARED
BETA = -4.0 / CUTOFF_SQUARED * 0.09
SLOPE = ALPHA / (5.0 * BETA)
PART = 128
TILES = OWN[0] * OWN[1] * OWN[2]
UNROLL = OWN[2]
FORCE_PART = 64
GROUP = 6
HIGHEST = lax.Precision.HIGHEST
NT = (((1,), (1,)), ((), ()))


def pieces(v):
    first = v.astype(BF16).astype(F32)
    rest = v - first
    second = rest.astype(BF16).astype(F32)
    return first, second, rest - second


def beside_features(v):
    a, b, c = pieces(v)
    return jnp.concatenate([a, b, a, b, c, a], axis=0).astype(BF16)


def own_features(v):
    a, b, c = pieces(v)
    return jnp.concatenate([a, a, b, b, a, c], axis=0).T.astype(BF16)


def rows_of(*rows):
    row = lax.broadcasted_iota(jnp.int32, (8, TILE), 0)
    out = jnp.zeros((8, TILE), F32)
    for index, value in enumerate(rows):
        if value is not None:
            out = jnp.where(row == index, value, out)
    return out


def tile_of(index, extent):
    plane = extent[1] * extent[2]
    return index // plane, (index // extent[2]) % extent[1], index % extent[2]


def span(offset, own, sending):
    if offset == 0:
        return pl.ds(1, own)
    if sending:
        return pl.ds(own if offset > 0 else 1, 1)
    return pl.ds(0 if offset > 0 else own + 1, 1)


def region(offset, sending):
    return tuple(span(o, n, sending) for o, n in zip(offset, OWN))


def exchange_kernel(
    sizes,
    pos_hbm,
    spec_hbm,
    count_hbm,
    full_ref,
    embed_ref,
    near_ref,
    begin_ref,
    used_ref,
    wire,
    slope,
    beside,
    own,
    totals,
    reach_rows,
    weights,
    columns_ref,
    pos_ref,
    spec_ref,
    count_ref,
    loads,
    sends,
    recvs,
):
    arrivals = [
        pltpu.make_async_copy(source, target, loads.at[k])
        for k, (source, target) in enumerate(
            ((count_hbm, count_ref), (pos_hbm, pos_ref), (spec_hbm, spec_ref))
        )
    ]
    for copy in arrivals:
        copy.start()
    me = [lax.axis_index(name) for name in ("gx", "gy", "gz")]

    def peer(offset):
        return tuple(lax.rem(m + o + n, n) for m, o, n in zip(me, offset, sizes))

    barrier = pltpu.get_barrier_semaphore()
    for offset in OFFSETS:
        pl.semaphore_signal(barrier, inc=1, device_id=peer(offset), device_id_type=MESH)

    for copy in arrivals:
        copy.wait()
    lane = lax.broadcasted_iota(jnp.int32, (1, TILE), 1)
    row4 = lax.broadcasted_iota(jnp.int32, (4, TILE), 0)
    for x in range(OWN[0]):
        for y in range(OWN[1]):
            for z in range(OWN[2]):
                kind = spec_ref[x, y, z : z + 1, :]
                weight = jnp.where(
                    lane < count_ref[x, y, z], jnp.where(kind == 1, 7.0, 5.0), 0.0
                )
                value = jnp.broadcast_to(weight, (4, TILE))
                for comp in range(3):
                    value = jnp.where(row4 == comp, pos_ref[comp, x, y, z : z + 1, :], value)
                wire[x + 1, y + 1, z + 1] = value
                index = (x * OWN[1] + y) * OWN[2] + z
                weights[index : index + 1, :] = weight
    pl.semaphore_wait(barrier, len(OFFSETS))

    def copies(ref, which):
        return [
            pltpu.make_async_remote_copy(
                src_ref=ref.at[region(offset, True)],
                dst_ref=ref.at[region(offset, False)],
                send_sem=sends.at[which],
                recv_sem=recvs.at[which],
                device_id=peer(offset),
                device_id_type=MESH,
            )
            for offset in OFFSETS
        ]

    def settle(ref, sems, which):
        whole = ref.at[:, :, 0 : EXT[2] - 1]
        pltpu.make_async_copy(whole, whole, sems.at[which]).wait()

    state_copies = copies(wire, 0)
    for copy in state_copies:
        copy.start()

    low = (me[2] > 0).astype(F32)
    high = (me[2] < sizes[2] - 1).astype(F32)

    def prepare(x, y, z):
        value = wire[x, y, z]
        weight = value[3:4] * (low if z == 0 else high if z == EXT[2] - 1 else 1.0)
        cx = (value[0:1] + (x - 2).astype(F32)) * SCALE
        cy = (value[1:2] + (y - 2).astype(F32)) * SCALE
        cz = (value[2:3] + float(z - 3)) * SCALE
        norm = 0.5 * (cx * cx + cy * cy + cz * cz)
        root = jnp.where(weight > 6.0, 1.4 ** (1.0 / 3.0), jnp.where(weight > 0.0, 1.0, 0.0))
        pair = jnp.where(weight > 0.0, 0.5 * weight - 0.5, 0.0)
        full = rows_of(cx, cy, cz, weight, 1.0, -norm, None, pair)
        full_ref[x, y, z] = full
        row = lax.broadcasted_iota(jnp.int32, (8, TILE), 0)
        part = root * jnp.where(row == 3, 1.0, jnp.where(row == 4, -norm, full))
        beside[x * EXT[1] + y, :, z * TILE : (z + 1) * TILE] = beside_features(
            jnp.where(row < 5, part, 0.0)
        )
        return full

    def prepare_own(index, _):
        x, y = 1 + index // OWN[1], 1 + index % OWN[1]
        for z in (0, EXT[2] - 1):
            beside[x * EXT[1] + y, :, z * TILE : (z + 1) * TILE] = jnp.zeros((48, TILE), BF16)
        for z in range(OWN[2]):
            full = prepare(x, y, z + 1)
            row = lax.broadcasted_iota(jnp.int32, (8, TILE), 0)
            value = jnp.where(row == 3, 1.0 + full[5:6], jnp.where(row < 5, full, 0.0))
            own[index * OWN[2] + z] = own_features(value)
        return _

    lax.fori_loop(0, OWN[0] * OWN[1], prepare_own, 0)

    def cubes(rows, there):
        value = jnp.maximum(jnp.dot(rows, there, preferred_element_type=F32), 0.0)
        return value * value * value

    def blocks(value):
        return sum(
            value[:, k * TILE : (k + 1) * TILE] for k in range(1, value.shape[1] // TILE)
        ) + value[:, :TILE]

    def window(column, z, width=3):
        if isinstance(z, int):
            return beside[column, :, z * TILE : (z + width) * TILE]
        return beside[column, :, pl.ds(pl.multiple_of(z * TILE, TILE), width * TILE)]

    parts = TILE // PART

    def inner_tile(step, z):
        x, y, index = step // OWN[1], lax.rem(step, OWN[1]), step * OWN[2] + z
        for part in range(parts):
            cut = slice(part * PART, (part + 1) * PART)
            rows = own[index, cut]
            total = jnp.zeros((PART, TILE), F32)
            for dx in range(OWN[0]):
                for dy in range(OWN[1]):
                    there = lax.rem(x + dx, OWN[0]) + 1, lax.rem(y + dy, OWN[1]) + 1
                    cube = cubes(rows, window(there[0] * EXT[1] + there[1], z))
                    if (dx, dy) == (0, 0):
                        here = lax.broadcasted_iota(jnp.int32, (PART, TILE), 0) + part * PART
                        self_pair = here == lax.broadcasted_iota(jnp.int32, (PART, TILE), 1)
                        middle = jnp.where(self_pair, 0.0, cube[:, TILE : 2 * TILE])
                        total = total + cube[:, :TILE] + middle + cube[:, 2 * TILE :]
                    else:
                        total = total + blocks(cube)
            totals[index, cut] = total

    def inner(step, _):
        for k in range(UNROLL):
            inner_tile(step, k)
        return _

    lax.fori_loop(0, TILES // UNROLL, inner, 0)

    settle(wire, recvs, 0)

    def prepare_side(index, _):
        x = jnp.where(index < 4, 0, jnp.where(index < 8, EXT[0] - 1, 1 + (index - 8) // 2))
        y = jnp.where(index < 8, lax.rem(index, 4), (EXT[1] - 1) * lax.rem(index, 2))
        for z in range(EXT[2]):
            prepare(x, y, z)
        return _

    lax.fori_loop(0, EXT[0] * EXT[1] - OWN[0] * OWN[1], prepare_side, 0)

    def prepare_ends(index, _):
        for z in (0, EXT[2] - 1):
            prepare(1 + index // OWN[1], 1 + index % OWN[1], z)
        return _

    lax.fori_loop(0, OWN[0] * OWN[1], prepare_ends, 0)

    def ends_tile(index):
        column, upper = index // 2, lax.rem(index, 2)
        tile = column * OWN[2] + upper * (OWN[2] - 1)
        for part in range(parts):
            cut = slice(part * PART, (part + 1) * PART)
            rows = own[tile, cut]
            total = totals[tile, cut]
            for x in range(OWN[0]):
                for y in range(OWN[1]):
                    there = (x + 1) * EXT[1] + y + 1
                    total = total + cubes(rows, window(there, upper * (EXT[2] - 1), 1))
            totals[tile, cut] = total

    def ends(step, _):
        for k in range(UNROLL):
            ends_tile(step * UNROLL + k)
        return _

    lax.fori_loop(0, 2 * OWN[0] * OWN[1] // UNROLL, ends, 0)

    lanes = lax.broadcasted_iota(jnp.int32, (TILE, TILE), 1)

    def outer_tile(index):
        x, y, z = tile_of(index, OWN)
        side_x, side_y = x * (EXT[0] - 1), y * (EXT[1] - 1)
        columns = [side_x * EXT[1] + y + dy for dy in range(3)]
        columns += [(dx + 1) * EXT[1] + side_y for dx in range(OWN[0])]
        total = totals[index]
        for column in columns:
            total = total + blocks(cubes(own[index], window(column, z)))
        return jnp.sum(total, axis=1, keepdims=True)

    slope_copies = copies(slope, 1)
    plane = OWN[0] * OWN[1]

    def finish_density(first_z, stride_z):
        def outer(step, _):
            value = columns_ref[...]
            for k in range(plane):
                index = k * OWN[2] + first_z + stride_z * step
                value = jnp.where(lanes == index, outer_tile(index), value)
            columns_ref[...] = value
            return _

        lax.fori_loop(0, 2, outer, 0)
        root = jnp.sqrt(1.0 + columns_ref[...].T[:TILES])
        weight = weights[...]
        strength = jnp.where(weight > 6.0, 0.7, jnp.where(weight > 0.0, 1.0, 0.0))
        embed_ref[...] = -strength * root
        rows = -0.5 * SLOPE * strength / root
        for z in (first_z, first_z + stride_z):
            for k in range(plane):
                index = k * OWN[2] + z
                slope[k // OWN[1] + 1, k % OWN[1] + 1, z + 1] = rows[index : index + 1]

    columns_ref[...] = jnp.zeros((TILE, TILE), F32)
    finish_density(0, OWN[2] - 1)
    for copy, offset in zip(slope_copies, OFFSETS):
        if offset[2] != 0:
            copy.start()
    finish_density(1, 1)
    for copy, offset in zip(slope_copies, OFFSETS):
        if offset[2] == 0:
            copy.start()

    def distances_of(step, z):
        x, y, index = step // OWN[1], lax.rem(step, OWN[1]), step * OWN[2] + z
        around, known = (ref.at[pl.ds(x, 3), pl.ds(y, 3)] for ref in (wire, full_ref))
        for k, offset in enumerate(OFFSETS):
            at = (offset[0] + 1, offset[1] + 1, z + 1 + offset[2])
            there = around[at]
            far = None
            for comp, o in enumerate(offset):
                if o:
                    gap = there[comp : comp + 1] if o > 0 else 1.0 - there[comp : comp + 1]
                    far = gap * gap if far is None else far + gap * gap
            weight = known[at + (slice(3, 4),)]
            reach_rows[index, k : k + 1, :] = jnp.where(weight > 0.0, far, 9.0)
        for k in range(len(OFFSETS), 32):
            reach_rows[index, k : k + 1, :] = jnp.full((1, TILE), 9.0, F32)

    def distances(step, _):
        for k in range(UNROLL):
            distances_of(step, k)
        return _

    lax.fori_loop(0, TILES // UNROLL, distances, 0)

    first = lax.broadcasted_iota(jnp.int32, (TILE, TILE), 0)
    second = lax.broadcasted_iota(jnp.int32, (TILE, TILE), 1)
    earlier = (first < second).astype(F32).astype(BF16)
    ones = jnp.ones((TILE, TILE), BF16)
    above_rows = ((second < first) & (second // 32 == first // 32)).astype(F32).astype(BF16)
    first_lane = (lax.broadcasted_iota(jnp.int32, (8, TILE), 1) == 0).astype(F32).astype(BF16)

    def compress_rows(group):
        rows = reach_rows[pl.ds(group * 4, 4)].reshape(TILE, TILE)
        near = rows < CUTOFF_SQUARED * 1.00002
        flags = near.astype(F32).astype(BF16)
        before = jnp.dot(flags, earlier, preferred_element_type=F32).astype(jnp.int32)
        held = jnp.dot(flags, ones, preferred_element_type=F32).astype(BF16)
        filled = jnp.dot(above_rows, held, preferred_element_type=F32).astype(jnp.int32)
        word = jnp.where(near, 16384 + second * 128 + (second - before), 0)
        for bit in range(7):
            moved = pltpu.roll(word, TILE - (1 << bit), 1)
            stay = jnp.where((word & (1 << bit)) != 0, 0, word)
            word = jnp.where((moved & (1 << bit)) != 0, moved, stay)
        start = filled & (TILE - 1)
        turned = (second - start) & (TILE - 1)
        word = jnp.take_along_axis(word, turned, axis=1, mode="promise_in_bounds")
        code = ((word >> 7) & 127) + jnp.where(second < start, TILE, 0)
        near_ref[pl.ds(group * 4, 4)] = jnp.where(word >= 16384, code, 512).reshape(4, 32, TILE)
        cut = pl.ds(pl.multiple_of(group * TILE, TILE), TILE)
        for ref, value in (
            (begin_ref, 1 + (filled >> 7)),
            (used_ref, 1 + ((filled + TILE - 1) >> 7)),
        ):
            value = value.astype(F32).astype(BF16)
            value = lax.dot_general(first_lane, value, NT, preferred_element_type=F32)
            ref[:, cut] = value[0:1].astype(jnp.int32)

    def compress(step, _):
        for k in range(2):
            compress_rows(step * 2 + k)
        return _

    lax.fori_loop(0, 2, compress, 0)

    settle(wire, sends, 0)
    settle(slope, recvs, 1)

    def finish(index, _):
        for z in range(EXT[2]):
            at = (index // EXT[1], lax.rem(index, EXT[1]), z)
            value = slope[at]
            if z in (0, EXT[2] - 1):
                value = value * (high if z else low)
            full_ref[at + (slice(6, 7),)] = value
        return _

    lax.fori_loop(0, EXT[0] * EXT[1], finish, 0)
    settle(slope, sends, 1)


def force_kernel(
    full_ref, embed_ref, near_ref, begin_ref, used_ref, forces_ref, energy_ref, packed, sums, results
):
    row = lax.broadcasted_iota(jnp.int32, (8, TILE), 0)

    def pack_tile(step, z):
        x, y, index = step // OWN[1], lax.rem(step, OWN[1]), step * OWN[2] + z
        around = full_ref.at[pl.ds(x, 3), pl.ds(y, 3)]
        chosen = packed.at[index]
        chosen[0] = around[1, 1, z + 1]
        current = jnp.zeros((8, TILE), F32)
        chunk = begin_ref[0, index * 32]
        for k, offset in enumerate(OFFSETS):
            there = around[offset[0] + 1, offset[1] + 1, z + 1 + offset[2]]
            code = jnp.broadcast_to(near_ref[index, k : k + 1, :], (8, TILE))
            places = code & (TILE - 1)
            value = jnp.take_along_axis(there, places, axis=1, mode="promise_in_bounds")
            merged = jnp.where(code < TILE, value, current)
            beyond = jnp.where((code & TILE) != 0, value, 0.0)
            chosen[chunk] = merged
            chosen[chunk + 1] = beyond
            later = begin_ref[0, index * 32 + k + 1]
            current = jnp.where(later > chunk, beyond, merged)
            chunk = later
        for k in range(1, GROUP + 1):
            chosen[chunk + k] = jnp.zeros((8, TILE), F32)

    def pack(step, _):
        for k in range(UNROLL):
            pack_tile(step, k)
        return _

    lax.fori_loop(0, TILES // UNROLL, pack, 0)

    def group(index, own, start, count, with_self, room):
        shape = (FORCE_PART, TILE)
        lanes = lax.broadcasted_iota(jnp.int32, shape, 1)
        values = [packed[index, start + k] for k in range(count)]
        features = [
            jnp.concatenate([beside_features(value) for value in values[k : k + 2]], axis=1)
            for k in range(0, count, 2)
        ]
        for part in range(TILE // FORCE_PART):
            cut = slice(part * FORCE_PART, (part + 1) * FORCE_PART)
            total = [jnp.zeros(shape, F32) for _ in range(5)]
            for pair_index, feature in enumerate(features):
                products = [
                    jnp.dot(rows[cut], feature, preferred_element_type=F32) for rows in own
                ]
                for side in range(2):
                    k = 2 * pair_index + side
                    value = values[k]
                    reach, both, pair = (
                        product[:, side * TILE : (side + 1) * TILE] for product in products
                    )
                    q = jnp.maximum(reach, 0.0)
                    if with_self and k == 0:
                        here = lax.broadcasted_iota(jnp.int32, shape, 0) + part * FORCE_PART
                        q = jnp.where(here == lanes, 0.0, q)
                    square = q * q
                    pull = square * (q * pair)
                    coef = pull + square * both
                    for comp in range(3):
                        total[comp] = total[comp] + coef * value[comp : comp + 1]
                    total[3] = total[3] + coef
                    total[4] = total[4] + pull * q
            column = jnp.zeros(shape, F32)
            for k in range(5):
                column = jnp.where(lanes == k, jnp.sum(total[k], axis=1, keepdims=True), column)
            sums[room, cut, :] = column
        return sums[room].T[:8]

    def own_rows(value):
        out = jnp.where(row == 3, value[6:7], value)
        out = jnp.where(row == 4, 1.0 + value[5:6], out)
        out = jnp.where(row == 5, 1.0, out)
        a, b, c = pieces(jnp.where(row == 6, value[3:4], out))
        columns = jnp.concatenate([a, a, b, b, a, c], axis=0).T
        place = lax.broadcasted_iota(jnp.int32, columns.shape, 1) % 8
        masks = ((place < 3) | (place == 4) | (place == 5), (place == 3) | (place == 6), place == 7)
        return [jnp.where(mask, columns, 0.0).astype(BF16) for mask in masks]

    def forces(step, _):
        done = []
        for k in range(UNROLL):
            index = step * UNROLL + k
            own = own_rows(packed[index, 0])
            done.append((index, own, group(index, own, 0, GROUP, True, k)))
        for k, (index, own, result) in enumerate(done):
            results[index] = result
            more = (used_ref[0, index * 32 + 31] - GROUP + 1) // 2

            def further(extra, _, index=index, own=own, k=k):
                results[index] += group(index, own, GROUP + 2 * extra, 2, False, k)
                return _

            lax.fori_loop(0, jnp.maximum(more, 0), further, 0)
        return _

    lax.fori_loop(0, TILES // UNROLL, forces, 0)
    for index in range(TILES):
        x, y, z = tile_of(index, OWN)
        result = results[index]
        moved = (2.0 * BETA / SCALE) * (result - packed[index, 0] * result[3:4])
        for comp in range(3):
            forces_ref[comp, x, y, z : z + 1, :] = moved[comp : comp + 1]
        energy_ref[x, y, z : z + 1, :] = embed_ref[index : index + 1] + 0.045 * result[4:5]


def shards(sizes, positions, species, counts):
    vmem = pl.BlockSpec(memory_space=pltpu.VMEM)
    smem = pl.BlockSpec(memory_space=pltpu.SMEM)
    tiles = OWN[0] * OWN[1] * OWN[2]
    full, embed, near, begin, used = pl.pallas_call(
        lambda *refs: exchange_kernel(sizes, *refs),
        name="exchange",
        out_shape=(
            jax.ShapeDtypeStruct(EXT + (8, TILE), F32),
            jax.ShapeDtypeStruct((tiles, TILE), F32),
            jax.ShapeDtypeStruct((tiles, 32, TILE), jnp.int32),
            jax.ShapeDtypeStruct((1, tiles * 32), jnp.int32),
            jax.ShapeDtypeStruct((1, tiles * 32), jnp.int32),
        ),
        in_specs=[pl.BlockSpec(memory_space=pltpu.HBM)] * 3,
        out_specs=(vmem,) * 5,
        scratch_shapes=[
            pltpu.VMEM(EXT + (4, TILE), F32),
            pltpu.VMEM(EXT + (1, TILE), F32),
            pltpu.VMEM((EXT[0] * EXT[1], 48, EXT[2] * TILE), BF16),
            pltpu.VMEM((tiles, TILE, 48), BF16),
            pltpu.VMEM((tiles, TILE, TILE), F32),
            pltpu.VMEM((tiles, 32, TILE), F32),
            pltpu.VMEM((tiles, TILE), F32),
            pltpu.VMEM((TILE, TILE), F32),
            pltpu.VMEM((3,) + OWN + (TILE,), F32),
            pltpu.VMEM(OWN + (TILE,), jnp.int32),
            pltpu.SMEM(OWN, jnp.int32),
            pltpu.SemaphoreType.DMA((3,)),
            pltpu.SemaphoreType.DMA((2,)),
            pltpu.SemaphoreType.DMA((2,)),
        ],
        compiler_params=pltpu.CompilerParams(collective_id=0, has_side_effects=True, vmem_limit_bytes=24 << 20),
    )(*(pltpu.with_memory_space_constraint(a, pltpu.HBM) for a in (positions, species, counts)))
    return pl.pallas_call(
        force_kernel,
        name="forces",
        out_shape=(
            jax.ShapeDtypeStruct((3,) + OWN + (TILE,), F32),
            jax.ShapeDtypeStruct(OWN + (TILE,), F32),
        ),
        in_specs=[vmem, vmem, vmem, smem, smem],
        out_specs=(vmem, vmem),
        scratch_shapes=[
            pltpu.VMEM((tiles, 32 + GROUP, 8, TILE), F32),
            pltpu.VMEM((UNROLL, TILE, TILE), F32),
            pltpu.VMEM((tiles, 8, TILE), F32),
        ],
        compiler_params=pltpu.CompilerParams(vmem_limit_bytes=24 << 20),
    )(full, embed, near, begin, used)


def solution(mesh):
    placed = (P(None, "gx", "gy", "gz", None), P("gx", "gy", "gz", None), P("gx", "gy", "gz"))
    sizes = tuple(mesh.shape[name] for name in ("gx", "gy", "gz"))
    return jax.shard_map(
        lambda *args: shards(sizes, *args),
        mesh=mesh,
        in_specs=placed,
        out_specs=(P(None, "gx", "gy", "gz", None), P("gx", "gy", "gz", None)),
        check_vma=False,
    )
```

```python
import math

import jax
import jax.numpy as jnp
from jax import lax
from jax.experimental import pallas as pl
from jax.experimental.pallas import tpu as pltpu
from jax.sharding import PartitionSpec as P

F32 = jnp.float32
BF16 = jnp.bfloat16
MESH = pl.DeviceIdType.MESH
CUTOFF_SQUARED = 0.2025
SCALE = math.sqrt(2.0 / CUTOFF_SQUARED)
TILE = 128
OWN = (2, 2, 4)
EXT = (4, 4, 6)
OFFSETS = sorted(
    [(a, b, c) for a in (-1, 0, 1) for b in (-1, 0, 1) for c in (-1, 0, 1) if a or b or c],
    key=lambda offset: -sum(map(abs, offset)),
)
ALPHA = -3.0 / CUTOFF_SQUARED
BETA = -4.0 / CUTOFF_SQUARED * 0.09
SLOPE = ALPHA / (5.0 * BETA)
PART = 128
TILES = OWN[0] * OWN[1] * OWN[2]
UNROLL = OWN[2]
FORCE_PART = 64
GROUP = 6
HIGHEST = lax.Precision.HIGHEST
NT = (((1,), (1,)), ((), ()))


def pieces(v):
    first = v.astype(BF16).astype(F32)
    rest = v - first
    second = rest.astype(BF16).astype(F32)
    return first, second, rest - second


def beside_features(v):
    a, b, c = pieces(v)
    return jnp.concatenate([a, b, a, b, c, a], axis=0).astype(BF16)


def own_features(v):
    a, b, c = pieces(v)
    return jnp.concatenate([a, a, b, b, a, c], axis=0).T.astype(BF16)


def rows_of(*rows):
    row = lax.broadcasted_iota(jnp.int32, (8, TILE), 0)
    out = jnp.zeros((8, TILE), F32)
    for index, value in enumerate(rows):
        if value is not None:
            out = jnp.where(row == index, value, out)
    return out


def tile_of(index, extent):
    plane = extent[1] * extent[2]
    return index // plane, (index // extent[2]) % extent[1], index % extent[2]


def span(offset, own, sending):
    if offset == 0:
        return pl.ds(1, own)
    if sending:
        return pl.ds(own if offset > 0 else 1, 1)
    return pl.ds(0 if offset > 0 else own + 1, 1)


def region(offset, sending):
    return tuple(span(o, n, sending) for o, n in zip(offset, OWN))


def exchange_kernel(
    sizes,
    pos_hbm,
    spec_hbm,
    count_hbm,
    full_ref,
    embed_ref,
    near_ref,
    begin_ref,
    used_ref,
    wire,
    slope,
    beside,
    own,
    totals,
    reach_rows,
    weights,
    columns_ref,
    pos_ref,
    spec_ref,
    count_ref,
    loads,
    sends,
    recvs,
):
    arrivals = [
        pltpu.make_async_copy(source, target, loads.at[k])
        for k, (source, target) in enumerate(
            ((count_hbm, count_ref), (pos_hbm, pos_ref), (spec_hbm, spec_ref))
        )
    ]
    for copy in arrivals:
        copy.start()
    me = [lax.axis_index(name) for name in ("gx", "gy", "gz")]

    def peer(offset):
        return tuple(lax.rem(m + o + n, n) for m, o, n in zip(me, offset, sizes))

    barrier = pltpu.get_barrier_semaphore()
    for offset in OFFSETS:
        pl.semaphore_signal(barrier, inc=1, device_id=peer(offset), device_id_type=MESH)

    for copy in arrivals:
        copy.wait()
    lane = lax.broadcasted_iota(jnp.int32, (1, TILE), 1)
    row4 = lax.broadcasted_iota(jnp.int32, (4, TILE), 0)
    for x in range(OWN[0]):
        for y in range(OWN[1]):
            for z in range(OWN[2]):
                kind = spec_ref[x, y, z : z + 1, :]
                weight = jnp.where(
                    lane < count_ref[x, y, z], jnp.where(kind == 1, 7.0, 5.0), 0.0
                )
                value = jnp.broadcast_to(weight, (4, TILE))
                for comp in range(3):
                    value = jnp.where(row4 == comp, pos_ref[comp, x, y, z : z + 1, :], value)
                wire[x + 1, y + 1, z + 1] = value
                index = (x * OWN[1] + y) * OWN[2] + z
                weights[index : index + 1, :] = weight
    pl.semaphore_wait(barrier, len(OFFSETS))

    def copies(ref, which, arrival):
        return [
            pltpu.make_async_remote_copy(
                src_ref=ref.at[region(offset, True)],
                dst_ref=ref.at[region(offset, False)],
                send_sem=sends.at[which],
                recv_sem=recvs.at[arrival(offset)],
                device_id=peer(offset),
                device_id_type=MESH,
            )
            for offset in OFFSETS
        ]

    def settle(part, sem):
        pltpu.make_async_copy(part, part, sem).wait()

    sides = wire.at[0:2, :, 0:4]
    others = wire.at[:, 0:3, 0:4]

    state_copies = copies(wire, 0, lambda o: 0 if o[2] == 0 and 0 in o[:2] else 1)
    for copy in state_copies:
        copy.start()

    low = (me[2] > 0).astype(F32)
    high = (me[2] < sizes[2] - 1).astype(F32)

    def prepare(x, y, z):
        value = wire[x, y, z]
        weight = value[3:4] * (low if z == 0 else high if z == EXT[2] - 1 else 1.0)
        cx = (value[0:1] + (x - 2).astype(F32)) * SCALE
        cy = (value[1:2] + (y - 2).astype(F32)) * SCALE
        cz = (value[2:3] + float(z - 3)) * SCALE
        norm = 0.5 * (cx * cx + cy * cy + cz * cz)
        root = jnp.where(weight > 6.0, 1.4 ** (1.0 / 3.0), jnp.where(weight > 0.0, 1.0, 0.0))
        pair = jnp.where(weight > 0.0, 0.5 * weight - 0.5, 0.0)
        full = rows_of(cx, cy, cz, weight, 1.0, -norm, None, pair)
        full_ref[x, y, z] = full
        row = lax.broadcasted_iota(jnp.int32, (8, TILE), 0)
        part = root * jnp.where(row == 3, 1.0, jnp.where(row == 4, -norm, full))
        beside[x * EXT[1] + y, :, z * TILE : (z + 1) * TILE] = beside_features(
            jnp.where(row < 5, part, 0.0)
        )
        return full

    def prepare_own(index, _):
        x, y = 1 + index // OWN[1], 1 + index % OWN[1]
        for z in (0, EXT[2] - 1):
            for column in range(4):
                beside[index * 4 + column, :, z * TILE : (z + 1) * TILE] = jnp.zeros((48, TILE), BF16)
        for z in range(OWN[2]):
            full = prepare(x, y, z + 1)
            row = lax.broadcasted_iota(jnp.int32, (8, TILE), 0)
            value = jnp.where(row == 3, 1.0 + full[5:6], jnp.where(row < 5, full, 0.0))
            own[index * OWN[2] + z] = own_features(value)
        return _

    lax.fori_loop(0, OWN[0] * OWN[1], prepare_own, 0)

    def cubes(rows, there):
        value = jnp.maximum(jnp.dot(rows, there, preferred_element_type=F32), 0.0)
        return value * value * value

    def blocks(value):
        return sum(
            value[:, k * TILE : (k + 1) * TILE] for k in range(1, value.shape[1] // TILE)
        ) + value[:, :TILE]

    def window(column, z, width=3):
        if isinstance(z, int):
            return beside[column, :, z * TILE : (z + width) * TILE]
        return beside[column, :, pl.ds(pl.multiple_of(z * TILE, TILE), width * TILE)]

    parts = TILE // PART

    def inner_tile(step, z):
        x, y, index = step // OWN[1], lax.rem(step, OWN[1]), step * OWN[2] + z
        for part in range(parts):
            cut = slice(part * PART, (part + 1) * PART)
            rows = own[index, cut]
            total = jnp.zeros((PART, TILE), F32)
            for dx in range(OWN[0]):
                for dy in range(OWN[1]):
                    there = lax.rem(x + dx, OWN[0]) + 1, lax.rem(y + dy, OWN[1]) + 1
                    cube = cubes(rows, window(there[0] * EXT[1] + there[1], z))
                    if (dx, dy) == (0, 0):
                        here = lax.broadcasted_iota(jnp.int32, (PART, TILE), 0) + part * PART
                        self_pair = here == lax.broadcasted_iota(jnp.int32, (PART, TILE), 1)
                        middle = jnp.where(self_pair, 0.0, cube[:, TILE : 2 * TILE])
                        total = total + cube[:, :TILE] + middle + cube[:, 2 * TILE :]
                    else:
                        total = total + blocks(cube)
            totals[index, cut] = total

    def inner(step, _):
        for k in range(UNROLL):
            inner_tile(step, k)
        return _

    lax.fori_loop(0, TILES // UNROLL, inner, 0)

    settle(sides, recvs.at[0])
    last_x, last_y = EXT[0] - 1, EXT[1] - 1

    def side_column(index):
        half, which = index % 4 // 2, index % 2
        x = jnp.where(index < 4, half * last_x, 1 + half)
        y = jnp.where(index < 4, 1 + which, which * last_y)
        return x, y

    def prepare_sides(index, _):
        x, y = side_column(index)
        for z in range(1, EXT[2] - 1):
            prepare(x, y, z)
        return _

    lax.fori_loop(0, 8, prepare_sides, 0)

    def columns_beside(x, y):
        side_x, side_y = x * last_x, y * last_y
        beside_x = [side_x * EXT[1] + 1 + dy for dy in range(OWN[1])]
        beside_y = [(1 + dx) * EXT[1] + side_y for dx in range(OWN[0])]
        return beside_x + beside_y, side_x * EXT[1] + side_y

    def middle(step, _):
        x, y = step // OWN[1], lax.rem(step, OWN[1])
        for z in range(OWN[2]):
            index = step * OWN[2] + z
            total = totals[index]
            for column in columns_beside(x, y)[0]:
                total = total + blocks(cubes(own[index], window(column, z)))
            totals[index] = total
        return _

    lax.fori_loop(0, OWN[0] * OWN[1], middle, 0)

    settle(others, recvs.at[1])

    def prepare_corners(index, _):
        for z in range(EXT[2]):
            prepare((index // 2) * last_x, lax.rem(index, 2) * last_y, z)
        return _

    lax.fori_loop(0, 4, prepare_corners, 0)

    def prepare_ends(index, _):
        side = side_column(jnp.maximum(index - 4, 0))
        x = jnp.where(index < 4, 1 + index // 2, side[0])
        y = jnp.where(index < 4, 1 + lax.rem(index, 2), side[1])
        for z in (0, EXT[2] - 1):
            prepare(x, y, z)
        return _

    lax.fori_loop(0, 12, prepare_ends, 0)
    lanes = lax.broadcasted_iota(jnp.int32, (TILE, TILE), 1)

    def outer_tile(step, z):
        x, y, index = step // OWN[1], lax.rem(step, OWN[1]), step * OWN[2] + z
        near, corner = columns_beside(x, y)
        total = totals[index] + blocks(cubes(own[index], window(corner, z)))
        if z in (0, OWN[2] - 1):
            near = near + [(1 + dx) * EXT[1] + 1 + dy for dx in range(2) for dy in range(2)]
            there = [window(column, 0 if z == 0 else EXT[2] - 1, 1) for column in near]
            for k in range(0, 8, 2):
                pair = jnp.concatenate(there[k : k + 2], axis=1)
                total = total + blocks(cubes(own[index], pair))
        return jnp.sum(total, axis=1, keepdims=True)

    slope_copies = copies(slope, 1, lambda o: 2)
    plane = OWN[0] * OWN[1]

    def finish_density(heights):
        def outer(step, _):
            value = columns_ref[...]
            for z in heights:
                value = jnp.where(lanes == step * OWN[2] + z, outer_tile(step, z), value)
            columns_ref[...] = value
            return _

        lax.fori_loop(0, plane, outer, 0)
        root = jnp.sqrt(1.0 + columns_ref[...].T[:TILES])
        weight = weights[...]
        strength = jnp.where(weight > 6.0, 0.7, jnp.where(weight > 0.0, 1.0, 0.0))
        embed_ref[...] = -strength * root
        rows = -0.5 * SLOPE * strength / root
        for z in heights:
            for k in range(plane):
                index = k * OWN[2] + z
                slope[k // OWN[1] + 1, k % OWN[1] + 1, z + 1] = rows[index : index + 1]

    columns_ref[...] = jnp.zeros((TILE, TILE), F32)
    finish_density((0, OWN[2] - 1))
    for copy, offset in zip(slope_copies, OFFSETS):
        if offset[2] != 0:
            copy.start()
    finish_density((1, 2))
    for copy, offset in zip(slope_copies, OFFSETS):
        if offset[2] == 0:
            copy.start()

    def distances_of(step, z):
        x, y, index = step // OWN[1], lax.rem(step, OWN[1]), step * OWN[2] + z
        around, known = (ref.at[pl.ds(x, 3), pl.ds(y, 3)] for ref in (wire, full_ref))
        for k, offset in enumerate(OFFSETS):
            at = (offset[0] + 1, offset[1] + 1, z + 1 + offset[2])
            there = around[at]
            far = None
            for comp, o in enumerate(offset):
                if o:
                    gap = there[comp : comp + 1] if o > 0 else 1.0 - there[comp : comp + 1]
                    far = gap * gap if far is None else far + gap * gap
            weight = known[at + (slice(3, 4),)]
            reach_rows[index, k : k + 1, :] = jnp.where(weight > 0.0, far, 9.0)
        for k in range(len(OFFSETS), 32):
            reach_rows[index, k : k + 1, :] = jnp.full((1, TILE), 9.0, F32)

    def distances(step, _):
        for k in range(UNROLL):
            distances_of(step, k)
        return _

    lax.fori_loop(0, TILES // UNROLL, distances, 0)

    first = lax.broadcasted_iota(jnp.int32, (TILE, TILE), 0)
    second = lax.broadcasted_iota(jnp.int32, (TILE, TILE), 1)
    earlier = (first < second).astype(F32).astype(BF16)
    ones = jnp.ones((TILE, TILE), BF16)
    above_rows = ((second < first) & (second // 32 == first // 32)).astype(F32).astype(BF16)
    first_lane = (lax.broadcasted_iota(jnp.int32, (8, TILE), 1) == 0).astype(F32).astype(BF16)

    def compress_rows(group):
        rows = reach_rows[pl.ds(group * 4, 4)].reshape(TILE, TILE)
        near = rows < CUTOFF_SQUARED * 1.00002
        flags = near.astype(F32).astype(BF16)
        before = jnp.dot(flags, earlier, preferred_element_type=F32).astype(jnp.int32)
        held = jnp.dot(flags, ones, preferred_element_type=F32).astype(BF16)
        filled = jnp.dot(above_rows, held, preferred_element_type=F32).astype(jnp.int32)
        word = jnp.where(near, 16384 + second * 128 + (second - before), 0)
        for bit in range(7):
            moved = pltpu.roll(word, TILE - (1 << bit), 1)
            stay = jnp.where((word & (1 << bit)) != 0, 0, word)
            word = jnp.where((moved & (1 << bit)) != 0, moved, stay)
        start = filled & (TILE - 1)
        turned = (second - start) & (TILE - 1)
        word = jnp.take_along_axis(word, turned, axis=1, mode="promise_in_bounds")
        code = ((word >> 7) & 127) + jnp.where(second < start, TILE, 0)
        near_ref[pl.ds(group * 4, 4)] = jnp.where(word >= 16384, code, 512).reshape(4, 32, TILE)
        cut = pl.ds(pl.multiple_of(group * TILE, TILE), TILE)
        for ref, value in (
            (begin_ref, 1 + (filled >> 7)),
            (used_ref, 1 + ((filled + TILE - 1) >> 7)),
        ):
            value = value.astype(F32).astype(BF16)
            value = lax.dot_general(first_lane, value, NT, preferred_element_type=F32)
            ref[:, cut] = value[0:1].astype(jnp.int32)

    def compress(step, _):
        for k in range(2):
            compress_rows(step * 2 + k)
        return _

    lax.fori_loop(0, 2, compress, 0)

    settle(wire.at[:, :, 0 : EXT[2] - 1], sends.at[0])
    settle(slope.at[:, :, 0 : EXT[2] - 1], recvs.at[2])

    def finish(index, _):
        for z in range(EXT[2]):
            at = (index // EXT[1], lax.rem(index, EXT[1]), z)
            value = slope[at]
            if z in (0, EXT[2] - 1):
                value = value * (high if z else low)
            full_ref[at + (slice(6, 7),)] = value
        return _

    lax.fori_loop(0, EXT[0] * EXT[1], finish, 0)
    settle(slope.at[:, :, 0 : EXT[2] - 1], sends.at[1])


def force_kernel(
    full_ref, embed_ref, near_ref, begin_ref, used_ref, forces_ref, energy_ref, packed, sums, results
):
    row = lax.broadcasted_iota(jnp.int32, (8, TILE), 0)

    def pack_tile(step, z):
        x, y, index = step // OWN[1], lax.rem(step, OWN[1]), step * OWN[2] + z
        around = full_ref.at[pl.ds(x, 3), pl.ds(y, 3)]
        chosen = packed.at[index]
        chosen[0] = around[1, 1, z + 1]
        current = jnp.zeros((8, TILE), F32)
        chunk = begin_ref[0, index * 32]
        for k, offset in enumerate(OFFSETS):
            there = around[offset[0] + 1, offset[1] + 1, z + 1 + offset[2]]
            code = jnp.broadcast_to(near_ref[index, k : k + 1, :], (8, TILE))
            places = code & (TILE - 1)
            value = jnp.take_along_axis(there, places, axis=1, mode="promise_in_bounds")
            merged = jnp.where(code < TILE, value, current)
            beyond = jnp.where((code & TILE) != 0, value, 0.0)
            chosen[chunk] = merged
            chosen[chunk + 1] = beyond
            later = begin_ref[0, index * 32 + k + 1]
            current = jnp.where(later > chunk, beyond, merged)
            chunk = later
        for k in range(1, GROUP + 1):
            chosen[chunk + k] = jnp.zeros((8, TILE), F32)

    def pack(step, _):
        for k in range(UNROLL):
            pack_tile(step, k)
        return _

    lax.fori_loop(0, TILES // UNROLL, pack, 0)

    def group(index, own, start, count, with_self, room):
        shape = (FORCE_PART, TILE)
        lanes = lax.broadcasted_iota(jnp.int32, shape, 1)
        values = [packed[index, start + k] for k in range(count)]
        features = [
            jnp.concatenate([beside_features(value) for value in values[k : k + 2]], axis=1)
            for k in range(0, count, 2)
        ]
        for part in range(TILE // FORCE_PART):
            cut = slice(part * FORCE_PART, (part + 1) * FORCE_PART)
            total = [jnp.zeros(shape, F32) for _ in range(5)]
            for pair_index, feature in enumerate(features):
                products = [
                    jnp.dot(rows[cut], feature, preferred_element_type=F32) for rows in own
                ]
                for side in range(2):
                    k = 2 * pair_index + side
                    value = values[k]
                    reach, both, pair = (
                        product[:, side * TILE : (side + 1) * TILE] for product in products
                    )
                    q = jnp.maximum(reach, 0.0)
                    if with_self and k == 0:
                        here = lax.broadcasted_iota(jnp.int32, shape, 0) + part * FORCE_PART
                        q = jnp.where(here == lanes, 0.0, q)
                    square = q * q
                    pull = square * (q * pair)
                    coef = pull + square * both
                    for comp in range(3):
                        total[comp] = total[comp] + coef * value[comp : comp + 1]
                    total[3] = total[3] + coef
                    total[4] = total[4] + pull * q
            column = jnp.zeros(shape, F32)
            for k in range(5):
                column = jnp.where(lanes == k, jnp.sum(total[k], axis=1, keepdims=True), column)
            sums[room, cut, :] = column
        return sums[room].T[:8]

    def own_rows(value):
        out = jnp.where(row == 3, value[6:7], value)
        out = jnp.where(row == 4, 1.0 + value[5:6], out)
        out = jnp.where(row == 5, 1.0, out)
        a, b, c = pieces(jnp.where(row == 6, value[3:4], out))
        columns = jnp.concatenate([a, a, b, b, a, c], axis=0).T
        place = lax.broadcasted_iota(jnp.int32, columns.shape, 1) % 8
        masks = ((place < 3) | (place == 4) | (place == 5), (place == 3) | (place == 6), place == 7)
        return [jnp.where(mask, columns, 0.0).astype(BF16) for mask in masks]

    def forces(step, _):
        done = []
        for k in range(UNROLL):
            index = step * UNROLL + k
            own = own_rows(packed[index, 0])
            done.append((index, own, group(index, own, 0, GROUP, True, k)))
        for k, (index, own, result) in enumerate(done):
            results[index] = result
            more = (used_ref[0, index * 32 + 31] - GROUP + 1) // 2

            def further(extra, _, index=index, own=own, k=k):
                results[index] += group(index, own, GROUP + 2 * extra, 2, False, k)
                return _

            lax.fori_loop(0, jnp.maximum(more, 0), further, 0)
        return _

    lax.fori_loop(0, TILES // UNROLL, forces, 0)
    for index in range(TILES):
        x, y, z = tile_of(index, OWN)
        result = results[index]
        moved = (2.0 * BETA / SCALE) * (result - packed[index, 0] * result[3:4])
        for comp in range(3):
            forces_ref[comp, x, y, z : z + 1, :] = moved[comp : comp + 1]
        energy_ref[x, y, z : z + 1, :] = embed_ref[index : index + 1] + 0.045 * result[4:5]


def shards(sizes, positions, species, counts):
    vmem = pl.BlockSpec(memory_space=pltpu.VMEM)
    smem = pl.BlockSpec(memory_space=pltpu.SMEM)
    tiles = OWN[0] * OWN[1] * OWN[2]
    full, embed, near, begin, used = pl.pallas_call(
        lambda *refs: exchange_kernel(sizes, *refs),
        name="exchange",
        out_shape=(
            jax.ShapeDtypeStruct(EXT + (8, TILE), F32),
            jax.ShapeDtypeStruct((tiles, TILE), F32),
            jax.ShapeDtypeStruct((tiles, 32, TILE), jnp.int32),
            jax.ShapeDtypeStruct((1, tiles * 32), jnp.int32),
            jax.ShapeDtypeStruct((1, tiles * 32), jnp.int32),
        ),
        in_specs=[pl.BlockSpec(memory_space=pltpu.HBM)] * 3,
        out_specs=(vmem,) * 5,
        scratch_shapes=[
            pltpu.VMEM(EXT + (4, TILE), F32),
            pltpu.VMEM(EXT + (1, TILE), F32),
            pltpu.VMEM((EXT[0] * EXT[1], 48, EXT[2] * TILE), BF16),
            pltpu.VMEM((tiles, TILE, 48), BF16),
            pltpu.VMEM((tiles, TILE, TILE), F32),
            pltpu.VMEM((tiles, 32, TILE), F32),
            pltpu.VMEM((tiles, TILE), F32),
            pltpu.VMEM((TILE, TILE), F32),
            pltpu.VMEM((3,) + OWN + (TILE,), F32),
            pltpu.VMEM(OWN + (TILE,), jnp.int32),
            pltpu.SMEM(OWN, jnp.int32),
            pltpu.SemaphoreType.DMA((3,)),
            pltpu.SemaphoreType.DMA((2,)),
            pltpu.SemaphoreType.DMA((3,)),
        ],
        compiler_params=pltpu.CompilerParams(collective_id=0, has_side_effects=True, vmem_limit_bytes=24 << 20),
    )(*(pltpu.with_memory_space_constraint(a, pltpu.HBM) for a in (positions, species, counts)))
    return pl.pallas_call(
        force_kernel,
        name="forces",
        out_shape=(
            jax.ShapeDtypeStruct((3,) + OWN + (TILE,), F32),
            jax.ShapeDtypeStruct(OWN + (TILE,), F32),
        ),
        in_specs=[vmem, vmem, vmem, smem, smem],
        out_specs=(vmem, vmem),
        scratch_shapes=[
            pltpu.VMEM((tiles, 32 + GROUP, 8, TILE), F32),
            pltpu.VMEM((UNROLL, TILE, TILE), F32),
            pltpu.VMEM((tiles, 8, TILE), F32),
        ],
        compiler_params=pltpu.CompilerParams(vmem_limit_bytes=24 << 20),
    )(full, embed, near, begin, used)


def solution(mesh):
    placed = (P(None, "gx", "gy", "gz", None), P("gx", "gy", "gz", None), P("gx", "gy", "gz"))
    sizes = tuple(mesh.shape[name] for name in ("gx", "gy", "gz"))
    return jax.shard_map(
        lambda *args: shards(sizes, *args),
        mesh=mesh,
        in_specs=placed,
        out_specs=(P(None, "gx", "gy", "gz", None), P("gx", "gy", "gz", None)),
        check_vma=False,
    )
```

```python
import math

import jax
import jax.numpy as jnp
from jax import lax
from jax.experimental import pallas as pl
from jax.experimental.pallas import tpu as pltpu
from jax.sharding import PartitionSpec as P

F32 = jnp.float32
BF16 = jnp.bfloat16
MESH = pl.DeviceIdType.MESH
CUTOFF_SQUARED = 0.2025
SCALE = math.sqrt(2.0 / CUTOFF_SQUARED)
TILE = 128
OWN = (2, 2, 4)
EXT = (4, 4, 6)
OFFSETS = sorted(
    [(a, b, c) for a in (-1, 0, 1) for b in (-1, 0, 1) for c in (-1, 0, 1) if a or b or c],
    key=lambda offset: -sum(map(abs, offset)),
)
ALPHA = -3.0 / CUTOFF_SQUARED
BETA = -4.0 / CUTOFF_SQUARED * 0.09
SLOPE = ALPHA / (5.0 * BETA)
TILES = OWN[0] * OWN[1] * OWN[2]
UNROLL = OWN[2]
FORCE_PART = 64
GROUP = 6
WEAVE = 2
HIGHEST = lax.Precision.HIGHEST
NT = (((1,), (1,)), ((), ()))


def pieces(v):
    first = v.astype(BF16).astype(F32)
    rest = v - first
    second = rest.astype(BF16).astype(F32)
    return first, second, rest - second


def beside_features(v):
    a, b, c = pieces(v)
    return jnp.concatenate([a, b, a, b, c, a], axis=0).astype(BF16)


def own_features(v):
    a, b, c = pieces(v)
    return jnp.concatenate([a, a, b, b, a, c], axis=0).T.astype(BF16)


def rows_of(*rows):
    row = lax.broadcasted_iota(jnp.int32, (8, TILE), 0)
    out = jnp.zeros((8, TILE), F32)
    for index, value in enumerate(rows):
        if value is not None:
            out = jnp.where(row == index, value, out)
    return out


def lane_gather(value, places):
    return lax.gather(
        value,
        places[..., None],
        lax.GatherDimensionNumbers(
            offset_dims=(),
            collapsed_slice_dims=(1,),
            start_index_map=(1,),
            operand_batching_dims=(0,),
            start_indices_batching_dims=(0,),
        ),
        slice_sizes=(1, 1),
        mode=lax.GatherScatterMode.PROMISE_IN_BOUNDS,
    )


def tile_of(index, extent):
    plane = extent[1] * extent[2]
    return index // plane, (index // extent[2]) % extent[1], index % extent[2]


def span(offset, own, sending):
    if offset == 0:
        return pl.ds(1, own)
    if sending:
        return pl.ds(own if offset > 0 else 1, 1)
    return pl.ds(0 if offset > 0 else own + 1, 1)


def region(offset, sending):
    return tuple(span(o, n, sending) for o, n in zip(offset, OWN))


def exchange_kernel(
    sizes,
    pos_hbm,
    spec_hbm,
    count_hbm,
    full_ref,
    embed_ref,
    near_ref,
    begin_ref,
    used_ref,
    wire,
    slope,
    beside,
    own,
    totals,
    reach_rows,
    weights,
    columns_ref,
    pos_ref,
    spec_ref,
    count_ref,
    loads,
    sends,
    recvs,
):
    arrivals = [
        pltpu.make_async_copy(source, target, loads.at[k])
        for k, (source, target) in enumerate(
            ((count_hbm, count_ref), (pos_hbm, pos_ref), (spec_hbm, spec_ref))
        )
    ]
    for copy in arrivals:
        copy.start()
    me = [lax.axis_index(name) for name in ("gx", "gy", "gz")]

    def peer(offset):
        return tuple(lax.rem(m + o + n, n) for m, o, n in zip(me, offset, sizes))

    barrier = pltpu.get_barrier_semaphore()
    for offset in OFFSETS:
        pl.semaphore_signal(barrier, inc=1, device_id=peer(offset), device_id_type=MESH)

    for copy in arrivals:
        copy.wait()
    lane = lax.broadcasted_iota(jnp.int32, (1, TILE), 1)
    row4 = lax.broadcasted_iota(jnp.int32, (4, TILE), 0)
    for x in range(OWN[0]):
        for y in range(OWN[1]):
            for z in range(OWN[2]):
                kind = spec_ref[x, y, z : z + 1, :]
                weight = jnp.where(
                    lane < count_ref[x, y, z], jnp.where(kind == 1, 7.0, 5.0), 0.0
                )
                value = jnp.broadcast_to(weight, (4, TILE))
                for comp in range(3):
                    value = jnp.where(row4 == comp, pos_ref[comp, x, y, z : z + 1, :], value)
                wire[x + 1, y + 1, z + 1] = value
                index = (x * OWN[1] + y) * OWN[2] + z
                weights[index : index + 1, :] = weight
    pl.semaphore_wait(barrier, len(OFFSETS))

    def copies(ref, which):
        return [
            pltpu.make_async_remote_copy(
                src_ref=ref.at[region(offset, True)],
                dst_ref=ref.at[region(offset, False)],
                send_sem=sends.at[which],
                recv_sem=recvs.at[which],
                device_id=peer(offset),
                device_id_type=MESH,
            )
            for offset in OFFSETS
        ]

    def settle(ref, sems, which):
        whole = ref.at[:, :, 0 : EXT[2] - 1]
        pltpu.make_async_copy(whole, whole, sems.at[which]).wait()

    state_copies = copies(wire, 0)
    for copy in state_copies:
        copy.start()

    low = (me[2] > 0).astype(F32)
    high = (me[2] < sizes[2] - 1).astype(F32)

    def prepare(x, y, z):
        value = wire[x, y, z]
        weight = value[3:4] * (low if z == 0 else high if z == EXT[2] - 1 else 1.0)
        cx = (value[0:1] + (x - 2).astype(F32)) * SCALE
        cy = (value[1:2] + (y - 2).astype(F32)) * SCALE
        cz = (value[2:3] + float(z - 3)) * SCALE
        norm = 0.5 * (cx * cx + cy * cy + cz * cz)
        root = jnp.where(weight > 6.0, 1.4 ** (1.0 / 3.0), jnp.where(weight > 0.0, 1.0, 0.0))
        pair = jnp.where(weight > 0.0, 0.5 * weight - 0.5, 0.0)
        full = rows_of(cx, cy, cz, weight, 1.0, -norm, None, pair)
        full_ref[x, y, z] = full
        row = lax.broadcasted_iota(jnp.int32, (8, TILE), 0)
        part = root * jnp.where(row == 3, 1.0, jnp.where(row == 4, -norm, full))
        beside[x * EXT[1] + y, :, z * TILE : (z + 1) * TILE] = beside_features(
            jnp.where(row < 5, part, 0.0)
        )
        return full

    def prepare_own(index, _):
        x, y = 1 + index // OWN[1], 1 + index % OWN[1]
        for z in range(OWN[2]):
            full = prepare(x, y, z + 1)
            row = lax.broadcasted_iota(jnp.int32, (8, TILE), 0)
            value = jnp.where(row == 3, 1.0 + full[5:6], jnp.where(row < 5, full, 0.0))
            own[index * OWN[2] + z] = own_features(value)
        return _

    lax.fori_loop(0, OWN[0] * OWN[1], prepare_own, 0)

    def cubes(rows, there):
        value = jnp.maximum(jnp.dot(rows, there, preferred_element_type=F32), 0.0)
        return value * value * value

    def blocks(value):
        return sum(
            value[:, k * TILE : (k + 1) * TILE] for k in range(1, value.shape[1] // TILE)
        ) + value[:, :TILE]

    def window(column, z, width=3):
        if isinstance(z, int):
            return beside[column, :, z * TILE : (z + width) * TILE]
        return beside[column, :, pl.ds(pl.multiple_of(z * TILE, TILE), width * TILE)]

    def inner_tile(step, z):
        x, y, index = step // OWN[1], lax.rem(step, OWN[1]), step * OWN[2] + z
        first = max(z, 1)
        width = min(z + 2, OWN[2]) - first + 1
        total = jnp.zeros((TILE, TILE), F32)
        for dx in range(OWN[0]):
            for dy in range(OWN[1]):
                there = lax.rem(x + dx, OWN[0]) + 1, lax.rem(y + dy, OWN[1]) + 1
                cube = cubes(own[index], window(there[0] * EXT[1] + there[1], first, width))
                if (dx, dy) == (0, 0):
                    here = lax.broadcasted_iota(jnp.int32, cube.shape, 0) + (z + 1 - first) * TILE
                    self_pair = here == lax.broadcasted_iota(jnp.int32, cube.shape, 1)
                    cube = jnp.where(self_pair, 0.0, cube)
                total = total + blocks(cube)
        totals[index] = total

    def inner(step, _):
        for k in range(UNROLL):
            inner_tile(step, k)
        return _

    lax.fori_loop(0, TILES // UNROLL, inner, 0)

    settle(wire, recvs, 0)

    def prepare_side(index, _):
        x = jnp.where(index < 4, 0, jnp.where(index < 8, EXT[0] - 1, 1 + (index - 8) // 2))
        y = jnp.where(index < 8, lax.rem(index, 4), (EXT[1] - 1) * lax.rem(index, 2))
        for z in range(EXT[2]):
            prepare(x, y, z)
        return _

    lax.fori_loop(0, EXT[0] * EXT[1] - OWN[0] * OWN[1], prepare_side, 0)

    def prepare_ends(index, _):
        for z in (0, EXT[2] - 1):
            prepare(1 + index // OWN[1], 1 + index % OWN[1], z)
        return _

    lax.fori_loop(0, OWN[0] * OWN[1], prepare_ends, 0)

    lanes = lax.broadcasted_iota(jnp.int32, (TILE, TILE), 1)

    def outer_tile(step, z):
        x, y, index = step // OWN[1], lax.rem(step, OWN[1]), step * OWN[2] + z
        side_x, side_y = x * (EXT[0] - 1), y * (EXT[1] - 1)
        columns = [side_x * EXT[1] + y + dy for dy in range(3)]
        columns += [(dx + 1) * EXT[1] + side_y for dx in range(OWN[0])]
        total = totals[index]
        for column in columns:
            total = total + blocks(cubes(own[index], window(column, z)))
        if z in (0, OWN[2] - 1):
            end = 0 if z == 0 else EXT[2] - 1
            for dx in range(OWN[0]):
                pair = [window((dx + 1) * EXT[1] + dy + 1, end, 1) for dy in range(OWN[1])]
                total = total + blocks(cubes(own[index], jnp.concatenate(pair, axis=1)))
        return jnp.sum(total, axis=1, keepdims=True)

    slope_copies = copies(slope, 1)
    plane = OWN[0] * OWN[1]

    def finish_density(heights):
        def outer(step, _):
            value = columns_ref[...]
            for column in (2 * step, 2 * step + 1):
                for z in heights:
                    index = column * OWN[2] + z
                    value = jnp.where(lanes == index, outer_tile(column, z), value)
            columns_ref[...] = value
            return _

        lax.fori_loop(0, plane // 2, outer, 0)
        root = jnp.sqrt(1.0 + columns_ref[...].T[:TILES])
        weight = weights[...]
        strength = jnp.where(weight > 6.0, 0.7, jnp.where(weight > 0.0, 1.0, 0.0))
        embed_ref[...] = -strength * root
        rows = -0.5 * SLOPE * strength / root
        for z in heights:
            for k in range(plane):
                index = k * OWN[2] + z
                slope[k // OWN[1] + 1, k % OWN[1] + 1, z + 1] = rows[index : index + 1]

    columns_ref[...] = jnp.zeros((TILE, TILE), F32)
    finish_density((0, OWN[2] - 1))
    for copy, offset in zip(slope_copies, OFFSETS):
        if offset[2] != 0:
            copy.start()
    finish_density((1, 2))
    for copy, offset in zip(slope_copies, OFFSETS):
        if offset[2] == 0:
            copy.start()

    def distances_of(step, z):
        x, y, index = step // OWN[1], lax.rem(step, OWN[1]), step * OWN[2] + z
        around, known = (ref.at[pl.ds(x, 3), pl.ds(y, 3)] for ref in (wire, full_ref))
        for k, offset in enumerate(OFFSETS):
            at = (offset[0] + 1, offset[1] + 1, z + 1 + offset[2])
            there = around[at]
            far = None
            for comp, o in enumerate(offset):
                if o:
                    gap = there[comp : comp + 1] if o > 0 else 1.0 - there[comp : comp + 1]
                    far = gap * gap if far is None else far + gap * gap
            weight = known[at + (slice(3, 4),)]
            reach_rows[index, k : k + 1, :] = jnp.where(weight > 0.0, far, 9.0)
        for k in range(len(OFFSETS), 32):
            reach_rows[index, k : k + 1, :] = jnp.full((1, TILE), 9.0, F32)

    def distances(step, _):
        for k in range(UNROLL):
            distances_of(step, k)
        return _

    lax.fori_loop(0, TILES // UNROLL, distances, 0)

    first = lax.broadcasted_iota(jnp.int32, (TILE, TILE), 0)
    second = lax.broadcasted_iota(jnp.int32, (TILE, TILE), 1)
    earlier = (first < second).astype(F32).astype(BF16)
    ones = jnp.ones((TILE, TILE), BF16)
    above_rows = ((second < first) & (second // 32 == first // 32)).astype(F32).astype(BF16)
    first_lane = (lax.broadcasted_iota(jnp.int32, (8, TILE), 1) == 0).astype(F32).astype(BF16)

    def compress_rows(group):
        rows = reach_rows[pl.ds(group * 4, 4)].reshape(TILE, TILE)
        near = rows < CUTOFF_SQUARED * 1.00002
        flags = near.astype(F32).astype(BF16)
        before = jnp.dot(flags, earlier, preferred_element_type=F32).astype(jnp.int32)
        held = jnp.dot(flags, ones, preferred_element_type=F32).astype(BF16)
        filled = jnp.dot(above_rows, held, preferred_element_type=F32).astype(jnp.int32)
        word = jnp.where(near, 16384 + second * 128 + (second - before), 0)
        for bit in range(7):
            moved = pltpu.roll(word, TILE - (1 << bit), 1)
            stay = jnp.where((word & (1 << bit)) != 0, 0, word)
            word = jnp.where((moved & (1 << bit)) != 0, moved, stay)
        start = filled & (TILE - 1)
        turned = (second - start) & (TILE - 1)
        word = lane_gather(word, turned)
        code = ((word >> 7) & 127) + jnp.where(second < start, TILE, 0)
        near_ref[pl.ds(group * 4, 4)] = jnp.where(word >= 16384, code, 512).reshape(4, 32, TILE)
        cut = pl.ds(pl.multiple_of(group * TILE, TILE), TILE)
        for ref, value in (
            (begin_ref, 1 + (filled >> 7)),
            (used_ref, 1 + ((filled + TILE - 1) >> 7)),
        ):
            value = value.astype(F32).astype(BF16)
            value = lax.dot_general(first_lane, value, NT, preferred_element_type=F32)
            ref[:, cut] = value[0:1].astype(jnp.int32)

    def compress(step, _):
        for k in range(2):
            compress_rows(step * 2 + k)
        return _

    lax.fori_loop(0, 2, compress, 0)

    settle(wire, sends, 0)
    settle(slope, recvs, 1)

    def finish(index, _):
        for z in range(EXT[2]):
            at = (index // EXT[1], lax.rem(index, EXT[1]), z)
            value = slope[at]
            if z in (0, EXT[2] - 1):
                value = value * (high if z else low)
            full_ref[at + (slice(6, 7),)] = value
        return _

    lax.fori_loop(0, EXT[0] * EXT[1], finish, 0)
    settle(slope, sends, 1)


def force_kernel(
    full_ref, embed_ref, near_ref, begin_ref, used_ref, forces_ref, energy_ref, even, odd, sums, results
):
    row = lax.broadcasted_iota(jnp.int32, (8, TILE), 0)

    def pack_tile(packed, step, z):
        x, y, index = step // OWN[1], lax.rem(step, OWN[1]), step * OWN[2] + z
        around = full_ref.at[pl.ds(x, 3), pl.ds(y, 3)]
        chosen = packed.at[z]
        chosen[0] = around[1, 1, z + 1]
        current = jnp.zeros((8, TILE), F32)
        chunk = begin_ref[0, index * 32]
        for k, offset in enumerate(OFFSETS):
            there = around[offset[0] + 1, offset[1] + 1, z + 1 + offset[2]]
            code = jnp.broadcast_to(near_ref[index, k : k + 1, :], (8, TILE))
            places = code & (TILE - 1)
            value = lane_gather(there, places)
            merged = jnp.where(code < TILE, value, current)
            beyond = jnp.where((code & TILE) != 0, value, 0.0)
            chosen[chunk] = merged
            chosen[chunk + 1] = beyond
            later = begin_ref[0, index * 32 + k + 1]
            current = jnp.where(later > chunk, beyond, merged)
            chunk = later
            yield
        for k in range(1, GROUP + 1):
            chosen[chunk + k] = jnp.zeros((8, TILE), F32)

    def pack(packed, step):
        for z in range(UNROLL):
            yield from pack_tile(packed, step, z)

    def group(packed, place, own, start, count, with_self, keep):
        shape = (FORCE_PART, TILE)
        lanes = lax.broadcasted_iota(jnp.int32, shape, 1)
        values = [packed[place, start + k] for k in range(count)]
        features = [
            jnp.concatenate([beside_features(value) for value in values[k : k + 2]], axis=1)
            for k in range(0, count, 2)
        ]
        for part in range(TILE // FORCE_PART):
            cut = slice(part * FORCE_PART, (part + 1) * FORCE_PART)
            total = [jnp.zeros(shape, F32) for _ in range(5)]
            for pair_index, feature in enumerate(features):
                products = [
                    jnp.dot(rows[cut], feature, preferred_element_type=F32) for rows in own
                ]
                for side in range(2):
                    k = 2 * pair_index + side
                    value = values[k]
                    reach, both, pair = (
                        product[:, side * TILE : (side + 1) * TILE] for product in products
                    )
                    q = jnp.maximum(reach, 0.0)
                    if with_self and k == 0:
                        here = lax.broadcasted_iota(jnp.int32, shape, 0) + part * FORCE_PART
                        q = jnp.where(here == lanes, 0.0, q)
                    square = q * q
                    pull = square * (q * pair)
                    coef = pull + square * both
                    for comp in range(3):
                        total[comp] = total[comp] + coef * value[comp : comp + 1]
                    total[3] = total[3] + coef
                    total[4] = total[4] + pull * q
                    yield
            column = jnp.zeros(shape, F32)
            for k in range(5):
                column = jnp.where(lanes == k, jnp.sum(total[k], axis=1, keepdims=True), column)
            sums[place, cut, :] = column
        keep(sums[place].T[:8])

    def own_rows(value):
        out = jnp.where(row == 3, value[6:7], value)
        out = jnp.where(row == 4, 1.0 + value[5:6], out)
        out = jnp.where(row == 5, 1.0, out)
        a, b, c = pieces(jnp.where(row == 6, value[3:4], out))
        columns = jnp.concatenate([a, a, b, b, a, c], axis=0).T
        place = lax.broadcasted_iota(jnp.int32, columns.shape, 1) % 8
        masks = ((place < 3) | (place == 4) | (place == 5), (place == 3) | (place == 6), place == 7)
        return [jnp.where(mask, columns, 0.0).astype(BF16) for mask in masks]

    def drain(steps):
        for _ in steps:
            pass

    def forces(packed, step, beside):
        owns = [own_rows(packed[place, 0]) for place in range(UNROLL)]
        for place, own in enumerate(owns):

            def keep(result, index=step * UNROLL + place):
                results[index] = result

            for _ in group(packed, place, own, 0, GROUP, True, keep):
                for _ in range(WEAVE):
                    next(beside, None)
        drain(beside)
        for place, own in enumerate(owns):
            index = step * UNROLL + place
            more = (used_ref[0, index * 32 + 31] - GROUP + 1) // 2

            def further(extra, _, place=place, index=index, own=own):
                def keep(result):
                    results[index] += result

                drain(group(packed, place, own, GROUP + 2 * extra, 2, False, keep))
                return _

            lax.fori_loop(0, jnp.maximum(more, 0), further, 0)

    steps = TILES // UNROLL
    drain(pack(even, 0))

    def two_steps(index, _):
        first = 2 * index
        forces(even, first, pack(odd, first + 1))
        forces(odd, first + 1, pack(even, jnp.minimum(first + 2, steps - 1)))
        return _

    lax.fori_loop(0, steps // 2, two_steps, 0)
    for index in range(TILES):
        x, y, z = tile_of(index, OWN)
        result = results[index]
        moved = (2.0 * BETA / SCALE) * (result - full_ref[x + 1, y + 1, z + 1] * result[3:4])
        for comp in range(3):
            forces_ref[comp, x, y, z : z + 1, :] = moved[comp : comp + 1]
        energy_ref[x, y, z : z + 1, :] = embed_ref[index : index + 1] + 0.045 * result[4:5]


def shards(sizes, positions, species, counts):
    vmem = pl.BlockSpec(memory_space=pltpu.VMEM)
    smem = pl.BlockSpec(memory_space=pltpu.SMEM)
    tiles = OWN[0] * OWN[1] * OWN[2]
    full, embed, near, begin, used = pl.pallas_call(
        lambda *refs: exchange_kernel(sizes, *refs),
        name="exchange",
        out_shape=(
            jax.ShapeDtypeStruct(EXT + (8, TILE), F32),
            jax.ShapeDtypeStruct((tiles, TILE), F32),
            jax.ShapeDtypeStruct((tiles, 32, TILE), jnp.int32),
            jax.ShapeDtypeStruct((1, tiles * 32), jnp.int32),
            jax.ShapeDtypeStruct((1, tiles * 32), jnp.int32),
        ),
        in_specs=[pl.BlockSpec(memory_space=pltpu.HBM)] * 3,
        out_specs=(vmem,) * 5,
        scratch_shapes=[
            pltpu.VMEM(EXT + (4, TILE), F32),
            pltpu.VMEM(EXT + (1, TILE), F32),
            pltpu.VMEM((EXT[0] * EXT[1], 48, EXT[2] * TILE), BF16),
            pltpu.VMEM((tiles, TILE, 48), BF16),
            pltpu.VMEM((tiles, TILE, TILE), F32),
            pltpu.VMEM((tiles, 32, TILE), F32),
            pltpu.VMEM((tiles, TILE), F32),
            pltpu.VMEM((TILE, TILE), F32),
            pltpu.VMEM((3,) + OWN + (TILE,), F32),
            pltpu.VMEM(OWN + (TILE,), jnp.int32),
            pltpu.SMEM(OWN, jnp.int32),
            pltpu.SemaphoreType.DMA((3,)),
            pltpu.SemaphoreType.DMA((2,)),
            pltpu.SemaphoreType.DMA((2,)),
        ],
        compiler_params=pltpu.CompilerParams(collective_id=0, has_side_effects=True, vmem_limit_bytes=24 << 20),
    )(*(pltpu.with_memory_space_constraint(a, pltpu.HBM) for a in (positions, species, counts)))
    return pl.pallas_call(
        force_kernel,
        name="forces",
        out_shape=(
            jax.ShapeDtypeStruct((3,) + OWN + (TILE,), F32),
            jax.ShapeDtypeStruct(OWN + (TILE,), F32),
        ),
        in_specs=[vmem, vmem, vmem, smem, smem],
        out_specs=(vmem, vmem),
        scratch_shapes=[
            pltpu.VMEM((UNROLL, 32 + GROUP, 8, TILE), F32),
            pltpu.VMEM((UNROLL, 32 + GROUP, 8, TILE), F32),
            pltpu.VMEM((UNROLL, TILE, TILE), F32),
            pltpu.VMEM((tiles, 8, TILE), F32),
        ],
        compiler_params=pltpu.CompilerParams(vmem_limit_bytes=24 << 20),
    )(full, embed, near, begin, used)


def solution(mesh):
    placed = (P(None, "gx", "gy", "gz", None), P("gx", "gy", "gz", None), P("gx", "gy", "gz"))
    sizes = tuple(mesh.shape[name] for name in ("gx", "gy", "gz"))
    return jax.shard_map(
        lambda *args: shards(sizes, *args),
        mesh=mesh,
        in_specs=placed,
        out_specs=(P(None, "gx", "gy", "gz", None), P("gx", "gy", "gz", None)),
        check_vma=False,
    )
```

```python
import math

import jax
import jax.numpy as jnp
from jax import lax
from jax.experimental import pallas as pl
from jax.experimental.pallas import tpu as pltpu
from jax.sharding import PartitionSpec as P

F32 = jnp.float32
BF16 = jnp.bfloat16
MESH = pl.DeviceIdType.MESH
CUTOFF_SQUARED = 0.2025
SCALE = math.sqrt(2.0 / CUTOFF_SQUARED)
TILE = 128
OWN = (2, 2, 4)
EXT = (4, 4, 6)
OFFSETS = sorted(
    [(a, b, c) for a in (-1, 0, 1) for b in (-1, 0, 1) for c in (-1, 0, 1) if a or b or c],
    key=lambda offset: -sum(map(abs, offset)),
)
ALPHA = -3.0 / CUTOFF_SQUARED
BETA = -4.0 / CUTOFF_SQUARED * 0.09
SLOPE = ALPHA / (5.0 * BETA)
TILES = OWN[0] * OWN[1] * OWN[2]
UNROLL = OWN[2]
FORCE_PART = 64
GROUP = 6
WEAVE = 2
HIGHEST = lax.Precision.HIGHEST
NT = (((1,), (1,)), ((), ()))


def pieces(v):
    first = v.astype(BF16).astype(F32)
    rest = v - first
    second = rest.astype(BF16).astype(F32)
    return first, second, rest - second


def beside_features(v):
    a, b, c = pieces(v)
    return jnp.concatenate([a, b, a, b, c, a], axis=0).astype(BF16)


def own_features(v):
    a, b, c = pieces(v)
    return jnp.concatenate([a, a, b, b, a, c], axis=0).T.astype(BF16)


def rows_of(*rows):
    row = lax.broadcasted_iota(jnp.int32, (8, TILE), 0)
    out = jnp.zeros((8, TILE), F32)
    for index, value in enumerate(rows):
        if value is not None:
            out = jnp.where(row == index, value, out)
    return out


def lane_gather(value, places):
    return lax.gather(
        value,
        places[..., None],
        lax.GatherDimensionNumbers(
            offset_dims=(),
            collapsed_slice_dims=(1,),
            start_index_map=(1,),
            operand_batching_dims=(0,),
            start_indices_batching_dims=(0,),
        ),
        slice_sizes=(1, 1),
        mode=lax.GatherScatterMode.PROMISE_IN_BOUNDS,
    )


def tile_of(index, extent):
    plane = extent[1] * extent[2]
    return index // plane, (index // extent[2]) % extent[1], index % extent[2]


def span(offset, own, sending):
    if offset == 0:
        return pl.ds(1, own)
    if sending:
        return pl.ds(own if offset > 0 else 1, 1)
    return pl.ds(0 if offset > 0 else own + 1, 1)


def region(offset, sending):
    return tuple(span(o, n, sending) for o, n in zip(offset, OWN))


def exchange_kernel(
    sizes,
    pos_hbm,
    spec_hbm,
    count_hbm,
    full_ref,
    embed_ref,
    near_ref,
    begin_ref,
    wire,
    slope,
    beside,
    own,
    totals,
    reach_rows,
    weights,
    columns_ref,
    pos_ref,
    spec_ref,
    count_ref,
    loads,
    sends,
    recvs,
):
    arrivals = [
        pltpu.make_async_copy(source, target, loads.at[k])
        for k, (source, target) in enumerate(
            ((count_hbm, count_ref), (pos_hbm, pos_ref), (spec_hbm, spec_ref))
        )
    ]
    for copy in arrivals:
        copy.start()
    me = [lax.axis_index(name) for name in ("gx", "gy", "gz")]

    def peer(offset):
        return tuple(lax.rem(m + o + n, n) for m, o, n in zip(me, offset, sizes))

    barrier = pltpu.get_barrier_semaphore()
    for offset in OFFSETS:
        pl.semaphore_signal(barrier, inc=1, device_id=peer(offset), device_id_type=MESH)

    for copy in arrivals:
        copy.wait()
    lane = lax.broadcasted_iota(jnp.int32, (1, TILE), 1)
    row4 = lax.broadcasted_iota(jnp.int32, (4, TILE), 0)
    for x in range(OWN[0]):
        for y in range(OWN[1]):
            for z in range(OWN[2]):
                kind = spec_ref[x, y, z : z + 1, :]
                weight = jnp.where(
                    lane < count_ref[x, y, z], jnp.where(kind == 1, 7.0, 5.0), 0.0
                )
                value = jnp.broadcast_to(weight, (4, TILE))
                for comp in range(3):
                    value = jnp.where(row4 == comp, pos_ref[comp, x, y, z : z + 1, :], value)
                wire[x + 1, y + 1, z + 1] = value
                index = (x * OWN[1] + y) * OWN[2] + z
                weights[index : index + 1, :] = weight
    pl.semaphore_wait(barrier, len(OFFSETS))

    def copies(ref, which):
        return [
            pltpu.make_async_remote_copy(
                src_ref=ref.at[region(offset, True)],
                dst_ref=ref.at[region(offset, False)],
                send_sem=sends.at[which],
                recv_sem=recvs.at[which],
                device_id=peer(offset),
                device_id_type=MESH,
            )
            for offset in OFFSETS
        ]

    def settle(ref, sems, which):
        whole = ref.at[:, :, 0 : EXT[2] - 1]
        pltpu.make_async_copy(whole, whole, sems.at[which]).wait()

    state_copies = copies(wire, 0)
    for copy in state_copies:
        copy.start()

    low = (me[2] > 0).astype(F32)
    high = (me[2] < sizes[2] - 1).astype(F32)

    def prepare(x, y, z):
        value = wire[x, y, z]
        weight = value[3:4] * (low if z == 0 else high if z == EXT[2] - 1 else 1.0)
        cx = (value[0:1] + (x - 2).astype(F32)) * SCALE
        cy = (value[1:2] + (y - 2).astype(F32)) * SCALE
        cz = (value[2:3] + float(z - 3)) * SCALE
        norm = 0.5 * (cx * cx + cy * cy + cz * cz)
        root = jnp.where(weight > 6.0, 1.4 ** (1.0 / 3.0), jnp.where(weight > 0.0, 1.0, 0.0))
        pair = jnp.where(weight > 0.0, 0.5 * weight - 0.5, 0.0)
        full = rows_of(cx, cy, cz, weight, 1.0, -norm, None, pair)
        full_ref[x, y, z] = full
        row = lax.broadcasted_iota(jnp.int32, (8, TILE), 0)
        part = root * jnp.where(row == 3, 1.0, jnp.where(row == 4, -norm, full))
        beside[x * EXT[1] + y, :, z * TILE : (z + 1) * TILE] = beside_features(
            jnp.where(row < 5, part, 0.0)
        )
        return full

    def prepare_own(index, _):
        x, y = 1 + index // OWN[1], 1 + index % OWN[1]
        for z in range(OWN[2]):
            full = prepare(x, y, z + 1)
            row = lax.broadcasted_iota(jnp.int32, (8, TILE), 0)
            value = jnp.where(row == 3, 1.0 + full[5:6], jnp.where(row < 5, full, 0.0))
            own[index * OWN[2] + z] = own_features(value)
        return _

    lax.fori_loop(0, OWN[0] * OWN[1], prepare_own, 0)

    def cubes(rows, there):
        value = jnp.maximum(jnp.dot(rows, there, preferred_element_type=F32), 0.0)
        return value * value * value

    def blocks(value):
        return sum(
            value[:, k * TILE : (k + 1) * TILE] for k in range(1, value.shape[1] // TILE)
        ) + value[:, :TILE]

    def window(column, z, width=3):
        if isinstance(z, int):
            return beside[column, :, z * TILE : (z + width) * TILE]
        return beside[column, :, pl.ds(pl.multiple_of(z * TILE, TILE), width * TILE)]

    def inner_tile(step, z):
        x, y, index = step // OWN[1], lax.rem(step, OWN[1]), step * OWN[2] + z
        first = max(z, 1)
        width = min(z + 2, OWN[2]) - first + 1
        total = jnp.zeros((TILE, TILE), F32)
        for dx in range(OWN[0]):
            for dy in range(OWN[1]):
                there = lax.rem(x + dx, OWN[0]) + 1, lax.rem(y + dy, OWN[1]) + 1
                cube = cubes(own[index], window(there[0] * EXT[1] + there[1], first, width))
                if (dx, dy) == (0, 0):
                    here = lax.broadcasted_iota(jnp.int32, cube.shape, 0) + (z + 1 - first) * TILE
                    self_pair = here == lax.broadcasted_iota(jnp.int32, cube.shape, 1)
                    cube = jnp.where(self_pair, 0.0, cube)
                total = total + blocks(cube)
        totals[index] = total

    def inner(step, _):
        for k in range(UNROLL):
            inner_tile(step, k)
        return _

    lax.fori_loop(0, TILES // UNROLL, inner, 0)

    settle(wire, recvs, 0)

    def prepare_side(index, _):
        x = jnp.where(index < 4, 0, jnp.where(index < 8, EXT[0] - 1, 1 + (index - 8) // 2))
        y = jnp.where(index < 8, lax.rem(index, 4), (EXT[1] - 1) * lax.rem(index, 2))
        for z in range(EXT[2]):
            prepare(x, y, z)
        return _

    lax.fori_loop(0, EXT[0] * EXT[1] - OWN[0] * OWN[1], prepare_side, 0)

    def prepare_ends(index, _):
        for z in (0, EXT[2] - 1):
            prepare(1 + index // OWN[1], 1 + index % OWN[1], z)
        return _

    lax.fori_loop(0, OWN[0] * OWN[1], prepare_ends, 0)

    lanes = lax.broadcasted_iota(jnp.int32, (TILE, TILE), 1)

    def outer_tile(step, z):
        x, y, index = step // OWN[1], lax.rem(step, OWN[1]), step * OWN[2] + z
        side_x, side_y = x * (EXT[0] - 1), y * (EXT[1] - 1)
        columns = [side_x * EXT[1] + y + dy for dy in range(3)]
        columns += [(dx + 1) * EXT[1] + side_y for dx in range(OWN[0])]
        total = totals[index]
        for column in columns:
            total = total + blocks(cubes(own[index], window(column, z)))
        if z in (0, OWN[2] - 1):
            end = 0 if z == 0 else EXT[2] - 1
            for dx in range(OWN[0]):
                pair = [window((dx + 1) * EXT[1] + dy + 1, end, 1) for dy in range(OWN[1])]
                total = total + blocks(cubes(own[index], jnp.concatenate(pair, axis=1)))
        return jnp.sum(total, axis=1, keepdims=True)

    slope_copies = copies(slope, 1)
    plane = OWN[0] * OWN[1]

    def finish_density(heights):
        def outer(step, _):
            value = columns_ref[...]
            for column in (2 * step, 2 * step + 1):
                for z in heights:
                    index = column * OWN[2] + z
                    value = jnp.where(lanes == index, outer_tile(column, z), value)
            columns_ref[...] = value
            return _

        lax.fori_loop(0, plane // 2, outer, 0)
        root = jnp.sqrt(1.0 + columns_ref[...].T[:TILES])
        weight = weights[...]
        strength = jnp.where(weight > 6.0, 0.7, jnp.where(weight > 0.0, 1.0, 0.0))
        embed_ref[...] = -strength * root
        rows = -0.5 * SLOPE * strength / root
        for z in heights:
            for k in range(plane):
                index = k * OWN[2] + z
                slope[k // OWN[1] + 1, k % OWN[1] + 1, z + 1] = rows[index : index + 1]

    columns_ref[...] = jnp.zeros((TILE, TILE), F32)
    finish_density((0, OWN[2] - 1))
    for copy, offset in zip(slope_copies, OFFSETS):
        if offset[2] != 0:
            copy.start()
    finish_density((1, 2))
    for copy, offset in zip(slope_copies, OFFSETS):
        if offset[2] == 0:
            copy.start()

    def distances_of(step, z):
        x, y, index = step // OWN[1], lax.rem(step, OWN[1]), step * OWN[2] + z
        around, known = (ref.at[pl.ds(x, 3), pl.ds(y, 3)] for ref in (wire, full_ref))
        for k, offset in enumerate(OFFSETS):
            at = (offset[0] + 1, offset[1] + 1, z + 1 + offset[2])
            there = around[at]
            far = None
            for comp, o in enumerate(offset):
                if o:
                    gap = there[comp : comp + 1] if o > 0 else 1.0 - there[comp : comp + 1]
                    far = gap * gap if far is None else far + gap * gap
            weight = known[at + (slice(3, 4),)]
            reach_rows[index, k : k + 1, :] = jnp.where(weight > 0.0, far, 9.0)
        for k in range(len(OFFSETS), 32):
            reach_rows[index, k : k + 1, :] = jnp.full((1, TILE), 9.0, F32)

    def distances(step, _):
        for k in range(UNROLL):
            distances_of(step, k)
        return _

    lax.fori_loop(0, TILES // UNROLL, distances, 0)

    first = lax.broadcasted_iota(jnp.int32, (TILE, TILE), 0)
    second = lax.broadcasted_iota(jnp.int32, (TILE, TILE), 1)
    earlier = (first < second).astype(F32).astype(BF16)
    ones = jnp.ones((TILE, TILE), BF16)
    above_rows = ((second < first) & (second // 32 == first // 32)).astype(F32).astype(BF16)
    first_lane = (lax.broadcasted_iota(jnp.int32, (8, TILE), 1) == 0).astype(F32).astype(BF16)

    def compress_rows(group):
        rows = reach_rows[pl.ds(group * 4, 4)].reshape(TILE, TILE)
        near = rows < CUTOFF_SQUARED * 1.00002
        flags = near.astype(F32).astype(BF16)
        before = jnp.dot(flags, earlier, preferred_element_type=F32).astype(jnp.int32)
        held = jnp.dot(flags, ones, preferred_element_type=F32).astype(BF16)
        filled = jnp.dot(above_rows, held, preferred_element_type=F32).astype(jnp.int32)
        word = jnp.where(near, 16384 + second * 128 + (second - before), 0)
        for bit in range(7):
            moved = pltpu.roll(word, TILE - (1 << bit), 1)
            stay = jnp.where((word & (1 << bit)) != 0, 0, word)
            word = jnp.where((moved & (1 << bit)) != 0, moved, stay)
        start = filled & (TILE - 1)
        turned = (second - start) & (TILE - 1)
        word = lane_gather(word, turned)
        code = ((word >> 7) & 127) + jnp.where(second < start, TILE, 0)
        near_ref[pl.ds(group * 4, 4)] = jnp.where(word >= 16384, code, 512).reshape(4, 32, TILE)
        cut = pl.ds(pl.multiple_of(group * TILE, TILE), TILE)
        closing = jnp.where(first % 32 == 31, TILE - 1, 0)
        value = (1 + ((filled + closing) >> 7)).astype(F32).astype(BF16)
        value = lax.dot_general(first_lane, value, NT, preferred_element_type=F32)
        begin_ref[:, cut] = value[0:1].astype(jnp.int32)

    def compress(step, _):
        for k in range(2):
            compress_rows(step * 2 + k)
        return _

    lax.fori_loop(0, 2, compress, 0)

    settle(wire, sends, 0)
    settle(slope, recvs, 1)

    def finish(index, _):
        for y in range(EXT[1]):
            for z in range(EXT[2]):
                value = slope[index, y, z]
                if z in (0, EXT[2] - 1):
                    value = value * (high if z else low)
                full_ref[index, y, z, 6:7, :] = value
        return _

    lax.fori_loop(0, EXT[0], finish, 0)
    settle(slope, sends, 1)


def force_kernel(
    full_ref, embed_ref, near_ref, begin_ref, forces_ref, energy_ref, even, odd, sums, results
):
    row = lax.broadcasted_iota(jnp.int32, (8, TILE), 0)

    def pack_tile(packed, step, z):
        x, y, index = step // OWN[1], lax.rem(step, OWN[1]), step * OWN[2] + z
        around = full_ref.at[pl.ds(x, 3), pl.ds(y, 3)]
        chosen = packed.at[z]
        chosen[0] = around[1, 1, z + 1]
        current = jnp.zeros((8, TILE), F32)
        chunk = begin_ref[0, index * 32]
        for k, offset in enumerate(OFFSETS):
            there = around[offset[0] + 1, offset[1] + 1, z + 1 + offset[2]]
            code = jnp.broadcast_to(near_ref[index, k : k + 1, :], (8, TILE))
            places = code & (TILE - 1)
            value = lane_gather(there, places)
            merged = jnp.where(code < TILE, value, current)
            beyond = jnp.where((code & TILE) != 0, value, 0.0)
            chosen[chunk] = merged
            chosen[chunk + 1] = beyond
            later = begin_ref[0, index * 32 + k + 1]
            current = jnp.where(later > chunk, beyond, merged)
            chunk = later
            yield
        for k in range(1, GROUP + 1):
            chosen[chunk + k] = jnp.zeros((8, TILE), F32)

    def pack(packed, step):
        for z in range(UNROLL):
            yield from pack_tile(packed, step, z)

    def group(packed, place, own, start, count, with_self, keep):
        shape = (FORCE_PART, TILE)
        lanes = lax.broadcasted_iota(jnp.int32, shape, 1)
        values = [packed[place, start + k] for k in range(count)]
        features = [
            jnp.concatenate([beside_features(value) for value in values[k : k + 2]], axis=1)
            for k in range(0, count, 2)
        ]
        for part in range(TILE // FORCE_PART):
            cut = slice(part * FORCE_PART, (part + 1) * FORCE_PART)
            total = [jnp.zeros(shape, F32) for _ in range(5)]
            for pair_index, feature in enumerate(features):
                products = [
                    jnp.dot(rows[cut], feature, preferred_element_type=F32) for rows in own
                ]
                for side in range(2):
                    k = 2 * pair_index + side
                    value = values[k]
                    reach, both, pair = (
                        product[:, side * TILE : (side + 1) * TILE] for product in products
                    )
                    q = jnp.maximum(reach, 0.0)
                    if with_self and k == 0:
                        here = lax.broadcasted_iota(jnp.int32, shape, 0) + part * FORCE_PART
                        q = jnp.where(here == lanes, 0.0, q)
                    square = q * q
                    pull = square * (q * pair)
                    coef = pull + square * both
                    for comp in range(3):
                        total[comp] = total[comp] + coef * value[comp : comp + 1]
                    total[3] = total[3] + coef
                    total[4] = total[4] + pull * q
                    yield
            column = jnp.zeros(shape, F32)
            for k in range(5):
                column = jnp.where(lanes == k, jnp.sum(total[k], axis=1, keepdims=True), column)
            sums[place, cut, :] = column
        keep(sums[place].T[:8])

    def own_rows(value):
        out = jnp.where(row == 3, value[6:7], value)
        out = jnp.where(row == 4, 1.0 + value[5:6], out)
        out = jnp.where(row == 5, 1.0, out)
        a, b, c = pieces(jnp.where(row == 6, value[3:4], out))
        columns = jnp.concatenate([a, a, b, b, a, c], axis=0).T
        place = lax.broadcasted_iota(jnp.int32, columns.shape, 1) % 8
        masks = ((place < 3) | (place == 4) | (place == 5), (place == 3) | (place == 6), place == 7)
        return [jnp.where(mask, columns, 0.0).astype(BF16) for mask in masks]

    def drain(steps):
        for _ in steps:
            pass

    def forces(packed, step, beside):
        owns = [own_rows(packed[place, 0]) for place in range(UNROLL)]
        for place, own in enumerate(owns):

            def keep(result, index=step * UNROLL + place):
                results[index] = result

            for _ in group(packed, place, own, 0, GROUP, True, keep):
                for _ in range(WEAVE):
                    next(beside, None)
        drain(beside)
        for place, own in enumerate(owns):
            index = step * UNROLL + place
            more = (begin_ref[0, index * 32 + 31] - GROUP + 1) // 2

            def further(extra, _, place=place, index=index, own=own):
                def keep(result):
                    results[index] += result

                drain(group(packed, place, own, GROUP + 2 * extra, 2, False, keep))
                return _

            lax.fori_loop(0, jnp.maximum(more, 0), further, 0)

    steps = TILES // UNROLL
    drain(pack(even, 0))

    def two_steps(index, _):
        first = 2 * index
        forces(even, first, pack(odd, first + 1))
        forces(odd, first + 1, pack(even, jnp.minimum(first + 2, steps - 1)))
        return _

    lax.fori_loop(0, steps // 2, two_steps, 0)
    for index in range(TILES):
        x, y, z = tile_of(index, OWN)
        result = results[index]
        moved = (2.0 * BETA / SCALE) * (result - full_ref[x + 1, y + 1, z + 1] * result[3:4])
        for comp in range(3):
            forces_ref[comp, x, y, z : z + 1, :] = moved[comp : comp + 1]
        energy_ref[x, y, z : z + 1, :] = embed_ref[index : index + 1] + 0.045 * result[4:5]


def shards(sizes, positions, species, counts):
    vmem = pl.BlockSpec(memory_space=pltpu.VMEM)
    smem = pl.BlockSpec(memory_space=pltpu.SMEM)
    tiles = OWN[0] * OWN[1] * OWN[2]
    full, embed, near, begin = pl.pallas_call(
        lambda *refs: exchange_kernel(sizes, *refs),
        name="exchange",
        out_shape=(
            jax.ShapeDtypeStruct(EXT + (8, TILE), F32),
            jax.ShapeDtypeStruct((tiles, TILE), F32),
            jax.ShapeDtypeStruct((tiles, 32, TILE), jnp.int32),
            jax.ShapeDtypeStruct((1, tiles * 32), jnp.int32),
        ),
        in_specs=[pl.BlockSpec(memory_space=pltpu.HBM)] * 3,
        out_specs=(vmem,) * 4,
        scratch_shapes=[
            pltpu.VMEM(EXT + (4, TILE), F32),
            pltpu.VMEM(EXT + (1, TILE), F32),
            pltpu.VMEM((EXT[0] * EXT[1], 48, EXT[2] * TILE), BF16),
            pltpu.VMEM((tiles, TILE, 48), BF16),
            pltpu.VMEM((tiles, TILE, TILE), F32),
            pltpu.VMEM((tiles, 32, TILE), F32),
            pltpu.VMEM((tiles, TILE), F32),
            pltpu.VMEM((TILE, TILE), F32),
            pltpu.VMEM((3,) + OWN + (TILE,), F32),
            pltpu.VMEM(OWN + (TILE,), jnp.int32),
            pltpu.SMEM(OWN, jnp.int32),
            pltpu.SemaphoreType.DMA((3,)),
            pltpu.SemaphoreType.DMA((2,)),
            pltpu.SemaphoreType.DMA((2,)),
        ],
        compiler_params=pltpu.CompilerParams(collective_id=0, has_side_effects=True, vmem_limit_bytes=24 << 20),
    )(*(pltpu.with_memory_space_constraint(a, pltpu.HBM) for a in (positions, species, counts)))
    return pl.pallas_call(
        force_kernel,
        name="forces",
        out_shape=(
            jax.ShapeDtypeStruct((3,) + OWN + (TILE,), F32),
            jax.ShapeDtypeStruct(OWN + (TILE,), F32),
        ),
        in_specs=[vmem, vmem, vmem, smem],
        out_specs=(vmem, vmem),
        scratch_shapes=[
            pltpu.VMEM((UNROLL, 32 + GROUP, 8, TILE), F32),
            pltpu.VMEM((UNROLL, 32 + GROUP, 8, TILE), F32),
            pltpu.VMEM((UNROLL, TILE, TILE), F32),
            pltpu.VMEM((tiles, 8, TILE), F32),
        ],
        compiler_params=pltpu.CompilerParams(vmem_limit_bytes=24 << 20),
    )(full, embed, near, begin)


def solution(mesh):
    placed = (P(None, "gx", "gy", "gz", None), P("gx", "gy", "gz", None), P("gx", "gy", "gz"))
    sizes = tuple(mesh.shape[name] for name in ("gx", "gy", "gz"))
    return jax.shard_map(
        lambda *args: shards(sizes, *args),
        mesh=mesh,
        in_specs=placed,
        out_specs=(P(None, "gx", "gy", "gz", None), P("gx", "gy", "gz", None)),
        check_vma=False,
    )
```
